512 devices in a mesh: src: 4 (over x_hi, core), depth: 8 (over y), lat: 16 (over z, x_lo).
Axes of the slice: x: 4 (x_hi: 2, x_lo: 2; x = x_hi * 2 + x_lo), y: 8, z: 8, core: 2. Of those that a mesh axis runs over, the one named last changes fastest.
Arguments:
- conductivity: float32 [128, 128, 128], P('depth', 'lat'), may hold values from 0.2 to 2
- e_start: float32 [8, 3, 128, 128, 128], P('src', None, 'depth', 'lat'), may hold values from -6 to 6
- h_start: float32 [8, 3, 128, 128, 128], P('src', None, 'depth', 'lat'), may hold values from -6 to 6
- e_weight: float32 [8, 3, 128, 128, 128], P('src', None, 'depth', 'lat'), may hold values from -6 to 6
- h_weight: float32 [8, 3, 128, 128, 128], P('src', None, 'depth', 'lat'), may hold values from -6 to 6
- source_amp: float32 [8, 3], P('src'), may hold values from -12 to 12
- tow_cell: int32 [8], P('src'), may hold values from 0 to 2097151
- rec_cell: int32 [8, 16, 16], P('depth', 'lat'), may hold values from 0 to 16383
- rec_owner: int32 [8, 16, 16, 1], P('depth', 'lat'), may hold values from 0 to 15; in each aligned block of 16 rows (0 to 15, 16 to 31, ..., all dimensions but the last counted through in order) at most 2 rows name the same one
Outputs:
- grad: float32 [128, 128, 128], P('depth', 'lat')
- line_samples: float32 [8, 8, 16, 16, 2, 9], P('src', 'depth', 'lat')
The draws below stay inside these ranges and needn't reach their ends.
Inputs may be any that keep to these rules, and one draw needn't show every extreme that they name: `tow_cell`: a flat cell of the whole grid. `rec_cell`: a local flat cell of the receiver's block; cells may repeat. `rec_owner`: among the 16 receivers of one block, at most 2 have the same owner, and in some block exactly 2 do.
All inputs are finite; a program needn't handle non-finite values.
Results may differ from the reference program's by a relative error of at most 0.0003.
Values sent between devices are 32-bit elements; how exact they have to be, the bound alone decides.
No kernel may reach another device: no remote copies, remote signals or barrier semaphores. Data moves between devices by JAX's collectives and lax.ppermute only.
A program may use at most 128 MiB of HBM per device.

```python
import math
import jax
import jax.numpy as jnp
import numpy as np
from jax import lax

CX = 8
CZ = 16
NY = 128
STEPS = 3
RPD = 16
GROUPS = 8
DEPTH_BLOCKS = 8
LAT_TILES = 16
NZ = 128
NX = 128
CAP = 2


def plant(drawn, own_key, low, largest):
    longest = drawn.shape.index(max(drawn.shape))
    spots = []
    for shift in (0, 1):
        where = [jax.random.randint(jax.random.fold_in(own_key, axis), (), 0, length) for axis, length in enumerate(drawn.shape)]
        where[longest] = (where[longest] + shift) % drawn.shape[longest]
        spots.append(tuple(where))
    return drawn.at[spots[0]].set(low).at[spots[1]].set(largest)


def steps_of(stream_key, dims, shards, smallest, largest):
    def one(axis_at, shards_of):
        draws = jax.random.uniform(jax.random.fold_in(jax.random.fold_in(stream_key, 6), axis_at), (shards_of,), jnp.float32, smallest / len(shards), largest / len(shards))
        return jnp.repeat(jnp.exp(draws), dims[axis_at] // shards_of).reshape((-1,) + (1,) * (len(dims) - axis_at - 1))

    level = one(*shards[0])
    for cut in shards[1:]:
        level = level * one(*cut)
    return level


def routed_block(own_key, own, number, rows, number_of, top, limit, skew):
    order = jax.random.permutation(own_key, number_of)
    heavy_load, usual = load_shares(number_of, rows * top, limit, skew, True), load_shares(number_of, rows * top, limit, skew, False)
    places = jnp.arange(number_of)

    def named(sizes, offset_by):
        used = int((sizes > 0).sum())
        fixed = max(1, used // 4)
        shifted = fixed + (places - fixed + offset_by * (used - fixed)) % max(1, number_of - fixed)
        return jnp.zeros((number_of,), jnp.int32).at[order[jnp.where(places < fixed, places, shifted)]].set(jnp.asarray(sizes, jnp.int32))

    sizes = jnp.where(number % 4 == 0, named(heavy_load, number // 4), named(usual, number - number // 4 - 1))
    mixed = jax.random.permutation(jax.random.fold_in(own, 3), number_of)
    giver, sink = mixed[0:number_of // 2 * 2:2], mixed[1:number_of // 2 * 2:2]
    room = jnp.minimum(sizes[giver] - 1, limit - sizes[sink]) // 2
    room = jnp.where((giver == order[0]) | (sink == order[0]) | (sizes[sink] == 0), 0, jnp.maximum(room, 0))
    shifted = jax.random.randint(jax.random.fold_in(own, 4), (number_of // 2,), 0, 1 << 20) % (room + 1)
    sizes = sizes.at[giver].add(-shifted).at[sink].add(shifted)
    labels = jnp.searchsorted(jnp.cumsum(sizes), jnp.arange(rows * top), side="right").astype(jnp.int32)
    grid = labels.reshape(top, rows).T
    grid = grid[jax.random.permutation(jax.random.fold_in(own, 1), rows)]
    offset_by = jax.random.randint(jax.random.fold_in(own, 2), (rows, 1), 0, top)
    return jnp.take_along_axis(grid, (jnp.arange(top)[None, :] + offset_by) % top, axis=1)


def load_shares(count, total, reach, skew, full):
    loads = [(1 << 20) // math.isqrt(standing ** skew) + 1 for standing in range(1, count + 1)]
    largest = reach if full else min(reach, max(-(-total // count), total * loads[0] // sum(loads)))
    least = 1 if total - largest >= count - 1 else 0
    holding, spare = [largest] + [least] * (count - 1), total - largest - least * (count - 1)
    while spare > 0:
        candidates = [i for i in range(1, count) if holding[i] < largest] or [i for i in range(1, count) if holding[i] < reach]
        mass, budget = sum([loads[i] for i in candidates]), spare
        for i in candidates:
            more = min(reach - holding[i], max(1, budget * loads[i] // mass), spare)
            holding[i] = holding[i] + more
            spare = spare - more
    return np.array(holding)


def noise(stream_key, extent, scale, limit, split=(), held_as=jnp.bfloat16):
    values = scale * jax.random.normal(stream_key, extent, jnp.float32)
    if split:
        values = values * steps_of(stream_key, extent, split, -0.22, 0.18)
    return jnp.clip(values, -limit, limit).astype(held_as)


def setup_inputs(seed: int = 0) -> dict:
    key_of = jax.random.split(jax.random.key(seed), 10)
    conductivity = jnp.clip(jnp.exp(math.log(2.0) - 2.3025851 * jax.random.uniform(key_of[0], (NZ, NX, NY), jnp.float32) ** steps_of(key_of[0], (NZ, NX, NY), ((0, 8), (1, 16)), -0.2, 0.2)), 0.2, 2.0)
    e_start = noise(key_of[1], (GROUPS, 3, NZ, NX, NY), 1.0, 6.0, ((0, 4), (2, 8), (3, 16)), jnp.float32)
    h_start = noise(key_of[2], (GROUPS, 3, NZ, NX, NY), 1.0, 6.0, ((0, 4), (2, 8), (3, 16)), jnp.float32)
    e_weight = noise(key_of[3], (GROUPS, 3, NZ, NX, NY), 1.0, 6.0, ((0, 4), (2, 8), (3, 16)), jnp.float32)
    h_weight = noise(key_of[4], (GROUPS, 3, NZ, NX, NY), 1.0, 6.0, ((0, 4), (2, 8), (3, 16)), jnp.float32)
    source_amp = noise(key_of[5], (GROUPS, STEPS), 4.0, 12.0, ((0, 4),), jnp.float32)
    tow_cell = plant(jax.random.randint(key_of[6], (GROUPS,), 0, NZ * NX * NY), jax.random.fold_in(key_of[6], 1), 0, (NZ * NX * NY) - 1).astype(jnp.int32)
    rec_cell = plant(jax.random.randint(key_of[7], (DEPTH_BLOCKS, LAT_TILES, RPD), 0, CZ * CX * NY), jax.random.fold_in(key_of[7], 1), 0, (CZ * CX * NY) - 1).astype(jnp.int32)
    rec_owner_keys = jax.random.split(jax.random.fold_in(key_of[8], 1), DEPTH_BLOCKS * LAT_TILES * RPD // RPD)
    rec_owner_turns = jax.random.permutation(jax.random.fold_in(key_of[8], 3), DEPTH_BLOCKS * LAT_TILES * RPD // RPD)
    rec_owner = jax.vmap(lambda own, number: routed_block(jax.random.fold_in(key_of[8], 2), own, number, RPD, LAT_TILES, 1, CAP, 1))(rec_owner_keys, rec_owner_turns).reshape((DEPTH_BLOCKS, LAT_TILES, RPD, 1))
    return {"conductivity": conductivity, "e_start": e_start, "h_start": h_start, "e_weight": e_weight, "h_weight": h_weight, "source_amp": source_amp, "tow_cell": tow_cell, "rec_cell": rec_cell, "rec_owner": rec_owner}


ch_coef = 0.5
loss_rate = 0.5


def component(field, k):
    return field[..., k, :, :, :]


def curl_upper(field, rim_z, rim_x):
    fx = component(field, 0)
    fy = component(field, 1)
    fz = component(field, 2)
    zx = jnp.concatenate([fx, component(rim_z, 0)], axis=-3)[..., 1:, :, :] - fx
    zy = jnp.concatenate([fy, component(rim_z, 1)], axis=-3)[..., 1:, :, :] - fy
    xy = jnp.concatenate([fy, component(rim_x, 0)], axis=-2)[..., :, 1:, :] - fy
    xz = jnp.concatenate([fz, component(rim_x, 1)], axis=-2)[..., :, 1:, :] - fz
    yz = jnp.concatenate([fz[..., 1:], jnp.zeros_like(fz[..., :1])], axis=-1) - fz
    yx = jnp.concatenate([fx[..., 1:], jnp.zeros_like(fx[..., :1])], axis=-1) - fx
    return jnp.stack([yz - zy, zx - xz, xy - yx], axis=-4)


def curl_lower(field, rim_z, rim_x):
    fx = component(field, 0)
    fy = component(field, 1)
    fz = component(field, 2)
    zx = fx - jnp.concatenate([component(rim_z, 0), fx], axis=-3)[..., :-1, :, :]
    zy = fy - jnp.concatenate([component(rim_z, 1), fy], axis=-3)[..., :-1, :, :]
    xy = fy - jnp.concatenate([component(rim_x, 0), fy], axis=-2)[..., :, :-1, :]
    xz = fz - jnp.concatenate([component(rim_x, 1), fz], axis=-2)[..., :, :-1, :]
    yz = fz - jnp.concatenate([jnp.zeros_like(fz[..., :1]), fz[..., :-1]], axis=-1)
    yx = fx - jnp.concatenate([jnp.zeros_like(fx[..., :1]), fx[..., :-1]], axis=-1)
    return jnp.stack([yz - zy, zx - xz, xy - yx], axis=-4)


def coefficients(sigma):
    denom = 1.0 + loss_rate * sigma
    decay = (1.0 - loss_rate * sigma) / denom
    gain = ch_coef / denom
    decay_slope = -2.0 * loss_rate / (denom * denom)
    gain_slope = -ch_coef * loss_rate / (denom * denom)
    return decay, gain, decay_slope, gain_slope


def run_group(sigma, e_field, h_field, lam_e, lam_h, amps, tow, z_rec, x_rec, y_rec):
    decay, gain, decay_slope, gain_slope = coefficients(sigma)
    zero_z = jnp.zeros((2, 1, NX, NY), jnp.float32)
    zero_x = jnp.zeros((2, NZ, 1, NY), jnp.float32)
    flat = jnp.arange(NZ * NX * NY, dtype=jnp.int32).reshape(NZ, NX, NY)
    point = (flat == tow).astype(jnp.float32)
    blank = jnp.zeros((NZ, NX, NY), jnp.float32)
    kept = []
    samples = []
    for step in range(STEPS):
        h_field = h_field - ch_coef * curl_upper(e_field, zero_z, zero_x)
        drive = curl_lower(h_field, zero_z, zero_x) - jnp.stack([amps[step] * point, blank, blank], axis=0)
        kept.append((e_field, drive))
        e_field = decay * e_field + gain * drive
        samples.append(e_field[:, z_rec, x_rec, y_rec])
    total = jnp.zeros((NZ, NX, NY), jnp.float32)
    for step in range(STEPS - 1, -1, -1):
        e_old, drive = kept[step]
        total = total + jnp.sum(decay_slope * e_old * lam_e + gain_slope * drive * lam_e, axis=0)
        if step > 0:
            lam_h = lam_h + curl_upper(gain * lam_e, zero_z, zero_x)
            lam_e = decay * lam_e - ch_coef * curl_lower(lam_h, zero_z, zero_x)
    return total, jnp.stack(samples, axis=0)


def reference(conductivity, e_start, h_start, e_weight, h_weight, source_amp, tow_cell, rec_cell, rec_owner):
    blocks = jnp.arange(DEPTH_BLOCKS, dtype=jnp.int32)[:, None, None]
    tiles = jnp.arange(LAT_TILES, dtype=jnp.int32)[None, :, None]
    z_rec = blocks * CZ + rec_cell // (CX * NY)
    x_rec = tiles * CX + (rec_cell // NY) % CX
    y_rec = rec_cell % NY

    def one_group(total, inputs):
        e_field, h_field, lam_e, lam_h, amps, tow = inputs
        part, samples = run_group(conductivity, e_field, h_field, lam_e, lam_h, amps, tow, z_rec, x_rec, y_rec)
        return total + part, samples

    total, samples = lax.scan(one_group, jnp.zeros((NZ, NX, NY), jnp.float32),
                              (e_start, h_start, e_weight, h_weight, source_amp, tow_cell))
    values = jnp.transpose(samples, (0, 3, 4, 5, 1, 2)).reshape(GROUPS, DEPTH_BLOCKS, LAT_TILES, RPD, 3 * STEPS)
    owner = rec_owner[..., 0]
    order = jnp.arange(RPD, dtype=jnp.int32)
    same = owner[..., :, None] == owner[..., None, :]
    earlier = order[None, :] < order[:, None]
    rank = jnp.sum((same & earlier).astype(jnp.int32), axis=-1)
    owners = jnp.arange(LAT_TILES, dtype=jnp.int32)[:, None]
    slots = jnp.arange(CAP, dtype=jnp.int32)[None, :]
    hot = ((owner[..., None, None] == owners) & (rank[..., None, None] == slots)).astype(jnp.float32)
    table = jnp.sum(values[:, :, :, :, None, None, :] * hot[None, :, :, :, :, :, None], axis=3)
    return total, jnp.transpose(table, (0, 1, 3, 2, 4, 5))
```

```python
import functools

import jax
import jax.numpy as jnp
from jax import lax
from jax.experimental import pallas as pl
from jax.experimental.pallas import tpu as pltpu
from jax.sharding import PartitionSpec as P

CC = 0.5
KK = 0.5
ROWS = 24
F32 = jnp.float32
UP = ((0, 3), (3, 2), (5, 2), (7, 1), (8, 2))
DN = ((0, 3), (3, 3), (6, 2), (8, 2), (10, 2))
UP_ROWS = 9
DN_ROWS = 11


def shifted(block, axis, distance):
    n = lax.axis_size(axis)
    route = [(i, i + distance) for i in range(n) if 0 <= i + distance < n]
    return lax.ppermute(block, axis, route)


def lanes():
    return lax.broadcasted_iota(jnp.int32, (ROWS, 128), 1)


def zrow():
    r = lax.broadcasted_iota(jnp.int32, (ROWS, 128), 0)
    return jnp.where(r < 20, r, r - ROWS)


def yp(f):
    return jnp.where(lanes() == 127, 0.0, pltpu.roll(f, 127, 1))


def ym(f):
    return jnp.where(lanes() == 0, 0.0, pltpu.roll(f, 1, 1))


def zp(f):
    return pltpu.roll(f, ROWS - 1, 0)


def zm(f):
    return pltpu.roll(f, 1, 0)


def dpy(f):
    return yp(f) - f


def dpz(f):
    return zp(f) - f


def dmy(f):
    return f - ym(f)


def dmz(f):
    return f - zm(f)


def curl_p(f, nxt):
    fx, fy, fz = f
    return (dpy(fz) - dpz(fy), dpz(fx) - (nxt[2] - fz), (nxt[1] - fy) - dpy(fx))


def curl_m(f, prv):
    fx, fy, fz = f
    return (dmy(fz) - dmz(fy), dmz(fx) - (fz - prv[2]), (fy - prv[1]) - dmy(fx))


def slope(conductivity):
    return 1.0 / (1.0 + KK * conductivity)


def coefs(conductivity, keep):
    inv = slope(conductivity)
    a = jnp.where(keep, (1.0 - KK * conductivity) * inv, 0.0)
    b = jnp.where(keep, CC * inv, 0.0)
    return a, b


def first_row_mask(depth_at):
    return jnp.where((zrow() < 0) & (depth_at == 0), 0.0, 1.0)


def last_row_keep(depth_at, depth_n):
    return jnp.logical_not((zrow() > 15) & (depth_at == depth_n - 1))


def pack_kernel(e, h, le, lh, cond, up, dn, sems):
    copies = []

    def move(src, dst):
        c = pltpu.make_async_copy(src, dst, sems.at[len(copies)])
        c.start()
        copies.append(c)

    for field, ref in enumerate((e, h, le, lh)):
        at, n = UP[field]
        move(ref.at[:, :, pl.ds(0, n * 8)], up.at[:, :, pl.ds(at * 8, n * 8)])
        at, n = DN[field]
        move(ref.at[:, :, pl.ds((16 - n) * 8, n * 8)], dn.at[:, :, pl.ds(at * 8, n * 8)])
    for row in range(2):
        move(cond.at[pl.ds(row * 8, 8)], up.at[0, row, pl.ds((UP_ROWS - 1) * 8, 8)])
        move(cond.at[pl.ds((14 + row) * 8, 8)], dn.at[0, row, pl.ds((DN_ROWS - 1) * 8, 8)])
    for c in copies:
        c.wait()


def pack(e, h, le, lh, cond):
    g = e.shape[0]
    return pl.pallas_call(
        pack_kernel,
        out_shape=(
            jax.ShapeDtypeStruct((g, 3, UP_ROWS * 8, 128), F32),
            jax.ShapeDtypeStruct((g, 3, DN_ROWS * 8, 128), F32),
        ),
        in_specs=[pl.BlockSpec(memory_space=pl.ANY)] * 5,
        out_specs=(pl.BlockSpec(memory_space=pltpu.VMEM),) * 2,
        scratch_shapes=[pltpu.SemaphoreType.DMA((12,))],
        name="pack",
    )(e, h, le, lh, cond)


def halo_tile(up, dn, lead, x, field):
    r = lax.broadcasted_iota(jnp.int32, (8, 128), 0)
    at, _ = UP[field]
    s = min(at, UP_ROWS - 8)
    hi = up[(*lead, pl.ds(s * 8 + x, 8, stride=8), slice(None))]
    if at != s:
        hi = pltpu.roll(hi, (8 - (at - s)) % 8, 0)
    at, n = DN[field]
    s = min(at, DN_ROWS - 8)
    lo = dn[(*lead, pl.ds(s * 8 + x, 8, stride=8), slice(None))]
    turn = (8 - n - (at - s)) % 8
    if turn:
        lo = pltpu.roll(lo, turn, 0)
    return jnp.where(r < 4, hi, lo)


def planes_kernel(
    depth_n, lat_n, e, h, le, lh, cond, up, dn, amp, tow, te, th, tle, tlh, ta, tb, to_lo, to_hi
):
    groups = e.shape[0]
    depth_at = lax.axis_index("depth")
    lat_at = lax.axis_index("lat")
    for g in range(groups):

        def body(c, carry, g=g):
            for field, (src, dst) in enumerate(((e, te), (h, th), (le, tle), (lh, tlh))):
                for x in range(8):
                    dst[g, c, x, 0:8] = src[g, c, pl.ds(x, 8, stride=8), :]
                    dst[g, c, x, 8:16] = src[g, c, pl.ds(64 + x, 8, stride=8), :]
                    dst[g, c, x, 16:24] = halo_tile(up, dn, (g, c), x, field)
            return carry

        lax.fori_loop(0, 3, body, 0)
    keep = last_row_keep(depth_at, depth_n)
    r8 = lax.broadcasted_iota(jnp.int32, (8, 128), 0)
    u0 = up[0, 0, pl.ds((UP_ROWS - 1) * 8, 8), :]
    u1 = up[0, 1, pl.ds((UP_ROWS - 1) * 8, 8), :]
    d0 = dn[0, 0, pl.ds((DN_ROWS - 1) * 8, 8), :]
    d1 = dn[0, 1, pl.ds((DN_ROWS - 1) * 8, 8), :]
    for x in range(8):
        halo = jnp.where(r8 == 0, u0[x : x + 1], 1.0)
        halo = jnp.where(r8 == 1, u1[x : x + 1], halo)
        halo = jnp.where(r8 == 6, d0[x : x + 1], halo)
        halo = jnp.where(r8 == 7, d1[x : x + 1], halo)
        whole = jnp.concatenate(
            [cond[pl.ds(x, 8, stride=8), :], cond[pl.ds(64 + x, 8, stride=8), :], halo], axis=0
        )
        a, b = coefs(whole, keep)
        ta[x] = a
        tb[x] = b
        if x == 0:
            to_lo[groups * 11] = whole
        if x == 7:
            to_hi[groups * 13] = whole
    row_mask = first_row_mask(depth_at)
    z, lane = zrow(), lanes()

    def forward_planes(g, carry):
        s = -CC * row_mask
        cell = tow[g]
        lz = cell // (1024 * lat_n) - depth_at * 16
        lx = cell // 128 % (8 * lat_n) - lat_at * 8
        point = jnp.where((z == lz) & (lane == cell % 128), amp[g, 0], 0.0)

        def e0(x):
            return tuple(te[g, c, x] for c in range(3))

        def h0(x):
            return tuple(th[g, c, x] for c in range(3))

        def step_h(x):
            return tuple(f + s * k for f, k in zip(h0(x), curl_p(e0(x), e0(x + 1))))

        def put(ref, k, value):
            ref[g * (11 if ref is to_lo else 13) + k] = value

        a0, b0, a1, b1 = ta[0], tb[0], ta[1], tb[1]
        f0, f1 = e0(0), e0(1)
        h1 = step_h(0)
        put(to_lo, 0, f0[1])
        put(to_lo, 1, f0[2])
        put(to_lo, 2, a0 * f0[1] + b0 * (dmz(h1[0]) - h1[2]))
        put(to_lo, 3, a0 * f0[2] + b0 * (h1[1] - dmy(h1[0])))
        put(to_lo, 4, h1[0])
        hit = jnp.where(lx == 0, point, 0.0)
        ex = a0 * f0[0] + b0 * (dmy(h1[2]) - dmz(h1[1]) - hit)
        k1 = step_h(1)
        ey1 = a1 * f1[1] + b1 * (dmz(k1[0]) - k1[2] + h1[2])
        ez1 = a1 * f1[2] + b1 * (k1[1] - h1[1] - dmy(k1[0]))
        put(to_lo, 5, h1[1] + s * (dpz(ex) - ez1))
        put(to_lo, 6, h1[2] + s * (ey1 - dpy(ex)))
        a7, b7, a6, b6 = ta[7], tb[7], ta[6], tb[6]
        f7, f6 = e0(7), e0(6)
        g7 = h0(7)
        put(to_hi, 0, g7[1] + s * (dpz(f7[0]) + f7[2]))
        put(to_hi, 1, g7[2] - s * (f7[1] + dpy(f7[0])))
        put(to_hi, 2, f7[0])
        hx7 = g7[0] + s * (dpy(f7[2]) - dpz(f7[1]))
        h6 = step_h(6)
        put(to_hi, 3, a7 * f7[1] + b7 * (dmz(hx7) + h6[2]))
        put(to_hi, 4, a7 * f7[2] - b7 * (h6[1] + dmy(hx7)))
        put(to_hi, 5, hx7)
        h5 = step_h(5)
        m6 = curl_m(h6, h5)
        hit = jnp.where(lx == 6, point, 0.0)
        ex6 = a6 * f6[0] + b6 * (m6[0] - hit)
        ey6 = a6 * f6[1] + b6 * m6[1]
        ez6 = a6 * f6[2] + b6 * m6[2]
        put(to_hi, 6, h6[1] + s * (dpz(ex6) + ez6))
        put(to_hi, 7, h6[2] - s * (ey6 + dpy(ex6)))
        s = row_mask

        def l0(x):
            return tuple(tle[g, c, x] for c in range(3))

        def w0(x):
            return tuple(tb[x] * f for f in l0(x))

        def m0(x):
            return tuple(tlh[g, c, x] for c in range(3))

        def step_m(x):
            return tuple(f + s * k for f, k in zip(m0(x), curl_p(w0(x), w0(x + 1))))

        q0, v0 = l0(0), w0(0)
        m1 = step_m(0)
        put(to_lo, 7, v0[1])
        put(to_lo, 8, v0[2])
        put(to_lo, 9, a0 * q0[1] - CC * (dmz(m1[0]) - m1[2]))
        put(to_lo, 10, a0 * q0[2] - CC * (m1[1] - dmy(m1[0])))
        q7, v7, n7 = l0(7), w0(7), m0(7)
        put(to_hi, 8, n7[1] + s * (dpz(v7[0]) + v7[2]))
        put(to_hi, 9, n7[2] - s * (v7[1] + dpy(v7[0])))
        put(to_hi, 10, q7[0])
        mx7 = n7[0] + s * (dpy(v7[2]) - dpz(v7[1]))
        m6 = step_m(6)
        put(to_hi, 11, a7 * q7[1] - CC * (dmz(mx7) + m6[2]))
        put(to_hi, 12, a7 * q7[2] + CC * (m6[1] + dmy(mx7)))
        return carry

    lax.fori_loop(0, groups, forward_planes, 0)


def planes(e, h, le, lh, cond, up, dn, amp, tow, depth_n, lat_n):
    g = e.shape[0]
    vm = pl.BlockSpec(memory_space=pltpu.VMEM)
    sm = pl.BlockSpec(memory_space=pltpu.SMEM)
    field = jax.ShapeDtypeStruct((g, 3, 8, ROWS, 128), F32)
    coef = jax.ShapeDtypeStruct((8, ROWS, 128), F32)
    return pl.pallas_call(
        functools.partial(planes_kernel, depth_n, lat_n),
        out_shape=(
            field,
            field,
            field,
            field,
            coef,
            coef,
            jax.ShapeDtypeStruct((g * 11 + 1, ROWS, 128), F32),
            jax.ShapeDtypeStruct((g * 13 + 1, ROWS, 128), F32),
        ),
        in_specs=[vm] * 7 + [sm] * 2,
        out_specs=(vm,) * 8,
        compiler_params=pltpu.CompilerParams(vmem_limit_bytes=40 * 1024 * 1024),
        name="planes",
    )(e, h, le, lh, cond, up, dn, amp, tow)


def march_kernel(
    depth_n,
    lat_n,
    te,
    th,
    tle,
    tlh,
    ta,
    tb,
    cond,
    lo,
    hi,
    amp,
    tow,
    rcell,
    rowner,
    grad,
    send,
    ee,
    hh,
    ww,
    mm,
    l1,
    l2,
    acc,
    samp,
    count,
):
    groups = te.shape[0]
    depth_at = lax.axis_index("depth")
    lat_at = lax.axis_index("lat")
    row_mask = first_row_mask(depth_at)
    z, lane = zrow(), lanes()
    keep = last_row_keep(depth_at, depth_n)
    a8, b8 = coefs(hi[groups * 11], keep & (lat_at < lat_n - 1))
    al, bl = coefs(lo[groups * 13], keep)
    left = jnp.where(lat_at == 0, 0.0, 1.0)
    receivers = rcell.shape[0]

    def get(ref, g, x):
        return tuple(ref[g, c, x] for c in range(3))

    def put(ref, g, x, value):
        for c in range(3):
            ref[g, c, x] = value[c]

    def update_h(g, s, w, m):
        def body(x, carry):
            k = curl_p(get(w, g, x), get(w, g, x + 1))
            for c in range(3):
                m[g, c, x + 1] = m[g, c, x + 1] + s * k[c]
            return carry

        lax.fori_loop(0, 8, body, 0)

    def copy_in(g, carry):
        for c in range(3):
            for x in range(8):
                ee[g, c, x] = te[g, c, x]
                hh[g, c, x + 1] = th[g, c, x]
                mm[g, c, x + 1] = tlh[g, c, x]
                ww[g, c, x] = tb[x] * tle[g, c, x]
        return carry

    lax.fori_loop(0, groups, copy_in, 0)
    acc[...] = jnp.zeros_like(acc)

    def adjoint(g, carry):
        s = row_mask
        p, n = g * 11 + 7, g * 13 + 8
        ww[g, 1, 8] = hi[p]
        ww[g, 2, 8] = hi[p + 1]
        update_h(g, s, ww, mm)
        my = left * (lo[n] - s * ww[g, 2, 0])
        mz = left * (lo[n + 1] + s * ww[g, 1, 0])
        mm[g, 1, 0] = my
        mm[g, 2, 0] = mz

        def first(x, c0):
            k = curl_m(get(mm, g, x + 1), (None, mm[g, 1, x], mm[g, 2, x]))
            for c in range(3):
                new = ta[x] * tle[g, c, x] - CC * k[c]
                l1[g, c, x] = new
                ww[g, c, x] = tb[x] * new
            return c0

        lax.fori_loop(0, 8, first, 0)
        ww[g, 1, 8] = b8 * (hi[p + 2] - CC * mm[g, 2, 8])
        ww[g, 2, 8] = b8 * (hi[p + 3] + CC * mm[g, 1, 8])
        wx = bl * (al * lo[n + 2] - CC * (dmy(mz) - dmz(my)))
        wy = bl * (lo[n + 3] + CC * mz)
        wz = bl * (lo[n + 4] - CC * my)
        mm[g, 1, 0] = left * (my + s * (dpz(wx) - (ww[g, 2, 0] - wz)))
        mm[g, 2, 0] = left * (mz + s * ((ww[g, 1, 0] - wy) - dpy(wx)))
        update_h(g, s, ww, mm)

        def second(x, c0):
            k = curl_m(get(mm, g, x + 1), (None, mm[g, 1, x], mm[g, 2, x]))
            for c in range(3):
                l2[g, c, x] = ta[x] * l1[g, c, x] - CC * k[c]
            return c0

        lax.fori_loop(0, 8, second, 0)
        return carry

    lax.fori_loop(0, groups, adjoint, 0)

    def forward(g, carry):
        s = -CC * row_mask
        p, n = g * 11, g * 13
        cell = tow[g]
        lz = cell // (1024 * lat_n) - depth_at * 16
        lx = cell // 128 % (8 * lat_n) - lat_at * 8
        point = jnp.where((z == lz) & (lane == cell % 128), 1.0, 0.0)

        def update_e(step, weight):
            def body(x, c0):
                old = get(ee, g, x)
                k = curl_m(get(hh, g, x + 1), (None, hh[g, 1, x], hh[g, 2, x]))
                k = (k[0] - jnp.where(lx == x, amp[g, step], 0.0) * point, k[1], k[2])
                a, b = ta[x], tb[x]
                total = None
                for c in range(3):
                    t = (-2.0 * KK * old[c][0:16] - CC * KK * k[c][0:16]) * weight[g, c, x, 0:16]
                    total = t if total is None else total + t
                    ee[g, c, x] = a * old[c] + b * k[c]
                acc[x] += total
                return c0

            lax.fori_loop(0, 8, body, 0)

        def sample(step):
            def body(r, c0):
                cell_r = rcell[r]
                zr, xr, yr = cell_r // 1024, cell_r // 128 % 8, cell_r % 128
                one = lax.broadcasted_iota(jnp.int32, (1, 128), 1)
                for c in range(3):
                    row = ee[g, c, xr, pl.ds(zr, 1), :]
                    samp[r, pl.ds(g * 9 + 3 * step + c, 1), :] = jnp.where(one == yr, row, 0.0)
                return c0

            lax.fori_loop(0, receivers, body, 0)

        ee[g, 1, 8] = hi[p]
        ee[g, 2, 8] = hi[p + 1]
        hy = left * (lo[n] - s * ee[g, 2, 0])
        hz = left * (lo[n + 1] + s * ee[g, 1, 0])
        hh[g, 1, 0] = hy
        hh[g, 2, 0] = hz
        update_h(g, s, ee, hh)
        update_e(0, l2)
        sample(0)
        ey8 = hi[p + 2] + b8 * hh[g, 2, 8]
        ez8 = hi[p + 3] - b8 * hh[g, 1, 8]
        ee[g, 1, 8] = ey8
        ee[g, 2, 8] = ez8
        hit = jnp.where(lx == -1, amp[g, 0], 0.0) * point
        ex = al * lo[n + 2] + bl * (dmy(hz) - dmz(hy) - hit)
        ey = lo[n + 3] - bl * hz
        ez = lo[n + 4] + bl * hy
        hy2 = left * (hy + s * (dpz(ex) - (ee[g, 2, 0] - ez)))
        hz2 = left * (hz + s * ((ee[g, 1, 0] - ey) - dpy(ex)))
        hh[g, 1, 0] = hy2
        hh[g, 2, 0] = hz2
        update_h(g, s, ee, hh)
        update_e(1, l1)
        sample(1)
        gx = hi[p + 4] + s * (dpy(ez8) - dpz(ey8))
        gy = hi[p + 5] + s * ez8
        gz = hi[p + 6] - s * ey8
        ee[g, 1, 8] = a8 * ey8 + b8 * (dmz(gx) - gz + hh[g, 2, 8])
        ee[g, 2, 8] = a8 * ez8 + b8 * (gy - hh[g, 1, 8] - dmy(gx))
        hx2 = lo[n + 5] + s * (dpy(ez) - dpz(ey))
        hit = jnp.where(lx == -1, amp[g, 1], 0.0) * point
        hyf = lo[n + 6] - s * ez
        hzf = lo[n + 7] + s * ey
        ex2 = al * ex + bl * (dmy(hz2) - dmz(hy2) - hit)
        ey2 = al * ey + bl * (dmz(hx2) - hz2 + hzf)
        ez2 = al * ez + bl * (hy2 - hyf - dmy(hx2))
        hh[g, 1, 0] = left * (hy2 + s * (dpz(ex2) - (ee[g, 2, 0] - ez2)))
        hh[g, 2, 0] = left * (hz2 + s * ((ee[g, 1, 0] - ey2) - dpy(ex2)))
        update_h(g, s, ee, hh)
        update_e(2, tle)
        sample(2)
        return carry

    lax.fori_loop(0, groups, forward, 0)
    for x in range(8):
        for half in range(2):
            c = cond[pl.ds(half * 64 + x, 8, stride=8), :]
            inv = slope(c)
            grad[pl.ds(half * 64 + x, 8, stride=8), :] = acc[x, half * 8 : half * 8 + 8] * inv * inv
    send[...] = jnp.zeros_like(send)
    for o in range(send.shape[0]):
        count[o] = 0
    r24 = lax.broadcasted_iota(jnp.int32, (ROWS, 128), 0)

    def place(r, c0):
        o = rowner[r]
        slot = count[o]
        count[o] = slot + 1
        values = jnp.sum(samp[r], axis=-1, keepdims=True)
        used = (r24 == lane) & (r24 < groups * 9)
        row = jnp.sum(jnp.where(used, values, 0.0), axis=0, keepdims=True)
        send[o, pl.ds(slot, 1), :] = row
        return c0

    lax.fori_loop(0, receivers, place, 0)


def march(te, th, tle, tlh, ta, tb, cond, lo, hi, amp, tow, rcell, rowner, depth_n, lat_n):
    g = te.shape[0]
    vm = pl.BlockSpec(memory_space=pltpu.VMEM)
    sm = pl.BlockSpec(memory_space=pltpu.SMEM)
    return pl.pallas_call(
        functools.partial(march_kernel, depth_n, lat_n),
        out_shape=(
            jax.ShapeDtypeStruct((128, 128), F32),
            jax.ShapeDtypeStruct((lat_n, 8, 128), F32),
        ),
        in_specs=[vm] * 9 + [sm] * 4,
        out_specs=(vm,) * 2,
        scratch_shapes=[pltpu.VMEM((g, 3, 9, ROWS, 128), F32)] * 4
        + [pltpu.VMEM((g, 3, 8, ROWS, 128), F32)] * 2
        + [
            pltpu.VMEM((8, 16, 128), F32),
            pltpu.VMEM((rcell.shape[0], ROWS, 128), F32),
            pltpu.SMEM((lat_n,), jnp.int32),
        ],
        compiler_params=pltpu.CompilerParams(vmem_limit_bytes=40 * 1024 * 1024),
        name="march",
    )(te, th, tle, tlh, ta, tb, cond, lo, hi, amp, tow, rcell, rowner)


def src_sum(value):
    n = lax.axis_size("src")
    step = 1
    while step < n:
        value = value + lax.ppermute(value, "src", [(i, i ^ step) for i in range(n)])
        step *= 2
    return value


def per_device(
    conductivity, e_start, h_start, e_weight, h_weight, source_amp, tow_cell, rec_cell, rec_owner
):
    groups = e_start.shape[0]
    depth_n, lat_n = lax.axis_size("depth"), lax.axis_size("lat")

    def flat(f):
        return f.reshape(groups, 3, 128, 128)

    e, h, le, lh = flat(e_start), flat(h_start), flat(e_weight), flat(h_weight)
    cond = conductivity.reshape(128, 128)
    up, dn = pack(e, h, le, lh, cond)
    up = shifted(up, "depth", -1)
    dn = shifted(dn, "depth", 1)
    te, th, tle, tlh, ta, tb, to_lo, to_hi = planes(
        e, h, le, lh, cond, up, dn, source_amp, tow_cell, depth_n, lat_n
    )
    hi = shifted(to_lo, "lat", -1)
    lo = shifted(to_hi, "lat", 1)
    grad, send = march(
        te,
        th,
        tle,
        tlh,
        ta,
        tb,
        cond,
        lo,
        hi,
        source_amp,
        tow_cell,
        rec_cell.reshape(-1),
        rec_owner.reshape(-1),
        depth_n,
        lat_n,
    )
    got = lax.all_to_all(send, "lat", split_axis=0, concat_axis=0, tiled=True)
    total = src_sum(grad).reshape(16, 8, 128)
    lines = got[:, 0:2, 0 : groups * 9].reshape(lat_n, 2, groups, 9)
    lines = jnp.transpose(lines, (2, 0, 1, 3)).reshape(groups, 1, 1, lat_n, 2, 9)
    return (total, lines)


def solution(mesh):
    placed = (
        P("depth", "lat", None),
        P("src", None, "depth", "lat", None),
        P("src", None, "depth", "lat", None),
        P("src", None, "depth", "lat", None),
        P("src", None, "depth", "lat", None),
        P("src", None),
        P("src"),
        P("depth", "lat", None),
        P("depth", "lat", None, None),
    )
    return jax.shard_map(
        per_device,
        mesh=mesh,
        in_specs=placed,
        out_specs=(P("depth", "lat", None), P("src", "depth", "lat", None, None, None)),
        check_vma=False,
    )
```

```python
import functools

import jax
import jax.numpy as jnp
from jax import lax
from jax.experimental import pallas as pl
from jax.experimental.pallas import tpu as pltpu
from jax.sharding import PartitionSpec as P

CC = 0.5
KK = 0.5
ROWS = 24
F32 = jnp.float32
UP = ((0, 3), (3, 2), (5, 2), (7, 1), (8, 2))
DN = ((0, 3), (3, 3), (6, 2), (8, 2), (10, 2))
UP_ROWS = 9
DN_ROWS = 11


def shifted(block, axis, distance):
    n = lax.axis_size(axis)
    route = [(i, i + distance) for i in range(n) if 0 <= i + distance < n]
    return lax.ppermute(block, axis, route)


def swapped(block, axis, first):
    n = lax.axis_size(axis)
    lower = range(first, n - 1, 2)
    return lax.ppermute(block, axis, [p for i in lower for p in ((i, i + 1), (i + 1, i))])


def lanes():
    return lax.broadcasted_iota(jnp.int32, (ROWS, 128), 1)


def zrow():
    r = lax.broadcasted_iota(jnp.int32, (ROWS, 128), 0)
    return jnp.where(r < 20, r, r - ROWS)


def yp(f):
    return jnp.where(lanes() == 127, 0.0, pltpu.roll(f, 127, 1))


def ym(f):
    return jnp.where(lanes() == 0, 0.0, pltpu.roll(f, 1, 1))


def zp(f):
    return pltpu.roll(f, ROWS - 1, 0)


def zm(f):
    return pltpu.roll(f, 1, 0)


def dpy(f):
    return yp(f) - f


def dpz(f):
    return zp(f) - f


def dmy(f):
    return f - ym(f)


def dmz(f):
    return f - zm(f)


def curl_p(f, nxt):
    fx, fy, fz = f
    return (dpy(fz) - dpz(fy), dpz(fx) - (nxt[2] - fz), (nxt[1] - fy) - dpy(fx))


def curl_m(f, prv):
    fx, fy, fz = f
    return (dmy(fz) - dmz(fy), dmz(fx) - (fz - prv[2]), (fy - prv[1]) - dmy(fx))


def coefs(conductivity, keep):
    inv = 1.0 / (1.0 + KK * conductivity)
    a = jnp.where(keep, (1.0 - KK * conductivity) * inv, 0.0)
    b = jnp.where(keep, CC * inv, 0.0)
    return a, b


def first_row_mask(depth_at):
    return jnp.where((zrow() < 0) & (depth_at == 0), 0.0, 1.0)


def last_row_keep(depth_at, depth_n):
    return jnp.logical_not((zrow() > 15) & (depth_at == depth_n - 1))


def pack_kernel(e, h, le, lh, cond, one, two, sems):
    even = lax.axis_index("depth") % 2 == 0

    def fill(up, dn):
        copies = []

        def move(src, dst):
            c = pltpu.make_async_copy(src, dst, sems.at[len(copies)])
            c.start()
            copies.append(c)

        for field, ref in enumerate((e, h, le, lh)):
            at, n = UP[field]
            move(ref.at[:, :, pl.ds(0, n * 8)], up.at[:, :, pl.ds(at * 8, n * 8)])
            at, n = DN[field]
            move(ref.at[:, :, pl.ds((16 - n) * 8, n * 8)], dn.at[:, :, pl.ds(at * 8, n * 8)])
        for row in range(2):
            move(cond.at[pl.ds(row * 8, 8)], up.at[0, row, pl.ds((UP_ROWS - 1) * 8, 8)])
            move(cond.at[pl.ds((14 + row) * 8, 8)], dn.at[0, row, pl.ds((DN_ROWS - 1) * 8, 8)])
        for c in copies:
            c.wait()

    @pl.when(even)
    def _():
        fill(two, one)

    @pl.when(jnp.logical_not(even))
    def _():
        fill(one, two)


def pack(e, h, le, lh, cond):
    message = jax.ShapeDtypeStruct((e.shape[0], 3, DN_ROWS * 8, 128), F32)
    return pl.pallas_call(
        pack_kernel,
        out_shape=(message, message),
        in_specs=[pl.BlockSpec(memory_space=pl.ANY)] * 5,
        out_specs=(pl.BlockSpec(memory_space=pltpu.VMEM),) * 2,
        scratch_shapes=[pltpu.SemaphoreType.DMA((12,))],
        name="pack",
    )(e, h, le, lh, cond)


TO_LO = ((3, 17),) * 2 + ((2, 16),) * 2 + ((2, 15),) + ((1, 15),) * 2 + ((2, 16),) * 2 + ((1, 15),) * 2
TO_HI = (
    ((3, 17),) * 2
    + ((2, 17),)
    + ((2, 16),) * 2
    + ((2, 15),)
    + ((1, 15),) * 2
    + ((2, 16),) * 2
    + ((1, 16),)
    + ((1, 15),) * 2
)


def offset(table, k):
    return sum(lo + hi + 1 for lo, hi in table[:k])


def chunk(table):
    return -(-(offset(table, len(table)) + 12) // 8) * 8


def put_plane(ref, table, g, k, value):
    lo, hi = table[k]
    at = offset(table, k)
    ref[g, at : at + hi + 1] = value[0 : hi + 1]
    ref[g, at + hi + 1 : at + hi + 1 + lo] = value[ROWS - lo : ROWS]


def get_plane(ref, table, g, k):
    lo, hi = table[k]
    at = offset(table, k)
    end = at + lo + hi + 1
    rest = ref[g, end - 8 : end]
    if hi > 15:
        r = lax.broadcasted_iota(jnp.int32, (8, 128), 0)
        rest = jnp.where(r < 4, ref[g, at + 16 : at + 24], rest)
    return jnp.concatenate([ref[g, at : at + 16], rest], axis=0)


def put_conductivity(ref, table, value):
    at = offset(table, len(table))
    ref[0, at : at + 8] = value[0:8]
    ref[1, at : at + 8] = value[8:16]
    ref[1, at + 8 : at + 10] = value[16:18]
    ref[1, at + 10 : at + 12] = value[22:24]


def get_conductivity(ref, table):
    at = offset(table, len(table))
    r = lax.broadcasted_iota(jnp.int32, (8, 128), 0)
    rest = ref[1, at + 4 : at + 12]
    rest = jnp.where(r < 4, pltpu.roll(rest, 4, 0), rest)
    return jnp.concatenate([ref[0, at : at + 8], ref[1, at : at + 8], rest], axis=0)


def halo_tile(up, dn, lead, x, field):
    r = lax.broadcasted_iota(jnp.int32, (8, 128), 0)
    at, _ = UP[field]
    s = min(at, UP_ROWS - 8)
    hi = up[(*lead, pl.ds(s * 8 + x, 8, stride=8), slice(None))]
    if at != s:
        hi = pltpu.roll(hi, (8 - (at - s)) % 8, 0)
    at, n = DN[field]
    s = min(at, DN_ROWS - 8)
    lo = dn[(*lead, pl.ds(s * 8 + x, 8, stride=8), slice(None))]
    turn = (8 - n - (at - s)) % 8
    if turn:
        lo = pltpu.roll(lo, turn, 0)
    return jnp.where(r < 4, hi, lo)


def own_kernel(e, h, le, lh, cond, te, th, tle, tlh, tc, be, bh, ble, blh, bc, sems):
    pairs = ((e, be), (h, bh), (le, ble), (lh, blh), (cond, bc))
    copies = [pltpu.make_async_copy(src, dst, sems.at[k]) for k, (src, dst) in enumerate(pairs)]
    for c in copies:
        c.start()
    for k, (src, dst) in enumerate(((be, te), (bh, th), (ble, tle), (blh, tlh))):
        copies[k].wait()

        def body(g, carry, src=src, dst=dst):
            for c in range(3):
                for x in range(8):
                    dst[g, c, x, 0:8] = src[g, c, pl.ds(x, 8, stride=8), :]
                    dst[g, c, x, 8:16] = src[g, c, pl.ds(64 + x, 8, stride=8), :]
            return carry

        lax.fori_loop(0, e.shape[0], body, 0)
    copies[4].wait()
    for x in range(8):
        tc[x, 0:8] = bc[pl.ds(x, 8, stride=8), :]
        tc[x, 8:16] = bc[pl.ds(64 + x, 8, stride=8), :]


def own_planes(e, h, le, lh, cond):
    g = e.shape[0]
    vm = pl.BlockSpec(memory_space=pltpu.VMEM)
    field = jax.ShapeDtypeStruct((g, 3, 8, ROWS, 128), F32)
    return pl.pallas_call(
        own_kernel,
        out_shape=(field,) * 4 + (jax.ShapeDtypeStruct((8, 16, 128), F32),),
        in_specs=[pl.BlockSpec(memory_space=pltpu.HBM)] * 5,
        out_specs=(vm,) * 5,
        scratch_shapes=[pltpu.VMEM((g, 3, 128, 128), F32)] * 4
        + [pltpu.VMEM((128, 128), F32), pltpu.SemaphoreType.DMA((5,))],
        cost_estimate=pl.CostEstimate(flops=5_000_000, bytes_accessed=8_000_000, transcendentals=0),
        compiler_params=pltpu.CompilerParams(vmem_limit_bytes=24 * 1024 * 1024),
        name="own",
    )(e, h, le, lh, cond)


def planes_kernel(
    depth_n,
    lat_n,
    ie,
    ih,
    ile,
    ilh,
    tc,
    one,
    two,
    amp,
    tow,
    te,
    th,
    tle,
    tlh,
    ta,
    tb,
    to_lo,
    to_hi,
):
    groups = te.shape[0]
    depth_at = lax.axis_index("depth")
    lat_at = lax.axis_index("lat")

    even = depth_at % 2 == 0

    def halos(up, dn):
        def halo(g, carry):
            for c in range(3):
                for field, dst in enumerate((te, th, tle, tlh)):
                    for x in range(8):
                        dst[g, c, x, 16:24] = halo_tile(up, dn, (g, c), x, field)
            return carry

        lax.fori_loop(0, groups, halo, 0)

    @pl.when(even)
    def _():
        halos(one, two)

    @pl.when(jnp.logical_not(even))
    def _():
        halos(two, one)

    keep = last_row_keep(depth_at, depth_n)
    r8 = lax.broadcasted_iota(jnp.int32, (8, 128), 0)

    def edge(first, second, row, at):
        rows = pl.ds((at - 1) * 8, 8)
        return jnp.where(even, first[0, row, rows, :], second[0, row, rows, :])

    u0, u1 = (edge(one, two, row, UP_ROWS) for row in range(2))
    d0, d1 = (edge(two, one, row, DN_ROWS) for row in range(2))
    for x in range(8):
        rest = jnp.where(r8 == 0, u0[x : x + 1], 1.0)
        rest = jnp.where(r8 == 1, u1[x : x + 1], rest)
        rest = jnp.where(r8 == 6, d0[x : x + 1], rest)
        rest = jnp.where(r8 == 7, d1[x : x + 1], rest)
        whole = jnp.concatenate([tc[x], rest], axis=0)
        a, b = coefs(whole, keep)
        ta[x] = a
        tb[x] = b
        if x == 0:
            put_conductivity(to_lo, TO_LO, whole)
        if x == 7:
            put_conductivity(to_hi, TO_HI, whole)
    row_mask = first_row_mask(depth_at)
    z, lane = zrow(), lanes()

    def forward_planes(g, carry):
        s = -CC * row_mask
        cell = tow[g]
        lz = cell // (1024 * lat_n) - depth_at * 16
        lx = cell // 128 % (8 * lat_n) - lat_at * 8
        point = jnp.where((z == lz) & (lane == cell % 128), amp[g, 0], 0.0)

        def e0(x):
            return tuple(te[g, c, x] for c in range(3))

        def h0(x):
            return tuple(th[g, c, x] for c in range(3))

        def step_h(x):
            return tuple(f + s * k for f, k in zip(h0(x), curl_p(e0(x), e0(x + 1))))

        def put(ref, k, value):
            put_plane(ref, TO_LO if ref is to_lo else TO_HI, g, k, value)

        a0, b0, a1, b1 = ta[0], tb[0], ta[1], tb[1]
        f0, f1 = e0(0), e0(1)
        h1 = step_h(0)
        put(to_lo, 0, f0[1])
        put(to_lo, 1, f0[2])
        put(to_lo, 2, a0 * f0[1] + b0 * (dmz(h1[0]) - h1[2]))
        put(to_lo, 3, a0 * f0[2] + b0 * (h1[1] - dmy(h1[0])))
        put(to_lo, 4, h1[0])
        hit = jnp.where(lx == 0, point, 0.0)
        ex = a0 * f0[0] + b0 * (dmy(h1[2]) - dmz(h1[1]) - hit)
        k1 = step_h(1)
        ey1 = a1 * f1[1] + b1 * (dmz(k1[0]) - k1[2] + h1[2])
        ez1 = a1 * f1[2] + b1 * (k1[1] - h1[1] - dmy(k1[0]))
        put(to_lo, 5, h1[1] + s * (dpz(ex) - ez1))
        put(to_lo, 6, h1[2] + s * (ey1 - dpy(ex)))
        a7, b7, a6, b6 = ta[7], tb[7], ta[6], tb[6]
        f7, f6 = e0(7), e0(6)
        g7 = h0(7)
        put(to_hi, 0, g7[1] + s * (dpz(f7[0]) + f7[2]))
        put(to_hi, 1, g7[2] - s * (f7[1] + dpy(f7[0])))
        put(to_hi, 2, f7[0])
        hx7 = g7[0] + s * (dpy(f7[2]) - dpz(f7[1]))
        h6 = step_h(6)
        put(to_hi, 3, a7 * f7[1] + b7 * (dmz(hx7) + h6[2]))
        put(to_hi, 4, a7 * f7[2] - b7 * (h6[1] + dmy(hx7)))
        put(to_hi, 5, hx7)
        h5 = step_h(5)
        m6 = curl_m(h6, h5)
        hit = jnp.where(lx == 6, point, 0.0)
        ex6 = a6 * f6[0] + b6 * (m6[0] - hit)
        ey6 = a6 * f6[1] + b6 * m6[1]
        ez6 = a6 * f6[2] + b6 * m6[2]
        put(to_hi, 6, h6[1] + s * (dpz(ex6) + ez6))
        put(to_hi, 7, h6[2] - s * (ey6 + dpy(ex6)))
        s = row_mask

        def l0(x):
            return tuple(tle[g, c, x] for c in range(3))

        def w0(x):
            return tuple(tb[x] * f for f in l0(x))

        def m0(x):
            return tuple(tlh[g, c, x] for c in range(3))

        def step_m(x):
            return tuple(f + s * k for f, k in zip(m0(x), curl_p(w0(x), w0(x + 1))))

        q0, v0 = l0(0), w0(0)
        m1 = step_m(0)
        put(to_lo, 7, v0[1])
        put(to_lo, 8, v0[2])
        put(to_lo, 9, a0 * q0[1] - CC * (dmz(m1[0]) - m1[2]))
        put(to_lo, 10, a0 * q0[2] - CC * (m1[1] - dmy(m1[0])))
        q7, v7, n7 = l0(7), w0(7), m0(7)
        put(to_hi, 8, n7[1] + s * (dpz(v7[0]) + v7[2]))
        put(to_hi, 9, n7[2] - s * (v7[1] + dpy(v7[0])))
        put(to_hi, 10, q7[0])
        mx7 = n7[0] + s * (dpy(v7[2]) - dpz(v7[1]))
        m6 = step_m(6)
        put(to_hi, 11, a7 * q7[1] - CC * (dmz(mx7) + m6[2]))
        put(to_hi, 12, a7 * q7[2] + CC * (m6[1] + dmy(mx7)))
        return carry

    lax.fori_loop(0, groups, forward_planes, 0)


def planes(own, one, two, amp, tow, depth_n, lat_n):
    g = one.shape[0]
    vm = pl.BlockSpec(memory_space=pltpu.VMEM)
    sm = pl.BlockSpec(memory_space=pltpu.SMEM)
    field = jax.ShapeDtypeStruct((g, 3, 8, ROWS, 128), F32)
    coef = jax.ShapeDtypeStruct((8, ROWS, 128), F32)
    return pl.pallas_call(
        functools.partial(planes_kernel, depth_n, lat_n),
        out_shape=(
            field,
            field,
            field,
            field,
            coef,
            coef,
            jax.ShapeDtypeStruct((g, chunk(TO_LO), 128), F32),
            jax.ShapeDtypeStruct((g, chunk(TO_HI), 128), F32),
        ),
        in_specs=[vm] * 7 + [sm] * 2,
        out_specs=(vm,) * 8,
        input_output_aliases={0: 0, 1: 1, 2: 2, 3: 3},
        compiler_params=pltpu.CompilerParams(vmem_limit_bytes=24 * 1024 * 1024),
        name="planes",
    )(*own, one, two, amp, tow)


SLOTS = 24
STRIDE = 8 * ROWS


def e_at(g, n, c, x):
    return pl.ds(pl.multiple_of((g * 9 + n * 3 + c) * STRIDE + x * ROWS, 8), ROWS)


def triple(ref, g, x):
    return tuple(ref[g, c, x] for c in range(3))


def inside(n, x):
    return n + 1 <= x <= 6 - n


def weighted(old, drive, weight):
    total = None
    for c in range(3):
        t = (-2.0 * KK * old[c][0:16] - CC * KK * drive[c][0:16]) * weight[c][0:16]
        total = t if total is None else total + t
    return total


def take_samples(store, rcell, use, put):
    k = lax.broadcasted_iota(jnp.int32, (SLOTS, 128), 0)
    step = k // 3 % 3
    lane = lanes()

    def body(r, c0):
        cell = rcell[r]
        z, x, y = cell // 1024, cell // 128 % 8, cell % 128
        rows = store[pl.ds(x * ROWS + z, SLOTS, stride=STRIDE), :]
        near = (x >= step + 1) & (x <= 6 - step)
        put(r, jnp.where((lane == y) & use(near), rows, 0.0))
        return c0

    lax.fori_loop(0, rcell.shape[0], body, 0, unroll=4)


def tow_at(tow, g, depth_at, lat_at, lat_n):
    cell = tow[g]
    lz = cell // (1024 * lat_n) - depth_at * 16
    lx = cell // 128 % (8 * lat_n) - lat_at * 8
    point = jnp.where((zrow() == lz) & (lanes() == cell % 128), 1.0, 0.0)
    return lx, point


def inner_kernel(
    lat_n, te, th, tle, tlh, ta, tb, amp, tow, rcell, hh, mm, l1, l2, d0, ei, acc, samp
):
    groups = te.shape[0]
    depth_at = lax.axis_index("depth")
    lat_at = lax.axis_index("lat")
    row_mask = first_row_mask(depth_at)
    acc[...] = jnp.zeros_like(acc)

    def one_group(g, carry):
        lx, point = tow_at(tow, g, depth_at, lat_at, lat_n)
        lam = (tle, l1, l2)
        s = row_mask
        for n in range(2):
            w = {}

            def scaled(x, n=n, w=w):
                if x not in w:
                    w[x] = tuple(tb[x] * f for f in triple(lam[n], g, x))
                return w[x]

            for x in range(n, 7 - n):
                k = curl_p(scaled(x), scaled(x + 1))
                base = triple(tlh if n == 0 else mm, g, x)
                for c in range(3):
                    mm[g, c, x] = base[c] + s * k[c]
            for x in range(n + 1, 7 - n):
                k = curl_m(triple(mm, g, x), triple(mm, g, x - 1))
                old = triple(lam[n], g, x)
                for c in range(3):
                    lam[n + 1][g, c, x] = ta[x] * old[c] - CC * k[c]
        s = -CC * row_mask

        def e_of(n, x):
            if n == 0:
                return triple(te, g, x)
            return tuple(ei[e_at(g, n - 1, c, x), :] for c in range(3))

        for n in range(3):
            for x in range(n, 7 - n):
                k = curl_p(e_of(n, x), e_of(n, x + 1))
                base = triple(th if n == 0 else hh, g, x)
                for c in range(3):
                    hh[g, c, x] = base[c] + s * k[c]
            for x in range(n + 1, 7 - n):
                k = curl_m(triple(hh, g, x), triple(hh, g, x - 1))
                k = (k[0] - jnp.where(lx == x, amp[g, n], 0.0) * point, k[1], k[2])
                old = e_of(n, x)
                for c in range(3):
                    ei[e_at(g, n, c, x), :] = ta[x] * old[c] + tb[x] * k[c]
                if n == 0 and x in (1, 6):
                    for c in range(3):
                        d0[g, c, x // 6] = k[c][0:16]
                else:
                    acc[x] += weighted(old, k, triple(lam[2 - n], g, x))
        return carry

    lax.fori_loop(0, groups, one_group, 0)

    def put(r, values):
        samp[r] = values

    take_samples(ei, rcell, lambda near: near, put)


def inner(te, th, tle, tlh, ta, tb, amp, tow, rcell, lat_n):
    g, n = te.shape[0], rcell.shape[0]
    vm = pl.BlockSpec(memory_space=pltpu.VMEM)
    sm = pl.BlockSpec(memory_space=pltpu.SMEM)
    field = jax.ShapeDtypeStruct((g, 3, 8, ROWS, 128), F32)
    return pl.pallas_call(
        functools.partial(inner_kernel, lat_n),
        out_shape=(
            field,
            field,
            field,
            field,
            jax.ShapeDtypeStruct((g, 3, 2, 16, 128), F32),
            jax.ShapeDtypeStruct((SLOTS * STRIDE, 128), F32),
            jax.ShapeDtypeStruct((8, 16, 128), F32),
            jax.ShapeDtypeStruct((n, SLOTS, 128), F32),
        ),
        in_specs=[vm] * 6 + [sm] * 3,
        out_specs=(vm,) * 8,
        cost_estimate=pl.CostEstimate(flops=20_000_000, bytes_accessed=12_000_000, transcendentals=0),
        compiler_params=pltpu.CompilerParams(vmem_limit_bytes=24 * 1024 * 1024),
        name="inner",
    )(te, th, tle, tlh, ta, tb, amp, tow, rcell)


def outer_kernel(
    depth_n,
    lat_n,
    te,
    th,
    tle,
    tlh,
    ta,
    tb,
    hh,
    mm,
    l1,
    l2,
    d0,
    ei,
    acc,
    samp,
    lo,
    hi,
    amp,
    tow,
    rcell,
    rowner,
    grad,
    send,
    eo,
    ho,
    mo,
    o1,
    o2,
    total,
    count,
):
    groups = te.shape[0]
    depth_at = lax.axis_index("depth")
    lat_at = lax.axis_index("lat")
    row_mask = first_row_mask(depth_at)
    keep = last_row_keep(depth_at, depth_n)
    a8, b8 = coefs(get_conductivity(hi, TO_LO), keep & (lat_at < lat_n - 1))
    al, bl = coefs(get_conductivity(lo, TO_HI), keep)
    left = jnp.where(lat_at == 0, 0.0, 1.0)
    total[...] = acc[...]

    def lam(n, g, x):
        if n == 0:
            return triple(tle, g, x)
        near = inside(n - 1, x)
        return triple((l1 if near else o1) if n == 1 else (l2 if near else o2), g, x)

    def one_group(g, carry):
        def high(k):
            return get_plane(hi, TO_LO, g, k)

        def low(k):
            return get_plane(lo, TO_HI, g, k)

        lx, point = tow_at(tow, g, depth_at, lat_at, lat_n)
        s = row_mask
        p, q = 7, 8

        def m_of(n, x):
            return triple(mm if n <= x <= 6 - n else mo, g, x)

        def m_step(n, nxt):
            w = {8: nxt}

            def scaled(x):
                if x not in w:
                    w[x] = tuple(tb[x] * f for f in lam(n, g, x))
                return w[x]

            for x in range(8):
                if n <= x <= 6 - n:
                    continue
                k = curl_p(scaled(x), scaled(x + 1))
                base = triple(tlh, g, x) if n == 0 else m_of(n - 1, x)
                for c in range(3):
                    mo[g, c, x] = base[c] + s * k[c]

        def l_step(n, prv):
            out = (o1, o2)[n]
            for x in range(8):
                if inside(n, x):
                    continue
                k = curl_m(m_of(n, x), m_of(n, x - 1) if x else prv)
                old = lam(n, g, x)
                for c in range(3):
                    out[g, c, x] = ta[x] * old[c] - CC * k[c]

        m_step(0, (None, high(p), high(p + 1)))
        first = lam(0, g, 0)
        my = left * (low(q) - s * (tb[0] * first[2]))
        mz = left * (low(q + 1) + s * (tb[0] * first[1]))
        l_step(0, (None, my, mz))
        last = m_of(0, 7)
        m_step(1, (None, b8 * (high(p + 2) - CC * last[2]), b8 * (high(p + 3) + CC * last[1])))
        wx = bl * (al * low(q + 2) - CC * (dmy(mz) - dmz(my)))
        wy = bl * (low(q + 3) + CC * mz)
        wz = bl * (low(q + 4) - CC * my)
        first = lam(1, g, 0)
        my = left * (my + s * (dpz(wx) - (tb[0] * first[2] - wz)))
        mz = left * (mz + s * ((tb[0] * first[1] - wy) - dpy(wx)))
        l_step(1, (None, my, mz))
        s = -CC * row_mask
        p, q = 0, 0

        def e_of(n, x):
            if n == 0:
                return triple(te, g, x)
            ref = ei if inside(n - 1, x) else eo
            return tuple(ref[e_at(g, n - 1, c, x), :] for c in range(3))

        def h_of(n, x):
            return triple(hh if n <= x <= 6 - n else ho, g, x)

        def h_step(n, nxt):
            for x in range(8):
                if n <= x <= 6 - n:
                    continue
                k = curl_p(e_of(n, x), nxt if x == 7 else e_of(n, x + 1))
                base = triple(th, g, x) if n == 0 else h_of(n - 1, x)
                for c in range(3):
                    ho[g, c, x] = base[c] + s * k[c]

        def e_step(n, prv):
            for x in range(8):
                old = e_of(n, x)
                if inside(n, x):
                    if n == 0 and x in (1, 6):
                        k = tuple(d0[g, c, x // 6] for c in range(3))
                        total[x] += weighted(old, k, lam(2, g, x))
                    continue
                k = curl_m(h_of(n, x), h_of(n, x - 1) if x else prv)
                k = (k[0] - jnp.where(lx == x, amp[g, n], 0.0) * point, k[1], k[2])
                for c in range(3):
                    eo[e_at(g, n, c, x), :] = ta[x] * old[c] + tb[x] * k[c]
                total[x] += weighted(old, k, lam(2 - n, g, x))

        def drop(n):
            return jnp.where(lx == -1, amp[g, n], 0.0) * point

        h_step(0, (None, high(p), high(p + 1)))
        first = e_of(0, 0)
        hy = left * (low(q) - s * first[2])
        hz = left * (low(q + 1) + s * first[1])
        e_step(0, (None, hy, hz))
        last = h_of(0, 7)
        ey8 = high(p + 2) + b8 * last[2]
        ez8 = high(p + 3) - b8 * last[1]
        ex = al * low(q + 2) + bl * (dmy(hz) - dmz(hy) - drop(0))
        ey = low(q + 3) - bl * hz
        ez = low(q + 4) + bl * hy
        h_step(1, (None, ey8, ez8))
        first = e_of(1, 0)
        hy2 = left * (hy + s * (dpz(ex) - (first[2] - ez)))
        hz2 = left * (hz + s * ((first[1] - ey) - dpy(ex)))
        e_step(1, (None, hy2, hz2))
        last = h_of(1, 7)
        gx = high(p + 4) + s * (dpy(ez8) - dpz(ey8))
        gy = high(p + 5) + s * ez8
        gz = high(p + 6) - s * ey8
        ey9 = a8 * ey8 + b8 * (dmz(gx) - gz + last[2])
        ez9 = a8 * ez8 + b8 * (gy - last[1] - dmy(gx))
        hx2 = low(q + 5) + s * (dpy(ez) - dpz(ey))
        hyf = low(q + 6) - s * ez
        hzf = low(q + 7) + s * ey
        ex2 = al * ex + bl * (dmy(hz2) - dmz(hy2) - drop(1))
        ey2 = al * ey + bl * (dmz(hx2) - hz2 + hzf)
        ez2 = al * ez + bl * (hy2 - hyf - dmy(hx2))
        h_step(2, (None, ey9, ez9))
        first = e_of(2, 0)
        hy3 = left * (hy2 + s * (dpz(ex2) - (first[2] - ez2)))
        hz3 = left * (hz2 + s * ((first[1] - ey2) - dpy(ex2)))
        e_step(2, (None, hy3, hz3))
        return carry

    lax.fori_loop(0, groups, one_group, 0)
    for x in range(8):
        for half in range(2):
            rows = pl.ds(half * 64 + x, 8, stride=8)
            inv = tb[x, half * 8 : half * 8 + 8] * (1.0 / CC)
            grad[rows, :] = total[x, half * 8 : half * 8 + 8] * inv * inv
    send[...] = jnp.zeros_like(send)
    for o in range(send.shape[0]):
        count[o] = 0
    r24, lane = lax.broadcasted_iota(jnp.int32, (SLOTS, 128), 0), lanes()
    used = (r24 == lane) & (r24 < groups * 9)

    def put(r, values):
        o = rowner[r]
        slot = count[o]
        count[o] = slot + 1
        values = jnp.sum(samp[r] + values, axis=-1, keepdims=True)
        send[o, pl.ds(slot, 1), :] = jnp.sum(jnp.where(used, values, 0.0), axis=0, keepdims=True)

    take_samples(eo, rcell, jnp.logical_not, put)


def outer(te, th, tle, tlh, ta, tb, kept, lo, hi, amp, tow, rcell, rowner, depth_n, lat_n):
    g = te.shape[0]
    vm = pl.BlockSpec(memory_space=pltpu.VMEM)
    sm = pl.BlockSpec(memory_space=pltpu.SMEM)
    return pl.pallas_call(
        functools.partial(outer_kernel, depth_n, lat_n),
        out_shape=(
            jax.ShapeDtypeStruct((128, 128), F32),
            jax.ShapeDtypeStruct((lat_n, 8, 128), F32),
        ),
        in_specs=[vm] * 16 + [sm] * 4,
        out_specs=(vm,) * 2,
        scratch_shapes=[pltpu.VMEM((SLOTS * STRIDE, 128), F32)]
        + [pltpu.VMEM((g, 3, 8, ROWS, 128), F32)] * 4
        + [pltpu.VMEM((8, 16, 128), F32), pltpu.SMEM((lat_n,), jnp.int32)],
        cost_estimate=pl.CostEstimate(flops=10_000_000, bytes_accessed=12_000_000, transcendentals=0),
        compiler_params=pltpu.CompilerParams(vmem_limit_bytes=24 * 1024 * 1024),
        name="outer",
    )(te, th, tle, tlh, ta, tb, *kept, lo, hi, amp, tow, rcell, rowner)


def finish_kernel(mine, theirs, got, total, lines):
    total[...] = mine[...] + theirs[...]
    for slot in range(2):
        table = jnp.transpose(got[:, slot, :])
        for g in range(lines.shape[0]):
            lines[g, :, slot, :] = table[g * 9 : g * 9 + 9]


def finish(mine, theirs, got, groups):
    vm = pl.BlockSpec(memory_space=pltpu.VMEM)
    return pl.pallas_call(
        finish_kernel,
        out_shape=(
            jax.ShapeDtypeStruct(mine.shape, F32),
            jax.ShapeDtypeStruct((groups, 9, 2, got.shape[0]), F32),
        ),
        in_specs=[vm] * 3,
        out_specs=(vm,) * 2,
        compiler_params=pltpu.CompilerParams(vmem_limit_bytes=24 * 1024 * 1024),
        name="finish",
    )(mine, theirs, got)


def across(value, step):
    n = lax.axis_size("src")
    return lax.ppermute(value, "src", [(i, i ^ step) for i in range(n) if i ^ step < n])


def per_device(
    conductivity, e_start, h_start, e_weight, h_weight, source_amp, tow_cell, rec_cell, rec_owner
):
    groups = e_start.shape[0]
    depth_n, lat_n = lax.axis_size("depth"), lax.axis_size("lat")

    def flat(f):
        return f.reshape(groups, 3, 128, 128)

    e, h, le, lh = flat(e_start), flat(h_start), flat(e_weight), flat(h_weight)
    cond = conductivity.reshape(128, 128)
    one, two = pack(e, h, le, lh, cond)
    one = swapped(one, "depth", 0)
    two = swapped(two, "depth", 1)
    own = own_planes(e, h, le, lh, cond)
    te, th, tle, tlh, ta, tb, to_lo, to_hi = planes(
        own, one, two, source_amp, tow_cell, depth_n, lat_n
    )
    cells, owners = rec_cell.reshape(-1), rec_owner.reshape(-1)
    hi = shifted(to_lo, "lat", -1)
    lo = shifted(to_hi, "lat", 1)
    kept = inner(te, th, tle, tlh, ta, tb, source_amp, tow_cell, cells, lat_n)
    grad, send = outer(
        te,
        th,
        tle,
        tlh,
        ta,
        tb,
        kept,
        lo,
        hi,
        source_amp,
        tow_cell,
        cells,
        owners,
        depth_n,
        lat_n,
    )
    got = lax.all_to_all(send, "lat", split_axis=0, concat_axis=0, tiled=True)
    every = lax.all_gather(grad, "src", axis=0, tiled=False)
    total, lines = finish(every[0] + every[1], every[2] + every[3], got, groups)
    total = total.reshape(16, 8, 128)
    lines = jnp.transpose(lines.reshape(groups, 1, 1, 9, 2, lat_n), (0, 1, 2, 5, 4, 3))
    return (total, lines)


def solution(mesh):
    placed = (
        P("depth", "lat", None),
        P("src", None, "depth", "lat", None),
        P("src", None, "depth", "lat", None),
        P("src", None, "depth", "lat", None),
        P("src", None, "depth", "lat", None),
        P("src", None),
        P("src"),
        P("depth", "lat", None),
        P("depth", "lat", None, None),
    )
    return jax.shard_map(
        per_device,
        mesh=mesh,
        in_specs=placed,
        out_specs=(P("depth", "lat", None), P("src", "depth", "lat", None, None, None)),
        check_vma=False,
    )
```

```python
import functools

import jax
import jax.numpy as jnp
from jax import lax
from jax.experimental import pallas as pl
from jax.experimental.pallas import tpu as pltpu
from jax.sharding import PartitionSpec as P

CC = 0.5
KK = 0.5
ROWS = 24
F32 = jnp.float32
UP = ((0, 3), (3, 2), (5, 2), (7, 1), (8, 2))
DN = ((0, 3), (3, 3), (6, 2), (8, 2), (10, 2))
UP_ROWS = 9
DN_ROWS = 11


def shifted(block, axis, distance):
    n = lax.axis_size(axis)
    route = [(i, i + distance) for i in range(n) if 0 <= i + distance < n]
    return lax.ppermute(block, axis, route)


def swapped(block, axis, first):
    n = lax.axis_size(axis)
    lower = range(first, n - 1, 2)
    return lax.ppermute(block, axis, [p for i in lower for p in ((i, i + 1), (i + 1, i))])


def lanes():
    return lax.broadcasted_iota(jnp.int32, (ROWS, 128), 1)


def zrow():
    r = lax.broadcasted_iota(jnp.int32, (ROWS, 128), 0)
    return jnp.where(r < 20, r, r - ROWS)


def yp(f):
    return jnp.where(lanes() == 127, 0.0, pltpu.roll(f, 127, 1))


def ym(f):
    return jnp.where(lanes() == 0, 0.0, pltpu.roll(f, 1, 1))


def zp(f):
    return pltpu.roll(f, ROWS - 1, 0)


def zm(f):
    return pltpu.roll(f, 1, 0)


def dpy(f):
    return yp(f) - f


def dpz(f):
    return zp(f) - f


def dmy(f):
    return f - ym(f)


def dmz(f):
    return f - zm(f)


def curl_p(f, nxt):
    fx, fy, fz = f
    return (dpy(fz) - dpz(fy), dpz(fx) - (nxt[2] - fz), (nxt[1] - fy) - dpy(fx))


def curl_m(f, prv):
    fx, fy, fz = f
    return (dmy(fz) - dmz(fy), dmz(fx) - (fz - prv[2]), (fy - prv[1]) - dmy(fx))


def coefs(conductivity, keep):
    inv = 1.0 / (1.0 + KK * conductivity)
    a = jnp.where(keep, (1.0 - KK * conductivity) * inv, 0.0)
    b = jnp.where(keep, CC * inv, 0.0)
    return a, b


def first_row_mask(depth_at):
    return jnp.where((zrow() < 0) & (depth_at == 0), 0.0, 1.0)


def last_row_keep(depth_at, depth_n):
    return jnp.logical_not((zrow() > 15) & (depth_at == depth_n - 1))


def pack_kernel(e, h, le, lh, cond, one, two, sems):
    even = lax.axis_index("depth") % 2 == 0

    def fill(up, dn):
        copies = []

        def move(src, dst):
            c = pltpu.make_async_copy(src, dst, sems.at[len(copies)])
            c.start()
            copies.append(c)

        for field, ref in enumerate((e, h, le, lh)):
            at, n = UP[field]
            move(ref.at[:, :, pl.ds(0, n * 8)], up.at[:, :, pl.ds(at * 8, n * 8)])
            at, n = DN[field]
            move(ref.at[:, :, pl.ds((16 - n) * 8, n * 8)], dn.at[:, :, pl.ds(at * 8, n * 8)])
        for row in range(2):
            move(cond.at[pl.ds(row * 8, 8)], up.at[0, row, pl.ds((UP_ROWS - 1) * 8, 8)])
            move(cond.at[pl.ds((14 + row) * 8, 8)], dn.at[0, row, pl.ds((DN_ROWS - 1) * 8, 8)])
        for c in copies:
            c.wait()

    @pl.when(even)
    def _():
        fill(two, one)

    @pl.when(jnp.logical_not(even))
    def _():
        fill(one, two)


def pack(e, h, le, lh, cond):
    message = jax.ShapeDtypeStruct((e.shape[0], 3, DN_ROWS * 8, 128), F32)
    return pl.pallas_call(
        pack_kernel,
        out_shape=(message, message),
        in_specs=[pl.BlockSpec(memory_space=pl.ANY)] * 5,
        out_specs=(pl.BlockSpec(memory_space=pltpu.VMEM),) * 2,
        scratch_shapes=[pltpu.SemaphoreType.DMA((12,))],
        compiler_params=pltpu.CompilerParams(vmem_limit_bytes=25165824),
        name="pack",
    )(e, h, le, lh, cond)


TO_LO = ((3, 17),) * 2 + ((2, 16),) * 2 + ((2, 15),) + ((1, 15),) * 2 + ((2, 16),) * 2 + ((1, 15),) * 2
TO_HI = (
    ((3, 17),) * 2
    + ((2, 17),)
    + ((2, 16),) * 2
    + ((2, 15),)
    + ((1, 15),) * 2
    + ((2, 16),) * 2
    + ((1, 16),)
    + ((1, 15),) * 2
)


def offset(table, k):
    return sum(lo + hi + 1 for lo, hi in table[:k])


def chunk(table):
    return -(-(offset(table, len(table)) + 12) // 8) * 8


def put_plane(ref, table, g, k, value):
    lo, hi = table[k]
    at = offset(table, k)
    ref[g, at : at + hi + 1] = value[0 : hi + 1]
    ref[g, at + hi + 1 : at + hi + 1 + lo] = value[ROWS - lo : ROWS]


def get_plane(ref, table, g, k):
    lo, hi = table[k]
    at = offset(table, k)
    end = at + lo + hi + 1
    rest = ref[g, end - 8 : end]
    if hi > 15:
        r = lax.broadcasted_iota(jnp.int32, (8, 128), 0)
        rest = jnp.where(r < 4, ref[g, at + 16 : at + 24], rest)
    return jnp.concatenate([ref[g, at : at + 16], rest], axis=0)


def put_conductivity(ref, table, value):
    at = offset(table, len(table))
    ref[0, at : at + 8] = value[0:8]
    ref[1, at : at + 8] = value[8:16]
    ref[1, at + 8 : at + 10] = value[16:18]
    ref[1, at + 10 : at + 12] = value[22:24]


def get_conductivity(ref, table):
    at = offset(table, len(table))
    r = lax.broadcasted_iota(jnp.int32, (8, 128), 0)
    rest = ref[1, at + 4 : at + 12]
    rest = jnp.where(r < 4, pltpu.roll(rest, 4, 0), rest)
    return jnp.concatenate([ref[0, at : at + 8], ref[1, at : at + 8], rest], axis=0)


def halo_tile(up, dn, lead, x, field):
    r = lax.broadcasted_iota(jnp.int32, (8, 128), 0)
    at, _ = UP[field]
    s = min(at, UP_ROWS - 8)
    hi = up[(*lead, pl.ds(s * 8 + x, 8, stride=8), slice(None))]
    if at != s:
        hi = pltpu.roll(hi, (8 - (at - s)) % 8, 0)
    at, n = DN[field]
    s = min(at, DN_ROWS - 8)
    lo = dn[(*lead, pl.ds(s * 8 + x, 8, stride=8), slice(None))]
    turn = (8 - n - (at - s)) % 8
    if turn:
        lo = pltpu.roll(lo, turn, 0)
    return jnp.where(r < 4, hi, lo)


def own_kernel(e, h, le, lh, cond, te, th, tle, tlh, tc, be, bh, ble, blh, bc, sems):
    pairs = ((e, be), (h, bh), (le, ble), (lh, blh), (cond, bc))
    copies = [pltpu.make_async_copy(src, dst, sems.at[k]) for k, (src, dst) in enumerate(pairs)]
    for c in copies:
        c.start()
    for k, (src, dst) in enumerate(((be, te), (bh, th), (ble, tle), (blh, tlh))):
        copies[k].wait()

        def body(g, carry, src=src, dst=dst):
            for c in range(3):
                for x in range(8):
                    dst[g, c, x, 0:8] = src[g, c, pl.ds(x, 8, stride=8), :]
                    dst[g, c, x, 8:16] = src[g, c, pl.ds(64 + x, 8, stride=8), :]
            return carry

        lax.fori_loop(0, e.shape[0], body, 0)
    copies[4].wait()
    for x in range(8):
        tc[x, 0:8] = bc[pl.ds(x, 8, stride=8), :]
        tc[x, 8:16] = bc[pl.ds(64 + x, 8, stride=8), :]


def own_planes(e, h, le, lh, cond):
    g = e.shape[0]
    vm = pl.BlockSpec(memory_space=pltpu.VMEM)
    field = jax.ShapeDtypeStruct((g, 3, 8, ROWS, 128), F32)
    return pl.pallas_call(
        own_kernel,
        out_shape=(field,) * 4 + (jax.ShapeDtypeStruct((8, 16, 128), F32),),
        in_specs=[pl.BlockSpec(memory_space=pl.ANY)] * 5,
        out_specs=(vm,) * 5,
        scratch_shapes=[pltpu.VMEM((g, 3, 128, 128), F32)] * 4
        + [pltpu.VMEM((128, 128), F32), pltpu.SemaphoreType.DMA((5,))],
        cost_estimate=pl.CostEstimate(flops=5_000_000, bytes_accessed=8_000_000, transcendentals=0),
        compiler_params=pltpu.CompilerParams(vmem_limit_bytes=24 * 1024 * 1024),
        name="own",
    )(e, h, le, lh, cond)


def planes_kernel(
    depth_n,
    lat_n,
    ie,
    ih,
    ile,
    ilh,
    tc,
    one,
    two,
    amp,
    tow,
    te,
    th,
    tle,
    tlh,
    ta,
    tb,
    to_lo,
    to_hi,
):
    groups = te.shape[0]
    depth_at = lax.axis_index("depth")
    lat_at = lax.axis_index("lat")

    even = depth_at % 2 == 0

    def halos(up, dn):
        def halo(g, carry):
            for c in range(3):
                for field, dst in enumerate((te, th, tle, tlh)):
                    for x in range(8):
                        dst[g, c, x, 16:24] = halo_tile(up, dn, (g, c), x, field)
            return carry

        lax.fori_loop(0, groups, halo, 0)

    @pl.when(even)
    def _():
        halos(one, two)

    @pl.when(jnp.logical_not(even))
    def _():
        halos(two, one)

    keep = last_row_keep(depth_at, depth_n)
    r8 = lax.broadcasted_iota(jnp.int32, (8, 128), 0)

    def edge(first, second, row, at):
        rows = pl.ds((at - 1) * 8, 8)
        return jnp.where(even, first[0, row, rows, :], second[0, row, rows, :])

    u0, u1 = (edge(one, two, row, UP_ROWS) for row in range(2))
    d0, d1 = (edge(two, one, row, DN_ROWS) for row in range(2))
    for x in range(8):
        rest = jnp.where(r8 == 0, u0[x : x + 1], 1.0)
        rest = jnp.where(r8 == 1, u1[x : x + 1], rest)
        rest = jnp.where(r8 == 6, d0[x : x + 1], rest)
        rest = jnp.where(r8 == 7, d1[x : x + 1], rest)
        whole = jnp.concatenate([tc[x], rest], axis=0)
        a, b = coefs(whole, keep)
        ta[x] = a
        tb[x] = b
        if x == 0:
            put_conductivity(to_lo, TO_LO, whole)
        if x == 7:
            put_conductivity(to_hi, TO_HI, whole)
    row_mask = first_row_mask(depth_at)
    z, lane = zrow(), lanes()

    def forward_planes(g, carry):
        s = -CC * row_mask
        cell = tow[g]
        lz = cell // (1024 * lat_n) - depth_at * 16
        lx = cell // 128 % (8 * lat_n) - lat_at * 8
        point = jnp.where((z == lz) & (lane == cell % 128), amp[g, 0], 0.0)

        def e0(x):
            return tuple(te[g, c, x] for c in range(3))

        def h0(x):
            return tuple(th[g, c, x] for c in range(3))

        def step_h(x):
            return tuple(f + s * k for f, k in zip(h0(x), curl_p(e0(x), e0(x + 1))))

        def put(ref, k, value):
            put_plane(ref, TO_LO if ref is to_lo else TO_HI, g, k, value)

        a0, b0, a1, b1 = ta[0], tb[0], ta[1], tb[1]
        f0, f1 = e0(0), e0(1)
        h1 = step_h(0)
        put(to_lo, 0, f0[1])
        put(to_lo, 1, f0[2])
        put(to_lo, 2, a0 * f0[1] + b0 * (dmz(h1[0]) - h1[2]))
        put(to_lo, 3, a0 * f0[2] + b0 * (h1[1] - dmy(h1[0])))
        put(to_lo, 4, h1[0])
        hit = jnp.where(lx == 0, point, 0.0)
        ex = a0 * f0[0] + b0 * (dmy(h1[2]) - dmz(h1[1]) - hit)
        k1 = step_h(1)
        ey1 = a1 * f1[1] + b1 * (dmz(k1[0]) - k1[2] + h1[2])
        ez1 = a1 * f1[2] + b1 * (k1[1] - h1[1] - dmy(k1[0]))
        put(to_lo, 5, h1[1] + s * (dpz(ex) - ez1))
        put(to_lo, 6, h1[2] + s * (ey1 - dpy(ex)))
        a7, b7, a6, b6 = ta[7], tb[7], ta[6], tb[6]
        f7, f6 = e0(7), e0(6)
        g7 = h0(7)
        put(to_hi, 0, g7[1] + s * (dpz(f7[0]) + f7[2]))
        put(to_hi, 1, g7[2] - s * (f7[1] + dpy(f7[0])))
        put(to_hi, 2, f7[0])
        hx7 = g7[0] + s * (dpy(f7[2]) - dpz(f7[1]))
        h6 = step_h(6)
        put(to_hi, 3, a7 * f7[1] + b7 * (dmz(hx7) + h6[2]))
        put(to_hi, 4, a7 * f7[2] - b7 * (h6[1] + dmy(hx7)))
        put(to_hi, 5, hx7)
        h5 = step_h(5)
        m6 = curl_m(h6, h5)
        hit = jnp.where(lx == 6, point, 0.0)
        ex6 = a6 * f6[0] + b6 * (m6[0] - hit)
        ey6 = a6 * f6[1] + b6 * m6[1]
        ez6 = a6 * f6[2] + b6 * m6[2]
        put(to_hi, 6, h6[1] + s * (dpz(ex6) + ez6))
        put(to_hi, 7, h6[2] - s * (ey6 + dpy(ex6)))
        s = row_mask

        def l0(x):
            return tuple(tle[g, c, x] for c in range(3))

        def w0(x):
            return tuple(tb[x] * f for f in l0(x))

        def m0(x):
            return tuple(tlh[g, c, x] for c in range(3))

        def step_m(x):
            return tuple(f + s * k for f, k in zip(m0(x), curl_p(w0(x), w0(x + 1))))

        q0, v0 = l0(0), w0(0)
        m1 = step_m(0)
        put(to_lo, 7, v0[1])
        put(to_lo, 8, v0[2])
        put(to_lo, 9, a0 * q0[1] - CC * (dmz(m1[0]) - m1[2]))
        put(to_lo, 10, a0 * q0[2] - CC * (m1[1] - dmy(m1[0])))
        q7, v7, n7 = l0(7), w0(7), m0(7)
        put(to_hi, 8, n7[1] + s * (dpz(v7[0]) + v7[2]))
        put(to_hi, 9, n7[2] - s * (v7[1] + dpy(v7[0])))
        put(to_hi, 10, q7[0])
        mx7 = n7[0] + s * (dpy(v7[2]) - dpz(v7[1]))
        m6 = step_m(6)
        put(to_hi, 11, a7 * q7[1] - CC * (dmz(mx7) + m6[2]))
        put(to_hi, 12, a7 * q7[2] + CC * (m6[1] + dmy(mx7)))
        return carry

    lax.fori_loop(0, groups, forward_planes, 0, unroll=True)


def planes(own, one, two, amp, tow, depth_n, lat_n):
    g = one.shape[0]
    vm = pl.BlockSpec(memory_space=pltpu.VMEM)
    sm = pl.BlockSpec(memory_space=pltpu.SMEM)
    field = jax.ShapeDtypeStruct((g, 3, 8, ROWS, 128), F32)
    coef = jax.ShapeDtypeStruct((8, ROWS, 128), F32)
    return pl.pallas_call(
        functools.partial(planes_kernel, depth_n, lat_n),
        out_shape=(
            field,
            field,
            field,
            field,
            coef,
            coef,
            jax.ShapeDtypeStruct((g, chunk(TO_LO), 128), F32),
            jax.ShapeDtypeStruct((g, chunk(TO_HI), 128), F32),
        ),
        in_specs=[vm] * 7 + [sm] * 2,
        out_specs=(vm,) * 8,
        input_output_aliases={0: 0, 1: 1, 2: 2, 3: 3},
        compiler_params=pltpu.CompilerParams(vmem_limit_bytes=24 * 1024 * 1024),
        name="planes",
    )(*own, one, two, amp, tow)


SLOTS = 24
STRIDE = 8 * ROWS


def e_at(g, n, c, x):
    return pl.ds(pl.multiple_of((g * 9 + n * 3 + c) * STRIDE + x * ROWS, 8), ROWS)


def triple(ref, g, x):
    return tuple(ref[g, c, x] for c in range(3))


def inside(n, x):
    return n + 1 <= x <= 6 - n


def weighted(old, drive, weight):
    total = None
    for c in range(3):
        t = (-2.0 * KK * old[c][0:16] - CC * KK * drive[c][0:16]) * weight[c][0:16]
        total = t if total is None else total + t
    return total


def take_samples(store, rcell, use, put):
    k = lax.broadcasted_iota(jnp.int32, (SLOTS, 128), 0)
    step = k // 3 % 3
    lane = lanes()

    def body(r, c0):
        cell = rcell[r]
        z, x, y = cell // 1024, cell // 128 % 8, cell % 128
        rows = store[pl.ds(x * ROWS + z, SLOTS, stride=STRIDE), :]
        near = (x >= step + 1) & (x <= 6 - step)
        put(r, jnp.where((lane == y) & use(near), rows, 0.0))
        return c0

    lax.fori_loop(0, rcell.shape[0], body, 0, unroll=True)


def tow_at(tow, g, depth_at, lat_at, lat_n):
    cell = tow[g]
    lz = cell // (1024 * lat_n) - depth_at * 16
    lx = cell // 128 % (8 * lat_n) - lat_at * 8
    point = jnp.where((zrow() == lz) & (lanes() == cell % 128), 1.0, 0.0)
    return lx, point


def inner_kernel(
    lat_n, te, th, tle, tlh, ta, tb, amp, tow, rcell, hh, mm, l1, l2, d0, ei, acc, samp
):
    groups = te.shape[0]
    depth_at = lax.axis_index("depth")
    lat_at = lax.axis_index("lat")
    row_mask = first_row_mask(depth_at)
    acc[...] = jnp.zeros_like(acc)

    def one_group(g, carry):
        lx, point = tow_at(tow, g, depth_at, lat_at, lat_n)
        lam = (tle, l1, l2)
        s = row_mask
        for n in range(2):
            w = {}

            def scaled(x, n=n, w=w):
                if x not in w:
                    w[x] = tuple(tb[x] * f for f in triple(lam[n], g, x))
                return w[x]

            for x in range(n, 7 - n):
                k = curl_p(scaled(x), scaled(x + 1))
                base = triple(tlh if n == 0 else mm, g, x)
                for c in range(3):
                    mm[g, c, x] = base[c] + s * k[c]
            for x in range(n + 1, 7 - n):
                k = curl_m(triple(mm, g, x), triple(mm, g, x - 1))
                old = triple(lam[n], g, x)
                for c in range(3):
                    lam[n + 1][g, c, x] = ta[x] * old[c] - CC * k[c]
        s = -CC * row_mask

        def e_of(n, x):
            if n == 0:
                return triple(te, g, x)
            return tuple(ei[e_at(g, n - 1, c, x), :] for c in range(3))

        for n in range(3):
            for x in range(n, 7 - n):
                k = curl_p(e_of(n, x), e_of(n, x + 1))
                base = triple(th if n == 0 else hh, g, x)
                for c in range(3):
                    hh[g, c, x] = base[c] + s * k[c]
            for x in range(n + 1, 7 - n):
                k = curl_m(triple(hh, g, x), triple(hh, g, x - 1))
                k = (k[0] - jnp.where(lx == x, amp[g, n], 0.0) * point, k[1], k[2])
                old = e_of(n, x)
                for c in range(3):
                    ei[e_at(g, n, c, x), :] = ta[x] * old[c] + tb[x] * k[c]
                if n == 0 and x in (1, 6):
                    for c in range(3):
                        d0[g, c, x // 6] = k[c][0:16]
                else:
                    acc[x] += weighted(old, k, triple(lam[2 - n], g, x))
        return carry

    lax.fori_loop(0, groups, one_group, 0, unroll=True)

    def put(r, values):
        samp[r] = values

    take_samples(ei, rcell, lambda near: near, put)


def inner(te, th, tle, tlh, ta, tb, amp, tow, rcell, lat_n):
    g, n = te.shape[0], rcell.shape[0]
    vm = pl.BlockSpec(memory_space=pltpu.VMEM)
    sm = pl.BlockSpec(memory_space=pltpu.SMEM)
    field = jax.ShapeDtypeStruct((g, 3, 8, ROWS, 128), F32)
    return pl.pallas_call(
        functools.partial(inner_kernel, lat_n),
        out_shape=(
            field,
            field,
            field,
            field,
            jax.ShapeDtypeStruct((g, 3, 2, 16, 128), F32),
            jax.ShapeDtypeStruct((SLOTS * STRIDE, 128), F32),
            jax.ShapeDtypeStruct((8, 16, 128), F32),
            jax.ShapeDtypeStruct((n, SLOTS, 128), F32),
        ),
        in_specs=[vm] * 6 + [sm] * 3,
        out_specs=(vm,) * 8,
        cost_estimate=pl.CostEstimate(flops=20_000_000, bytes_accessed=12_000_000, transcendentals=0),
        compiler_params=pltpu.CompilerParams(vmem_limit_bytes=24 * 1024 * 1024),
        name="inner",
    )(te, th, tle, tlh, ta, tb, amp, tow, rcell)


def outer_kernel(
    depth_n,
    lat_n,
    te,
    th,
    tle,
    tlh,
    ta,
    tb,
    hh,
    mm,
    l1,
    l2,
    d0,
    ei,
    acc,
    samp,
    lo,
    hi,
    amp,
    tow,
    rcell,
    rowner,
    grad,
    send,
    eo,
    ho,
    mo,
    o1,
    o2,
    total,
    count,
):
    groups = te.shape[0]
    depth_at = lax.axis_index("depth")
    lat_at = lax.axis_index("lat")
    row_mask = first_row_mask(depth_at)
    keep = last_row_keep(depth_at, depth_n)
    a8, b8 = coefs(get_conductivity(hi, TO_LO), keep & (lat_at < lat_n - 1))
    al, bl = coefs(get_conductivity(lo, TO_HI), keep)
    left = jnp.where(lat_at == 0, 0.0, 1.0)
    total[...] = acc[...]

    def lam(n, g, x):
        if n == 0:
            return triple(tle, g, x)
        near = inside(n - 1, x)
        return triple((l1 if near else o1) if n == 1 else (l2 if near else o2), g, x)

    def one_group(g, carry):
        def high(k):
            return get_plane(hi, TO_LO, g, k)

        def low(k):
            return get_plane(lo, TO_HI, g, k)

        lx, point = tow_at(tow, g, depth_at, lat_at, lat_n)
        s = row_mask
        p, q = 7, 8

        def m_of(n, x):
            return triple(mm if n <= x <= 6 - n else mo, g, x)

        def m_step(n, nxt):
            w = {8: nxt}

            def scaled(x):
                if x not in w:
                    w[x] = tuple(tb[x] * f for f in lam(n, g, x))
                return w[x]

            for x in range(8):
                if n <= x <= 6 - n:
                    continue
                k = curl_p(scaled(x), scaled(x + 1))
                base = triple(tlh, g, x) if n == 0 else m_of(n - 1, x)
                for c in range(3):
                    mo[g, c, x] = base[c] + s * k[c]

        def l_step(n, prv):
            out = (o1, o2)[n]
            for x in range(8):
                if inside(n, x):
                    continue
                k = curl_m(m_of(n, x), m_of(n, x - 1) if x else prv)
                old = lam(n, g, x)
                for c in range(3):
                    out[g, c, x] = ta[x] * old[c] - CC * k[c]

        m_step(0, (None, high(p), high(p + 1)))
        first = lam(0, g, 0)
        my = left * (low(q) - s * (tb[0] * first[2]))
        mz = left * (low(q + 1) + s * (tb[0] * first[1]))
        l_step(0, (None, my, mz))
        last = m_of(0, 7)
        m_step(1, (None, b8 * (high(p + 2) - CC * last[2]), b8 * (high(p + 3) + CC * last[1])))
        wx = bl * (al * low(q + 2) - CC * (dmy(mz) - dmz(my)))
        wy = bl * (low(q + 3) + CC * mz)
        wz = bl * (low(q + 4) - CC * my)
        first = lam(1, g, 0)
        my = left * (my + s * (dpz(wx) - (tb[0] * first[2] - wz)))
        mz = left * (mz + s * ((tb[0] * first[1] - wy) - dpy(wx)))
        l_step(1, (None, my, mz))
        s = -CC * row_mask
        p, q = 0, 0

        def e_of(n, x):
            if n == 0:
                return triple(te, g, x)
            ref = ei if inside(n - 1, x) else eo
            return tuple(ref[e_at(g, n - 1, c, x), :] for c in range(3))

        def h_of(n, x):
            return triple(hh if n <= x <= 6 - n else ho, g, x)

        def h_step(n, nxt):
            for x in range(8):
                if n <= x <= 6 - n:
                    continue
                k = curl_p(e_of(n, x), nxt if x == 7 else e_of(n, x + 1))
                base = triple(th, g, x) if n == 0 else h_of(n - 1, x)
                for c in range(3):
                    ho[g, c, x] = base[c] + s * k[c]

        def e_step(n, prv):
            for x in range(8):
                old = e_of(n, x)
                if inside(n, x):
                    if n == 0 and x in (1, 6):
                        k = tuple(d0[g, c, x // 6] for c in range(3))
                        total[x] += weighted(old, k, lam(2, g, x))
                    continue
                k = curl_m(h_of(n, x), h_of(n, x - 1) if x else prv)
                k = (k[0] - jnp.where(lx == x, amp[g, n], 0.0) * point, k[1], k[2])
                for c in range(3):
                    eo[e_at(g, n, c, x), :] = ta[x] * old[c] + tb[x] * k[c]
                total[x] += weighted(old, k, lam(2 - n, g, x))

        def drop(n):
            return jnp.where(lx == -1, amp[g, n], 0.0) * point

        h_step(0, (None, high(p), high(p + 1)))
        first = e_of(0, 0)
        hy = left * (low(q) - s * first[2])
        hz = left * (low(q + 1) + s * first[1])
        e_step(0, (None, hy, hz))
        last = h_of(0, 7)
        ey8 = high(p + 2) + b8 * last[2]
        ez8 = high(p + 3) - b8 * last[1]
        ex = al * low(q + 2) + bl * (dmy(hz) - dmz(hy) - drop(0))
        ey = low(q + 3) - bl * hz
        ez = low(q + 4) + bl * hy
        h_step(1, (None, ey8, ez8))
        first = e_of(1, 0)
        hy2 = left * (hy + s * (dpz(ex) - (first[2] - ez)))
        hz2 = left * (hz + s * ((first[1] - ey) - dpy(ex)))
        e_step(1, (None, hy2, hz2))
        last = h_of(1, 7)
        gx = high(p + 4) + s * (dpy(ez8) - dpz(ey8))
        gy = high(p + 5) + s * ez8
        gz = high(p + 6) - s * ey8
        ey9 = a8 * ey8 + b8 * (dmz(gx) - gz + last[2])
        ez9 = a8 * ez8 + b8 * (gy - last[1] - dmy(gx))
        hx2 = low(q + 5) + s * (dpy(ez) - dpz(ey))
        hyf = low(q + 6) - s * ez
        hzf = low(q + 7) + s * ey
        ex2 = al * ex + bl * (dmy(hz2) - dmz(hy2) - drop(1))
        ey2 = al * ey + bl * (dmz(hx2) - hz2 + hzf)
        ez2 = al * ez + bl * (hy2 - hyf - dmy(hx2))
        h_step(2, (None, ey9, ez9))
        first = e_of(2, 0)
        hy3 = left * (hy2 + s * (dpz(ex2) - (first[2] - ez2)))
        hz3 = left * (hz2 + s * ((first[1] - ey2) - dpy(ex2)))
        e_step(2, (None, hy3, hz3))
        return carry

    lax.fori_loop(0, groups, one_group, 0, unroll=True)
    for x in range(8):
        for half in range(2):
            rows = pl.ds(half * 64 + x, 8, stride=8)
            inv = tb[x, half * 8 : half * 8 + 8] * (1.0 / CC)
            grad[rows, :] = total[x, half * 8 : half * 8 + 8] * inv * inv
    send[...] = jnp.zeros_like(send)
    for o in range(send.shape[0]):
        count[o] = 0
    r24, lane = lax.broadcasted_iota(jnp.int32, (SLOTS, 128), 0), lanes()
    used = (r24 == lane) & (r24 < groups * 9)

    def put(r, values):
        o = rowner[r]
        slot = count[o]
        count[o] = slot + 1
        values = jnp.sum(samp[r] + values, axis=-1, keepdims=True)
        send[o, pl.ds(slot, 1), :] = jnp.sum(jnp.where(used, values, 0.0), axis=0, keepdims=True)

    take_samples(eo, rcell, jnp.logical_not, put)


def outer(te, th, tle, tlh, ta, tb, kept, lo, hi, amp, tow, rcell, rowner, depth_n, lat_n):
    g = te.shape[0]
    vm = pl.BlockSpec(memory_space=pltpu.VMEM)
    sm = pl.BlockSpec(memory_space=pltpu.SMEM)
    return pl.pallas_call(
        functools.partial(outer_kernel, depth_n, lat_n),
        out_shape=(
            jax.ShapeDtypeStruct((128, 128), F32),
            jax.ShapeDtypeStruct((lat_n, 2, 128), F32),
        ),
        in_specs=[vm] * 16 + [sm] * 4,
        out_specs=(vm,) * 2,
        scratch_shapes=[pltpu.VMEM((SLOTS * STRIDE, 128), F32)]
        + [pltpu.VMEM((g, 3, 8, ROWS, 128), F32)] * 4
        + [pltpu.VMEM((8, 16, 128), F32), pltpu.SMEM((lat_n,), jnp.int32)],
        cost_estimate=pl.CostEstimate(flops=10_000_000, bytes_accessed=12_000_000, transcendentals=0),
        compiler_params=pltpu.CompilerParams(vmem_limit_bytes=24 * 1024 * 1024),
        name="outer",
    )(te, th, tle, tlh, ta, tb, *kept, lo, hi, amp, tow, rcell, rowner)


def finish_kernel(mine, theirs, got, total, lines):
    total[...] = mine[...] + theirs[...]
    for slot in range(2):
        table = jnp.transpose(got[:, slot, :])
        for g in range(lines.shape[0]):
            lines[g, :, slot, :] = table[g * 9 : g * 9 + 9]


def finish(mine, theirs, got, groups):
    vm = pl.BlockSpec(memory_space=pltpu.VMEM)
    return pl.pallas_call(
        finish_kernel,
        out_shape=(
            jax.ShapeDtypeStruct(mine.shape, F32),
            jax.ShapeDtypeStruct((groups, 9, 2, got.shape[0]), F32),
        ),
        in_specs=[vm] * 3,
        out_specs=(vm,) * 2,
        compiler_params=pltpu.CompilerParams(vmem_limit_bytes=24 * 1024 * 1024),
        name="finish",
    )(mine, theirs, got)


def across(value, step):
    n = lax.axis_size("src")
    return lax.ppermute(value, "src", [(i, i ^ step) for i in range(n) if i ^ step < n])


def per_device(
    conductivity, e_start, h_start, e_weight, h_weight, source_amp, tow_cell, rec_cell, rec_owner
):
    groups = e_start.shape[0]
    depth_n, lat_n = lax.axis_size("depth"), lax.axis_size("lat")

    def flat(f):
        return f.reshape(groups, 3, 128, 128)

    e, h, le, lh = flat(e_start), flat(h_start), flat(e_weight), flat(h_weight)
    cond = conductivity.reshape(128, 128)
    fields = [
        pltpu.with_memory_space_constraint(f, pltpu.HBM) for f in (e, h, le, lh, cond)
    ]
    one, two = pack(*fields)
    one = swapped(one, "depth", 0)
    two = swapped(two, "depth", 1)
    own = own_planes(*fields)
    te, th, tle, tlh, ta, tb, to_lo, to_hi = planes(
        own, one, two, source_amp, tow_cell, depth_n, lat_n
    )
    cells, owners = rec_cell.reshape(-1), rec_owner.reshape(-1)
    hi = shifted(to_lo, "lat", -1)
    lo = shifted(to_hi, "lat", 1)
    kept = inner(te, th, tle, tlh, ta, tb, source_amp, tow_cell, cells, lat_n)
    grad, send = outer(
        te,
        th,
        tle,
        tlh,
        ta,
        tb,
        kept,
        lo,
        hi,
        source_amp,
        tow_cell,
        cells,
        owners,
        depth_n,
        lat_n,
    )
    got = lax.all_to_all(send, "lat", split_axis=0, concat_axis=0, tiled=True)
    every = lax.all_gather(grad, "src", axis=0, tiled=False)
    total, lines = finish(every[0] + every[1], every[2] + every[3], got, groups)
    total = total.reshape(16, 8, 128)
    lines = jnp.transpose(lines.reshape(groups, 1, 1, 9, 2, lat_n), (0, 1, 2, 5, 4, 3))
    return (total, lines)


def solution(mesh):
    placed = (
        P("depth", "lat", None),
        P("src", None, "depth", "lat", None),
        P("src", None, "depth", "lat", None),
        P("src", None, "depth", "lat", None),
        P("src", None, "depth", "lat", None),
        P("src", None),
        P("src"),
        P("depth", "lat", None),
        P("depth", "lat", None, None),
    )
    return jax.shard_map(
        per_device,
        mesh=mesh,
        in_specs=placed,
        out_specs=(P("depth", "lat", None), P("src", "depth", "lat", None, None, None)),
        check_vma=False,
    )
```

```python
import functools

import jax
import jax.numpy as jnp
from jax import lax
from jax.experimental import pallas as pl
from jax.experimental.pallas import tpu as pltpu
from jax.sharding import PartitionSpec as P

CC = 0.5
KK = 0.5
ROWS = 24
F32 = jnp.float32
UP = ((0, 3), (3, 2), (5, 2), (7, 1), (8, 2))
DN = ((0, 3), (3, 3), (6, 2), (8, 2), (10, 2))
UP_ROWS = 9
DN_ROWS = 11


def shifted(block, axis, distance):
    n = lax.axis_size(axis)
    route = [(i, i + distance) for i in range(n) if 0 <= i + distance < n]
    return lax.ppermute(block, axis, route)


def swapped(block, axis, first):
    n = lax.axis_size(axis)
    lower = range(first, n - 1, 2)
    return lax.ppermute(block, axis, [p for i in lower for p in ((i, i + 1), (i + 1, i))])


def lanes():
    return lax.broadcasted_iota(jnp.int32, (ROWS, 128), 1)


def zrow():
    r = lax.broadcasted_iota(jnp.int32, (ROWS, 128), 0)
    return jnp.where(r < 20, r, r - ROWS)


def yp(f):
    return jnp.where(lanes() == 127, 0.0, pltpu.roll(f, 127, 1))


def ym(f):
    return jnp.where(lanes() == 0, 0.0, pltpu.roll(f, 1, 1))


def zp(f):
    return pltpu.roll(f, ROWS - 1, 0)


def zm(f):
    return pltpu.roll(f, 1, 0)


def dpy(f):
    return yp(f) - f


def dpz(f):
    return zp(f) - f


def dmy(f):
    return f - ym(f)


def dmz(f):
    return f - zm(f)


def curl_p(f, nxt):
    fx, fy, fz = f
    return (dpy(fz) - dpz(fy), dpz(fx) - (nxt[2] - fz), (nxt[1] - fy) - dpy(fx))


def curl_m(f, prv):
    fx, fy, fz = f
    return (dmy(fz) - dmz(fy), dmz(fx) - (fz - prv[2]), (fy - prv[1]) - dmy(fx))


def coefs(conductivity, keep):
    inv = 1.0 / (1.0 + KK * conductivity)
    a = jnp.where(keep, (1.0 - KK * conductivity) * inv, 0.0)
    b = jnp.where(keep, CC * inv, 0.0)
    return a, b


def first_row_mask(depth_at):
    return jnp.where((zrow() < 0) & (depth_at == 0), 0.0, 1.0)


def last_row_keep(depth_at, depth_n):
    return jnp.logical_not((zrow() > 15) & (depth_at == depth_n - 1))


def pack_kernel(e, h, le, lh, cond, one, two, sems):
    even = lax.axis_index("depth") % 2 == 0

    def fill(up, dn):
        copies = []

        def move(src, dst):
            c = pltpu.make_async_copy(src, dst, sems.at[len(copies)])
            c.start()
            copies.append(c)

        for field, ref in enumerate((e, h, le, lh)):
            at, n = UP[field]
            move(ref.at[:, :, pl.ds(0, n * 8)], up.at[:, :, pl.ds(at * 8, n * 8)])
            at, n = DN[field]
            move(ref.at[:, :, pl.ds((16 - n) * 8, n * 8)], dn.at[:, :, pl.ds(at * 8, n * 8)])
        for row in range(2):
            move(cond.at[pl.ds(row * 8, 8)], up.at[0, row, pl.ds((UP_ROWS - 1) * 8, 8)])
            move(cond.at[pl.ds((14 + row) * 8, 8)], dn.at[0, row, pl.ds((DN_ROWS - 1) * 8, 8)])
        for c in copies:
            c.wait()

    @pl.when(even)
    def _():
        fill(two, one)

    @pl.when(jnp.logical_not(even))
    def _():
        fill(one, two)


def pack(e, h, le, lh, cond):
    message = jax.ShapeDtypeStruct((e.shape[0], 3, DN_ROWS * 8, 128), F32)
    return pl.pallas_call(
        pack_kernel,
        out_shape=(message, message),
        in_specs=[pl.BlockSpec(memory_space=pl.ANY)] * 5,
        out_specs=(pl.BlockSpec(memory_space=pltpu.VMEM),) * 2,
        scratch_shapes=[pltpu.SemaphoreType.DMA((12,))],
        compiler_params=pltpu.CompilerParams(vmem_limit_bytes=25165824),
        name="pack",
    )(e, h, le, lh, cond)


TO_LO = ((3, 17),) * 2 + (((2, 16),) * 2 + ((1, 15),) * 2) * 2
TO_HI = ((2, 17),) * 2 + (((1, 16),) * 2 + ((0, 15),) * 2) * 2


def offset(table, k):
    return sum(lo + hi + 1 for lo, hi in table[:k])


def chunk(table):
    return -(-(offset(table, len(table)) + 12) // 8) * 8


def put_plane(ref, table, g, k, value):
    lo, hi = table[k]
    at = offset(table, k)
    ref[g, at : at + hi + 1] = value[0 : hi + 1]
    if lo:
        ref[g, at + hi + 1 : at + hi + 1 + lo] = value[ROWS - lo : ROWS]


def get_plane(ref, table, g, k):
    lo, hi = table[k]
    at = offset(table, k)
    end = at + lo + hi + 1
    rest = ref[g, end - 8 : end]
    if hi > 15:
        r = lax.broadcasted_iota(jnp.int32, (8, 128), 0)
        rest = jnp.where(r < 4, ref[g, at + 16 : at + 24], rest)
    return jnp.concatenate([ref[g, at : at + 16], rest], axis=0)


def put_conductivity(ref, table, value):
    at = offset(table, len(table))
    ref[0, at : at + 8] = value[0:8]
    ref[1, at : at + 8] = value[8:16]
    ref[1, at + 8 : at + 10] = value[16:18]
    ref[1, at + 10 : at + 12] = value[22:24]


def get_conductivity(ref, table):
    at = offset(table, len(table))
    r = lax.broadcasted_iota(jnp.int32, (8, 128), 0)
    rest = ref[1, at + 4 : at + 12]
    rest = jnp.where(r < 4, pltpu.roll(rest, 4, 0), rest)
    return jnp.concatenate([ref[0, at : at + 8], ref[1, at : at + 8], rest], axis=0)


def halo_tile(up, dn, lead, x, field):
    r = lax.broadcasted_iota(jnp.int32, (8, 128), 0)
    at, _ = UP[field]
    s = min(at, UP_ROWS - 8)
    hi = up[(*lead, pl.ds(s * 8 + x, 8, stride=8), slice(None))]
    if at != s:
        hi = pltpu.roll(hi, (8 - (at - s)) % 8, 0)
    at, n = DN[field]
    s = min(at, DN_ROWS - 8)
    lo = dn[(*lead, pl.ds(s * 8 + x, 8, stride=8), slice(None))]
    turn = (8 - n - (at - s)) % 8
    if turn:
        lo = pltpu.roll(lo, turn, 0)
    return jnp.where(r < 4, hi, lo)


def own_kernel(e, h, le, lh, cond, te, th, tle, tlh, tc, be, bh, ble, blh, bc, sems):
    pairs = ((e, be), (h, bh), (le, ble), (lh, blh), (cond, bc))
    copies = [pltpu.make_async_copy(src, dst, sems.at[k]) for k, (src, dst) in enumerate(pairs)]
    for c in copies:
        c.start()
    for k, (src, dst) in enumerate(((be, te), (bh, th), (ble, tle), (blh, tlh))):
        copies[k].wait()

        def body(g, carry, src=src, dst=dst):
            for c in range(3):
                for x in range(8):
                    dst[g, c, x, 0:8] = src[g, c, pl.ds(x, 8, stride=8), :]
                    dst[g, c, x, 8:16] = src[g, c, pl.ds(64 + x, 8, stride=8), :]
            return carry

        lax.fori_loop(0, e.shape[0], body, 0)
    copies[4].wait()
    for x in range(8):
        tc[x, 0:8] = bc[pl.ds(x, 8, stride=8), :]
        tc[x, 8:16] = bc[pl.ds(64 + x, 8, stride=8), :]


def own_planes(e, h, le, lh, cond):
    g = e.shape[0]
    vm = pl.BlockSpec(memory_space=pltpu.VMEM)
    field = jax.ShapeDtypeStruct((g, 3, 8, ROWS, 128), F32)
    return pl.pallas_call(
        own_kernel,
        out_shape=(field,) * 4 + (jax.ShapeDtypeStruct((8, 16, 128), F32),),
        in_specs=[pl.BlockSpec(memory_space=pl.ANY)] * 5,
        out_specs=(vm,) * 5,
        scratch_shapes=[pltpu.VMEM((g, 3, 128, 128), F32)] * 4
        + [pltpu.VMEM((128, 128), F32), pltpu.SemaphoreType.DMA((5,))],
        cost_estimate=pl.CostEstimate(flops=5_000_000, bytes_accessed=8_000_000, transcendentals=0),
        compiler_params=pltpu.CompilerParams(vmem_limit_bytes=24 * 1024 * 1024),
        name="own",
    )(e, h, le, lh, cond)


def planes_kernel(
    depth_n,
    lat_n,
    ie,
    ih,
    ile,
    ilh,
    tc,
    one,
    two,
    amp,
    tow,
    te,
    th,
    tle,
    tlh,
    ta,
    tb,
    to_lo,
    to_hi,
):
    groups = te.shape[0]
    depth_at = lax.axis_index("depth")
    lat_at = lax.axis_index("lat")

    even = depth_at % 2 == 0

    def halos(up, dn):
        def halo(g, carry):
            for c in range(3):
                for field, dst in enumerate((te, th, tle, tlh)):
                    for x in range(8):
                        dst[g, c, x, 16:24] = halo_tile(up, dn, (g, c), x, field)
            return carry

        lax.fori_loop(0, groups, halo, 0)

    @pl.when(even)
    def _():
        halos(one, two)

    @pl.when(jnp.logical_not(even))
    def _():
        halos(two, one)

    keep = last_row_keep(depth_at, depth_n)
    r8 = lax.broadcasted_iota(jnp.int32, (8, 128), 0)

    def edge(first, second, row, at):
        rows = pl.ds((at - 1) * 8, 8)
        return jnp.where(even, first[0, row, rows, :], second[0, row, rows, :])

    u0, u1 = (edge(one, two, row, UP_ROWS) for row in range(2))
    d0, d1 = (edge(two, one, row, DN_ROWS) for row in range(2))
    for x in range(8):
        rest = jnp.where(r8 == 0, u0[x : x + 1], 1.0)
        rest = jnp.where(r8 == 1, u1[x : x + 1], rest)
        rest = jnp.where(r8 == 6, d0[x : x + 1], rest)
        rest = jnp.where(r8 == 7, d1[x : x + 1], rest)
        whole = jnp.concatenate([tc[x], rest], axis=0)
        a, b = coefs(whole, keep)
        ta[x] = a
        tb[x] = b
        if x == 0:
            put_conductivity(to_lo, TO_LO, whole)
        if x == 7:
            put_conductivity(to_hi, TO_HI, whole)
    row_mask = first_row_mask(depth_at)
    z, lane = zrow(), lanes()

    def forward_planes(g, carry):
        s = -CC * row_mask
        cell = tow[g]
        lz = cell // (1024 * lat_n) - depth_at * 16
        lx = cell // 128 % (8 * lat_n) - lat_at * 8
        point = jnp.where((z == lz) & (lane == cell % 128), 1.0, 0.0)

        def e0(x):
            return tuple(te[g, c, x] for c in range(3))

        def h0(x):
            return tuple(th[g, c, x] for c in range(3))

        def step_h(x):
            return tuple(f + s * k for f, k in zip(h0(x), curl_p(e0(x), e0(x + 1))))

        def put(ref, k, value):
            put_plane(ref, TO_LO if ref is to_lo else TO_HI, g, k, value)

        def hit(x, n):
            return jnp.where(lx == x, amp[g, n], 0.0) * point

        zero = (None, 0.0, 0.0)
        a0, b0, a1, b1 = ta[0], tb[0], ta[1], tb[1]
        f0, f1 = e0(0), e0(1)
        h1, k1 = step_h(0), step_h(1)
        put(to_lo, 0, f0[1])
        put(to_lo, 1, f0[2])
        m = curl_m(h1, zero)
        e1 = (a0 * f0[0] + b0 * (m[0] - hit(0, 0)), a0 * f0[1] + b0 * m[1], a0 * f0[2] + b0 * m[2])
        put(to_lo, 2, e1[1])
        put(to_lo, 3, e1[2])
        m = curl_m(k1, h1)
        k = curl_p(e1, (None, a1 * f1[1] + b1 * m[1], a1 * f1[2] + b1 * m[2]))
        h2 = tuple(h1[c] + s * k[c] for c in range(3))
        m = curl_m(h2, zero)
        put(to_lo, 4, a0 * e1[1] + b0 * m[1])
        put(to_lo, 5, a0 * e1[2] + b0 * m[2])
        a7, b7, a6, b6 = ta[7], tb[7], ta[6], tb[6]
        f7, f6 = e0(7), e0(6)
        k = curl_p(f7, zero)
        h7 = tuple(f + s * t for f, t in zip(h0(7), k))
        put(to_hi, 0, h7[1])
        put(to_hi, 1, h7[2])
        h6, h5 = step_h(6), step_h(5)
        m7, m6 = curl_m(h7, h6), curl_m(h6, h5)
        e7 = (a7 * f7[0] + b7 * (m7[0] - hit(7, 0)), a7 * f7[1] + b7 * m7[1], a7 * f7[2] + b7 * m7[2])
        e6 = (a6 * f6[0] + b6 * (m6[0] - hit(6, 0)), a6 * f6[1] + b6 * m6[1], a6 * f6[2] + b6 * m6[2])
        k7, k6 = curl_p(e7, zero), curl_p(e6, e7)
        h7 = tuple(h7[c] + s * k7[c] for c in range(3))
        h6 = tuple(h6[c] + s * k6[c] for c in range(3))
        put(to_hi, 2, h7[1])
        put(to_hi, 3, h7[2])
        m7 = curl_m(h7, h6)
        e7 = (a7 * e7[0] + b7 * (m7[0] - hit(7, 1)), a7 * e7[1] + b7 * m7[1], a7 * e7[2] + b7 * m7[2])
        k7 = curl_p(e7, zero)
        put(to_hi, 4, h7[1] + s * k7[1])
        put(to_hi, 5, h7[2] + s * k7[2])
        s = row_mask

        def l0(x):
            return tuple(tle[g, c, x] for c in range(3))

        def w0(x):
            return tuple(tb[x] * f for f in l0(x))

        def m0(x):
            return tuple(tlh[g, c, x] for c in range(3))

        def step_m(x):
            return tuple(f + s * k for f, k in zip(m0(x), curl_p(w0(x), w0(x + 1))))

        q0, v0 = l0(0), w0(0)
        put(to_lo, 6, v0[1])
        put(to_lo, 7, v0[2])
        m = curl_m(step_m(0), zero)
        put(to_lo, 8, a0 * q0[1] - CC * m[1])
        put(to_lo, 9, a0 * q0[2] - CC * m[2])
        q7 = l0(7)
        k7 = curl_p(w0(7), zero)
        n7 = tuple(f + s * t for f, t in zip(m0(7), k7))
        put(to_hi, 6, n7[1])
        put(to_hi, 7, n7[2])
        m = curl_m(n7, step_m(6))
        k7 = curl_p(tuple(b7 * (a7 * q7[c] - CC * m[c]) for c in range(3)), zero)
        put(to_hi, 8, n7[1] + s * k7[1])
        put(to_hi, 9, n7[2] + s * k7[2])
        return carry

    lax.fori_loop(0, groups, forward_planes, 0, unroll=True)


def planes(own, one, two, amp, tow, depth_n, lat_n):
    g = one.shape[0]
    vm = pl.BlockSpec(memory_space=pltpu.VMEM)
    sm = pl.BlockSpec(memory_space=pltpu.SMEM)
    field = jax.ShapeDtypeStruct((g, 3, 8, ROWS, 128), F32)
    coef = jax.ShapeDtypeStruct((8, ROWS, 128), F32)
    return pl.pallas_call(
        functools.partial(planes_kernel, depth_n, lat_n),
        out_shape=(
            field,
            field,
            field,
            field,
            coef,
            coef,
            jax.ShapeDtypeStruct((g, chunk(TO_LO), 128), F32),
            jax.ShapeDtypeStruct((g, chunk(TO_HI), 128), F32),
        ),
        in_specs=[vm] * 7 + [sm] * 2,
        out_specs=(vm,) * 8,
        input_output_aliases={0: 0, 1: 1, 2: 2, 3: 3},
        compiler_params=pltpu.CompilerParams(vmem_limit_bytes=24 * 1024 * 1024),
        name="planes",
    )(*own, one, two, amp, tow)


SLOTS = 24
STRIDE = 8 * ROWS


def e_at(g, n, c, x):
    return pl.ds(pl.multiple_of((g * 9 + n * 3 + c) * STRIDE + x * ROWS, 8), ROWS)


def triple(ref, g, x):
    return tuple(ref[g, c, x] for c in range(3))


def inside(n, x):
    return n + 1 <= x <= 6 - n


def weighted(old, drive, weight):
    total = None
    for c in range(3):
        t = (-2.0 * KK * old[c][0:16] - CC * KK * drive[c][0:16]) * weight[c][0:16]
        total = t if total is None else total + t
    return total


def take_samples(store, rcell, use, put):
    k = lax.broadcasted_iota(jnp.int32, (SLOTS, 128), 0)
    step = k // 3 % 3
    lane = lanes()

    def body(r, c0):
        cell = rcell[r]
        z, x, y = cell // 1024, cell // 128 % 8, cell % 128
        rows = store[pl.ds(x * ROWS + z, SLOTS, stride=STRIDE), :]
        near = (x >= step + 1) & (x <= 6 - step)
        put(r, jnp.where((lane == y) & use(near), rows, 0.0))
        return c0

    lax.fori_loop(0, rcell.shape[0], body, 0, unroll=True)


def tow_at(tow, g, depth_at, lat_at, lat_n):
    cell = tow[g]
    lz = cell // (1024 * lat_n) - depth_at * 16
    lx = cell // 128 % (8 * lat_n) - lat_at * 8
    point = jnp.where((zrow() == lz) & (lanes() == cell % 128), 1.0, 0.0)
    return lx, point


def inner_kernel(
    lat_n, te, th, tle, tlh, ta, tb, amp, tow, rcell, hh, mm, l1, l2, d0, ei, acc, samp
):
    groups = te.shape[0]
    depth_at = lax.axis_index("depth")
    lat_at = lax.axis_index("lat")
    row_mask = first_row_mask(depth_at)
    acc[...] = jnp.zeros_like(acc)

    def one_group(g, carry):
        lx, point = tow_at(tow, g, depth_at, lat_at, lat_n)
        lam = (tle, l1, l2)
        s = row_mask
        for n in range(2):
            w = {}

            def scaled(x, n=n, w=w):
                if x not in w:
                    w[x] = tuple(tb[x] * f for f in triple(lam[n], g, x))
                return w[x]

            for x in range(n, 7 - n):
                k = curl_p(scaled(x), scaled(x + 1))
                base = triple(tlh if n == 0 else mm, g, x)
                for c in range(3):
                    mm[g, c, x] = base[c] + s * k[c]
            for x in range(n + 1, 7 - n):
                k = curl_m(triple(mm, g, x), triple(mm, g, x - 1))
                old = triple(lam[n], g, x)
                for c in range(3):
                    lam[n + 1][g, c, x] = ta[x] * old[c] - CC * k[c]
        s = -CC * row_mask

        def e_of(n, x):
            if n == 0:
                return triple(te, g, x)
            return tuple(ei[e_at(g, n - 1, c, x), :] for c in range(3))

        for n in range(3):
            for x in range(n, 7 - n):
                k = curl_p(e_of(n, x), e_of(n, x + 1))
                base = triple(th if n == 0 else hh, g, x)
                for c in range(3):
                    hh[g, c, x] = base[c] + s * k[c]
            for x in range(n + 1, 7 - n):
                k = curl_m(triple(hh, g, x), triple(hh, g, x - 1))
                k = (k[0] - jnp.where(lx == x, amp[g, n], 0.0) * point, k[1], k[2])
                old = e_of(n, x)
                for c in range(3):
                    ei[e_at(g, n, c, x), :] = ta[x] * old[c] + tb[x] * k[c]
                if n == 0 and x in (1, 6):
                    for c in range(3):
                        d0[g, c, x // 6] = k[c][0:16]
                else:
                    acc[x] += weighted(old, k, triple(lam[2 - n], g, x))
        return carry

    lax.fori_loop(0, groups, one_group, 0, unroll=True)

    def put(r, values):
        samp[r] = values

    take_samples(ei, rcell, lambda near: near, put)


def inner(te, th, tle, tlh, ta, tb, amp, tow, rcell, lat_n):
    g, n = te.shape[0], rcell.shape[0]
    vm = pl.BlockSpec(memory_space=pltpu.VMEM)
    sm = pl.BlockSpec(memory_space=pltpu.SMEM)
    field = jax.ShapeDtypeStruct((g, 3, 8, ROWS, 128), F32)
    return pl.pallas_call(
        functools.partial(inner_kernel, lat_n),
        out_shape=(
            field,
            field,
            field,
            field,
            jax.ShapeDtypeStruct((g, 3, 2, 16, 128), F32),
            jax.ShapeDtypeStruct((SLOTS * STRIDE, 128), F32),
            jax.ShapeDtypeStruct((8, 16, 128), F32),
            jax.ShapeDtypeStruct((n, SLOTS, 128), F32),
        ),
        in_specs=[vm] * 6 + [sm] * 3,
        out_specs=(vm,) * 8,
        cost_estimate=pl.CostEstimate(flops=20_000_000, bytes_accessed=12_000_000, transcendentals=0),
        compiler_params=pltpu.CompilerParams(vmem_limit_bytes=24 * 1024 * 1024),
        name="inner",
    )(te, th, tle, tlh, ta, tb, amp, tow, rcell)


def outer_kernel(
    depth_n,
    lat_n,
    te,
    th,
    tle,
    tlh,
    ta,
    tb,
    hh,
    mm,
    l1,
    l2,
    d0,
    ei,
    acc,
    samp,
    lo,
    hi,
    amp,
    tow,
    rcell,
    rowner,
    grad,
    send,
    eo,
    ho,
    mo,
    o1,
    o2,
    total,
    count,
):
    groups = te.shape[0]
    depth_at = lax.axis_index("depth")
    lat_at = lax.axis_index("lat")
    row_mask = first_row_mask(depth_at)
    keep = last_row_keep(depth_at, depth_n)
    a8, b8 = coefs(get_conductivity(hi, TO_LO), keep & (lat_at < lat_n - 1))
    al, bl = coefs(get_conductivity(lo, TO_HI), keep)
    left = jnp.where(lat_at == 0, 0.0, 1.0)
    total[...] = acc[...]

    def lam(n, g, x):
        if n == 0:
            return triple(tle, g, x)
        near = inside(n - 1, x)
        return triple((l1 if near else o1) if n == 1 else (l2 if near else o2), g, x)

    def one_group(g, carry):
        def high(k):
            return get_plane(hi, TO_LO, g, k)

        def low(k):
            return get_plane(lo, TO_HI, g, k)

        lx, point = tow_at(tow, g, depth_at, lat_at, lat_n)
        s = row_mask

        def m_of(n, x):
            return triple(mm if n <= x <= 6 - n else mo, g, x)

        def m_step(n, nxt):
            w = {8: nxt}

            def scaled(x):
                if x not in w:
                    w[x] = tuple(tb[x] * f for f in lam(n, g, x))
                return w[x]

            for x in range(8):
                if n <= x <= 6 - n:
                    continue
                k = curl_p(scaled(x), scaled(x + 1))
                base = triple(tlh, g, x) if n == 0 else m_of(n - 1, x)
                for c in range(3):
                    mo[g, c, x] = base[c] + s * k[c]

        def l_step(n, prv):
            out = (o1, o2)[n]
            for x in range(8):
                if inside(n, x):
                    continue
                k = curl_m(m_of(n, x), m_of(n, x - 1) if x else prv)
                old = lam(n, g, x)
                for c in range(3):
                    out[g, c, x] = ta[x] * old[c] - CC * k[c]

        m_step(0, (None, high(6), high(7)))
        first = lam(0, g, 0)
        dy, dz = -s * (tb[0] * first[2]), s * (tb[0] * first[1])
        l_step(0, (None, left * (low(6) + dy), left * (low(7) + dz)))
        last = m_of(0, 7)
        m_step(1, (None, b8 * (high(8) - CC * last[2]), b8 * (high(9) + CC * last[1])))
        wx, wy, wz = -CC * bl * (dmy(dz) - dmz(dy)), CC * bl * dz, -CC * bl * dy
        first = lam(1, g, 0)
        dy = dy + s * (dpz(wx) - (tb[0] * first[2] - wz))
        dz = dz + s * ((tb[0] * first[1] - wy) - dpy(wx))
        l_step(1, (None, left * (low(8) + dy), left * (low(9) + dz)))
        s = -CC * row_mask

        def e_of(n, x):
            if n == 0:
                return triple(te, g, x)
            ref = ei if inside(n - 1, x) else eo
            return tuple(ref[e_at(g, n - 1, c, x), :] for c in range(3))

        def h_of(n, x):
            return triple(hh if n <= x <= 6 - n else ho, g, x)

        def h_step(n, nxt):
            for x in range(8):
                if n <= x <= 6 - n:
                    continue
                k = curl_p(e_of(n, x), nxt if x == 7 else e_of(n, x + 1))
                base = triple(th, g, x) if n == 0 else h_of(n - 1, x)
                for c in range(3):
                    ho[g, c, x] = base[c] + s * k[c]

        def e_step(n, prv):
            for x in range(8):
                old = e_of(n, x)
                if inside(n, x):
                    if n == 0 and x in (1, 6):
                        k = tuple(d0[g, c, x // 6] for c in range(3))
                        total[x] += weighted(old, k, lam(2, g, x))
                    continue
                k = curl_m(h_of(n, x), h_of(n, x - 1) if x else prv)
                k = (k[0] - jnp.where(lx == x, amp[g, n], 0.0) * point, k[1], k[2])
                for c in range(3):
                    eo[e_at(g, n, c, x), :] = ta[x] * old[c] + tb[x] * k[c]
                total[x] += weighted(old, k, lam(2 - n, g, x))

        h_step(0, (None, high(0), high(1)))
        first = e_of(0, 0)
        dy, dz = -s * first[2], s * first[1]
        e_step(0, (None, left * (low(0) + dy), left * (low(1) + dz)))
        last = h_of(0, 7)
        uy, uz = b8 * last[2], -b8 * last[1]
        h_step(1, (None, high(2) + uy, high(3) + uz))
        ex, ey, ez = bl * (dmy(dz) - dmz(dy)), -bl * dz, bl * dy
        first = e_of(1, 0)
        dy = dy + s * (dpz(ex) - (first[2] - ez))
        dz = dz + s * ((first[1] - ey) - dpy(ex))
        e_step(1, (None, left * (low(2) + dy), left * (low(3) + dz)))
        last = h_of(1, 7)
        gx, gy, gz = s * (dpy(uz) - dpz(uy)), s * uz, -s * uy
        h_step(
            2,
            (
                None,
                high(4) + a8 * uy + b8 * (dmz(gx) - gz + last[2]),
                high(5) + a8 * uz + b8 * (gy - last[1] - dmy(gx)),
            ),
        )
        hx, hy, hz = s * (dpy(ez) - dpz(ey)), -s * ez, s * ey
        ex, ey, ez = (
            al * ex + bl * (dmy(dz) - dmz(dy)),
            al * ey + bl * (dmz(hx) - dz + hz),
            al * ez + bl * (dy - hy - dmy(hx)),
        )
        first = e_of(2, 0)
        dy = dy + s * (dpz(ex) - (first[2] - ez))
        dz = dz + s * ((first[1] - ey) - dpy(ex))
        e_step(2, (None, left * (low(4) + dy), left * (low(5) + dz)))
        return carry

    lax.fori_loop(0, groups, one_group, 0, unroll=True)
    for x in range(8):
        for half in range(2):
            rows = pl.ds(half * 64 + x, 8, stride=8)
            inv = tb[x, half * 8 : half * 8 + 8] * (1.0 / CC)
            grad[rows, :] = total[x, half * 8 : half * 8 + 8] * inv * inv
    send[...] = jnp.zeros_like(send)
    for o in range(send.shape[0]):
        count[o] = 0
    r24, lane = lax.broadcasted_iota(jnp.int32, (SLOTS, 128), 0), lanes()
    used = (r24 == lane) & (r24 < groups * 9)

    def put(r, values):
        o = rowner[r]
        slot = count[o]
        count[o] = slot + 1
        values = jnp.sum(samp[r] + values, axis=-1, keepdims=True)
        send[o, pl.ds(slot, 1), :] = jnp.sum(jnp.where(used, values, 0.0), axis=0, keepdims=True)

    take_samples(eo, rcell, jnp.logical_not, put)


def outer(te, th, tle, tlh, ta, tb, kept, lo, hi, amp, tow, rcell, rowner, depth_n, lat_n):
    g = te.shape[0]
    vm = pl.BlockSpec(memory_space=pltpu.VMEM)
    sm = pl.BlockSpec(memory_space=pltpu.SMEM)
    return pl.pallas_call(
        functools.partial(outer_kernel, depth_n, lat_n),
        out_shape=(
            jax.ShapeDtypeStruct((128, 128), F32),
            jax.ShapeDtypeStruct((lat_n, 2, 128), F32),
        ),
        in_specs=[vm] * 16 + [sm] * 4,
        out_specs=(vm,) * 2,
        scratch_shapes=[pltpu.VMEM((SLOTS * STRIDE, 128), F32)]
        + [pltpu.VMEM((g, 3, 8, ROWS, 128), F32)] * 4
        + [pltpu.VMEM((8, 16, 128), F32), pltpu.SMEM((lat_n,), jnp.int32)],
        cost_estimate=pl.CostEstimate(flops=10_000_000, bytes_accessed=12_000_000, transcendentals=0),
        compiler_params=pltpu.CompilerParams(vmem_limit_bytes=24 * 1024 * 1024),
        name="outer",
    )(te, th, tle, tlh, ta, tb, *kept, lo, hi, amp, tow, rcell, rowner)


def finish_kernel(mine, theirs, got, total, lines):
    total[...] = mine[...] + theirs[...]
    for slot in range(2):
        table = jnp.transpose(got[:, slot, :])
        for g in range(lines.shape[0]):
            lines[g, :, slot, :] = table[g * 9 : g * 9 + 9]


def finish(mine, theirs, got, groups):
    vm = pl.BlockSpec(memory_space=pltpu.VMEM)
    return pl.pallas_call(
        finish_kernel,
        out_shape=(
            jax.ShapeDtypeStruct(mine.shape, F32),
            jax.ShapeDtypeStruct((groups, 9, 2, got.shape[0]), F32),
        ),
        in_specs=[vm] * 3,
        out_specs=(vm,) * 2,
        compiler_params=pltpu.CompilerParams(vmem_limit_bytes=24 * 1024 * 1024),
        name="finish",
    )(mine, theirs, got)


def across(value, step):
    n = lax.axis_size("src")
    return lax.ppermute(value, "src", [(i, i ^ step) for i in range(n) if i ^ step < n])


def per_device(
    conductivity, e_start, h_start, e_weight, h_weight, source_amp, tow_cell, rec_cell, rec_owner
):
    groups = e_start.shape[0]
    depth_n, lat_n = lax.axis_size("depth"), lax.axis_size("lat")

    def flat(f):
        return f.reshape(groups, 3, 128, 128)

    e, h, le, lh = flat(e_start), flat(h_start), flat(e_weight), flat(h_weight)
    cond = conductivity.reshape(128, 128)
    fields = [
        pltpu.with_memory_space_constraint(f, pltpu.HBM) for f in (e, h, le, lh, cond)
    ]
    one, two = pack(*fields)
    one = swapped(one, "depth", 0)
    two = swapped(two, "depth", 1)
    own = own_planes(*fields)
    te, th, tle, tlh, ta, tb, to_lo, to_hi = planes(
        own, one, two, source_amp, tow_cell, depth_n, lat_n
    )
    cells, owners = rec_cell.reshape(-1), rec_owner.reshape(-1)
    hi = shifted(to_lo, "lat", -1)
    lo = shifted(to_hi, "lat", 1)
    kept = inner(te, th, tle, tlh, ta, tb, source_amp, tow_cell, cells, lat_n)
    grad, send = outer(
        te,
        th,
        tle,
        tlh,
        ta,
        tb,
        kept,
        lo,
        hi,
        source_amp,
        tow_cell,
        cells,
        owners,
        depth_n,
        lat_n,
    )
    got = lax.all_to_all(send, "lat", split_axis=0, concat_axis=0, tiled=True)
    every = lax.all_gather(grad, "src", axis=0, tiled=False)
    total, lines = finish(every[0] + every[1], every[2] + every[3], got, groups)
    total = total.reshape(16, 8, 128)
    lines = jnp.transpose(lines.reshape(groups, 1, 1, 9, 2, lat_n), (0, 1, 2, 5, 4, 3))
    return (total, lines)


def solution(mesh):
    placed = (
        P("depth", "lat", None),
        P("src", None, "depth", "lat", None),
        P("src", None, "depth", "lat", None),
        P("src", None, "depth", "lat", None),
        P("src", None, "depth", "lat", None),
        P("src", None),
        P("src"),
        P("depth", "lat", None),
        P("depth", "lat", None, None),
    )
    return jax.shard_map(
        per_device,
        mesh=mesh,
        in_specs=placed,
        out_specs=(P("depth", "lat", None), P("src", "depth", "lat", None, None, None)),
        check_vma=False,
    )
```

```python
import functools

import jax
import jax.numpy as jnp
from jax import lax
from jax.experimental import pallas as pl
from jax.experimental.pallas import tpu as pltpu
from jax.sharding import PartitionSpec as P

CC = 0.5
KK = 0.5
ROWS = 24
F32 = jnp.float32
UP = (0, 2, 4, 5)
DN = (1, 4, 5, 7)
SPAN = 8


def shifted(block, axis, distance):
    n = lax.axis_size(axis)
    route = [(i, i + distance) for i in range(n) if 0 <= i + distance < n]
    return lax.ppermute(block, axis, route)


def swapped(block, axis, first):
    n = lax.axis_size(axis)
    lower = range(first, n - 1, 2)
    return lax.ppermute(block, axis, [p for i in lower for p in ((i, i + 1), (i + 1, i))])


def lanes(rows=ROWS):
    return lax.broadcasted_iota(jnp.int32, (rows, 128), 1)


def zrow():
    r = lax.broadcasted_iota(jnp.int32, (ROWS, 128), 0)
    return jnp.where(r < 20, r, r - ROWS)


def yp(f):
    return jnp.where(lanes(f.shape[0]) == 127, 0.0, pltpu.roll(f, 127, 1))


def ym(f):
    return jnp.where(lanes() == 0, 0.0, pltpu.roll(f, 1, 1))


def zp(f):
    return pltpu.roll(f, ROWS - 1, 0)


def zm(f):
    return pltpu.roll(f, 1, 0)


def dpy(f):
    return yp(f) - f


def dpz(f):
    return zp(f) - f


def dmy(f):
    return f - ym(f)


def dmz(f):
    return f - zm(f)


def curl_p(f, nxt):
    fx, fy, fz = f
    return (dpy(fz) - dpz(fy), dpz(fx) - (nxt[2] - fz), (nxt[1] - fy) - dpy(fx))


def curl_m(f, prv):
    fx, fy, fz = f
    return (dmy(fz) - dmz(fy), dmz(fx) - (fz - prv[2]), (fy - prv[1]) - dmy(fx))


def coefs(conductivity, keep):
    inv = 1.0 / (1.0 + KK * conductivity)
    a = jnp.where(keep, (1.0 - KK * conductivity) * inv, 0.0)
    b = jnp.where(keep, CC * inv, 0.0)
    return a, b


def first_row_mask(depth_at):
    return jnp.where((zrow() < 0) & (depth_at == 0), 0.0, 1.0)


def unstepped(*rows):
    z = zrow()
    done = z == rows[0]
    for row in rows[1:]:
        done = done | (z == row)
    return jnp.where(done, 0.0, 1.0)


def last_row_keep(depth_at, depth_n):
    return jnp.logical_not((zrow() > 15) & (depth_at == depth_n - 1))


def stepped(fields, row, base, s, xp):
    fx, fy, fz = (fields(c, row) for c in range(3))
    gx, gy = fields(0, row + 1), fields(1, row + 1)
    return (
        base(0, row) + s * (dpy(fz) - (gy - fy)),
        base(1, row) + s * ((gx - fx) - (xp(fz) - fz)),
        base(2, row) + s * ((xp(fy) - fy) - dpy(fx)),
    )


def pack_kernel(e, h, le, lh, cond, one, two, ve, vh, vl, vm, vc, sems):
    even = lax.axis_index("depth") % 2 == 0
    copies = []
    for ref, dst in ((e, ve), (h, vh), (le, vl), (lh, vm)):
        n = dst.shape[2] // 16
        for k, first in enumerate((0, 16 - n)):
            copies.append(
                pltpu.make_async_copy(
                    ref.at[:, :, pl.ds(first * 8, n * 8)],
                    dst.at[:, :, pl.ds(k * n * 8, n * 8)],
                    sems.at[len(copies)],
                )
            )
    for k, first in enumerate((0, 14)):
        copies.append(
            pltpu.make_async_copy(
                cond.at[pl.ds(first * 8, 16)], vc.at[pl.ds(k * 16, 16)], sems.at[len(copies)]
            )
        )
    for c in copies:
        c.start()
    for c in copies:
        c.wait()
    sub = lax.broadcasted_iota(jnp.int32, (8, 128), 0)

    def xp(f):
        return jnp.where(sub == 7, 0.0, pltpu.roll(f, 7, 0))

    def tile(ref, g, c, z):
        n = ref.shape[2] // 16
        k = z if z < n else z - 16 + 2 * n
        return ref[g, c, k * 8 : k * 8 + 8]

    def layer(z):
        k = z if z < 2 else z - 12
        return vc[k * 8 : k * 8 + 8]

    def fill(up, dn):
        for g in range(e.shape[0]):

            def e_of(c, z, g=g):
                return tile(ve, g, c, z)

            def h_of(c, z, g=g):
                return tile(vh, g, c, z)

            def w_of(c, z, g=g):
                return CC / (1.0 + KK * layer(z)) * tile(vl, g, c, z)

            def m_of(c, z, g=g):
                return tile(vm, g, c, z)

            h17 = stepped(e_of, 1, h_of, -CC, xp)
            h3 = stepped(e_of, 13, h_of, -CC, xp)
            m16 = stepped(w_of, 0, m_of, 1.0, xp)
            m2 = stepped(w_of, 14, m_of, 1.0, xp)
            extra = jnp.where(sub == 0, e_of(2, 13), 0.0)
            extra = jnp.where(sub == 1, pltpu.roll(tile(vl, g, 2, 14), 1, 0), extra)
            for c in range(3):
                blank = jnp.zeros((8, 128), F32)
                ups = (e_of(c, 0), e_of(c, 1), h_of(c, 0), h17[c], tile(vl, g, c, 0), m16[c])
                ups += (layer(0), layer(1)) if g == 0 and c == 0 else (blank, blank)
                dns = (
                    e_of(c, 14),
                    e_of(c, 15),
                    h3[c] if c < 2 else extra,
                    h_of(c, 14),
                    h_of(c, 15),
                    tile(vl, g, c, 15),
                    m2[c] if c < 2 else layer(14 + g % 2),
                    m_of(c, 15),
                )
                for k in range(SPAN):
                    up[g, c, k * 8 : k * 8 + 8] = ups[k]
                    dn[g, c, k * 8 : k * 8 + 8] = dns[k]

    @pl.when(even)
    def _():
        fill(two, one)

    @pl.when(jnp.logical_not(even))
    def _():
        fill(one, two)


def pack(e, h, le, lh, cond):
    g = e.shape[0]
    message = jax.ShapeDtypeStruct((g, 3, SPAN * 8, 128), F32)
    return pl.pallas_call(
        pack_kernel,
        out_shape=(message, message),
        in_specs=[pl.BlockSpec(memory_space=pl.ANY)] * 5,
        out_specs=(pl.BlockSpec(memory_space=pltpu.VMEM),) * 2,
        scratch_shapes=[pltpu.VMEM((g, 3, 2 * n * 8, 128), F32) for n in (3, 3, 2, 2)]
        + [pltpu.VMEM((32, 128), F32), pltpu.SemaphoreType.DMA((10,))],
        compiler_params=pltpu.CompilerParams(vmem_limit_bytes=24 * 1024 * 1024),
        name="pack",
    )(e, h, le, lh, cond)


TO_LO = ((3, 17),) * 2 + (((2, 16),) * 2 + ((1, 15),) * 2) * 2
TO_HI = ((2, 17),) * 2 + (((1, 16),) * 2 + ((0, 15),) * 2) * 2


def offset(table, k):
    return sum(lo + hi + 1 for lo, hi in table[:k])


def chunk(table):
    return -(-(offset(table, len(table)) + 12) // 8) * 8


def put_plane(ref, table, g, k, value):
    lo, hi = table[k]
    at = offset(table, k)
    ref[g, at : at + hi + 1] = value[0 : hi + 1]
    if lo:
        ref[g, at + hi + 1 : at + hi + 1 + lo] = value[ROWS - lo : ROWS]


def get_plane(ref, table, g, k):
    lo, hi = table[k]
    at = offset(table, k)
    end = at + lo + hi + 1
    rest = ref[g, end - 8 : end]
    if hi > 15:
        r = lax.broadcasted_iota(jnp.int32, (8, 128), 0)
        rest = jnp.where(r < 4, ref[g, at + 16 : at + 24], rest)
    return jnp.concatenate([ref[g, at : at + 16], rest], axis=0)


def put_conductivity(ref, table, value):
    at = offset(table, len(table))
    ref[0, at : at + 8] = value[0:8]
    ref[1, at : at + 8] = value[8:16]
    ref[1, at + 8 : at + 10] = value[16:18]
    ref[1, at + 10 : at + 12] = value[22:24]


def get_conductivity(ref, table):
    at = offset(table, len(table))
    r = lax.broadcasted_iota(jnp.int32, (8, 128), 0)
    rest = ref[1, at + 4 : at + 12]
    rest = jnp.where(r < 4, pltpu.roll(rest, 4, 0), rest)
    return jnp.concatenate([ref[0, at : at + 8], ref[1, at : at + 8], rest], axis=0)


def own_kernel(e, h, le, lh, cond, te, th, tle, tlh, tc, be, bh, ble, blh, bc, sems):
    pairs = ((e, be), (h, bh), (le, ble), (lh, blh), (cond, bc))
    copies = [pltpu.make_async_copy(src, dst, sems.at[k]) for k, (src, dst) in enumerate(pairs)]
    for c in copies:
        c.start()
    for k, (src, dst) in enumerate(((be, te), (bh, th), (ble, tle), (blh, tlh))):
        copies[k].wait()

        def body(g, carry, src=src, dst=dst):
            for c in range(3):
                for x in range(8):
                    dst[g, c, x, 0:8] = src[g, c, pl.ds(x, 8, stride=8), :]
                    dst[g, c, x, 8:16] = src[g, c, pl.ds(64 + x, 8, stride=8), :]
            return carry

        lax.fori_loop(0, e.shape[0], body, 0)
    copies[4].wait()
    for x in range(8):
        tc[x, 0:8] = bc[pl.ds(x, 8, stride=8), :]
        tc[x, 8:16] = bc[pl.ds(64 + x, 8, stride=8), :]


def own_planes(e, h, le, lh, cond):
    g = e.shape[0]
    vm = pl.BlockSpec(memory_space=pltpu.VMEM)
    field = jax.ShapeDtypeStruct((g, 3, 8, ROWS, 128), F32)
    return pl.pallas_call(
        own_kernel,
        out_shape=(field,) * 4 + (jax.ShapeDtypeStruct((8, 16, 128), F32),),
        in_specs=[pl.BlockSpec(memory_space=pl.ANY)] * 5,
        out_specs=(vm,) * 5,
        scratch_shapes=[pltpu.VMEM((g, 3, 128, 128), F32)] * 4
        + [pltpu.VMEM((128, 128), F32), pltpu.SemaphoreType.DMA((5,))],
        cost_estimate=pl.CostEstimate(flops=5_000_000, bytes_accessed=8_000_000, transcendentals=0),
        compiler_params=pltpu.CompilerParams(vmem_limit_bytes=24 * 1024 * 1024),
        name="own",
    )(e, h, le, lh, cond)


def planes_kernel(
    depth_n,
    lat_n,
    ie,
    ih,
    ile,
    ilh,
    tc,
    one,
    two,
    amp,
    tow,
    te,
    th,
    tle,
    tlh,
    ta,
    tb,
    to_lo,
    to_hi,
):
    groups = te.shape[0]
    depth_at = lax.axis_index("depth")
    lat_at = lax.axis_index("lat")

    even = depth_at % 2 == 0

    r8 = lax.broadcasted_iota(jnp.int32, (8, 128), 0)

    def halos(up, dn):
        def halo(g, carry):
            for c in range(3):
                for x in range(8):
                    hi = up[g, c, pl.ds(x, 8, stride=8), :]
                    lo = dn[g, c, pl.ds(x, 8, stride=8), :]
                    for field, dst in enumerate((te, th, tle, tlh)):
                        a = pltpu.roll(hi, 8 - UP[field], 0) if UP[field] else hi
                        b = pltpu.roll(lo, 7 - DN[field], 0) if DN[field] != 7 else lo
                        dst[g, c, x, 16:24] = jnp.where(r8 < 4, a, b)
            te[g, 2, 0, 21:22] = dn[g, 2, 16:17]
            tle[g, 2, 0, 22:23] = dn[g, 2, 17:18]
            return carry

        lax.fori_loop(0, groups, halo, 0)

    @pl.when(even)
    def _():
        halos(one, two)

    @pl.when(jnp.logical_not(even))
    def _():
        halos(two, one)

    keep = last_row_keep(depth_at, depth_n)

    def edge(first, second, g, c, slot):
        rows = pl.ds(slot * 8, 8)
        return jnp.where(even, first[g, c, rows, :], second[g, c, rows, :])

    u0, u1 = (edge(one, two, 0, 0, 6 + k) for k in range(2))
    d0, d1 = (edge(two, one, k, 2, 6) for k in range(2))
    for x in range(8):
        rest = jnp.where(r8 == 0, u0[x : x + 1], 1.0)
        rest = jnp.where(r8 == 1, u1[x : x + 1], rest)
        rest = jnp.where(r8 == 6, d0[x : x + 1], rest)
        rest = jnp.where(r8 == 7, d1[x : x + 1], rest)
        whole = jnp.concatenate([tc[x], rest], axis=0)
        a, b = coefs(whole, keep)
        ta[x] = a
        tb[x] = b
        if x == 0:
            put_conductivity(to_lo, TO_LO, whole)
        if x == 7:
            put_conductivity(to_hi, TO_HI, whole)
    row_mask = first_row_mask(depth_at)
    z, lane = zrow(), lanes()

    first_e, first_l = unstepped(17, -3), unstepped(16, -2)

    def forward_planes(g, carry):
        s = -CC * row_mask
        s_first = s * first_e
        cell = tow[g]
        lz = cell // (1024 * lat_n) - depth_at * 16
        lx = cell // 128 % (8 * lat_n) - lat_at * 8
        point = jnp.where((z == lz) & (lane == cell % 128), 1.0, 0.0)

        def e0(x):
            return tuple(te[g, c, x] for c in range(3))

        def h0(x):
            return tuple(th[g, c, x] for c in range(3))

        def step_h(x):
            return tuple(f + s_first * k for f, k in zip(h0(x), curl_p(e0(x), e0(x + 1))))

        def put(ref, k, value):
            put_plane(ref, TO_LO if ref is to_lo else TO_HI, g, k, value)

        def hit(x, n):
            return jnp.where(lx == x, amp[g, n], 0.0) * point

        zero = (None, 0.0, 0.0)
        a0, b0, a1, b1 = ta[0], tb[0], ta[1], tb[1]
        f0, f1 = e0(0), e0(1)
        h1, k1 = step_h(0), step_h(1)
        put(to_lo, 0, f0[1])
        put(to_lo, 1, f0[2])
        m = curl_m(h1, zero)
        e1 = (a0 * f0[0] + b0 * (m[0] - hit(0, 0)), a0 * f0[1] + b0 * m[1], a0 * f0[2] + b0 * m[2])
        put(to_lo, 2, e1[1])
        put(to_lo, 3, e1[2])
        m = curl_m(k1, h1)
        k = curl_p(e1, (None, a1 * f1[1] + b1 * m[1], a1 * f1[2] + b1 * m[2]))
        h2 = tuple(h1[c] + s * k[c] for c in range(3))
        m = curl_m(h2, zero)
        put(to_lo, 4, a0 * e1[1] + b0 * m[1])
        put(to_lo, 5, a0 * e1[2] + b0 * m[2])
        a7, b7, a6, b6 = ta[7], tb[7], ta[6], tb[6]
        f7, f6 = e0(7), e0(6)
        k = curl_p(f7, zero)
        h7 = tuple(f + s_first * t for f, t in zip(h0(7), k))
        put(to_hi, 0, h7[1])
        put(to_hi, 1, h7[2])
        h6, h5 = step_h(6), step_h(5)
        m7, m6 = curl_m(h7, h6), curl_m(h6, h5)
        e7 = (a7 * f7[0] + b7 * (m7[0] - hit(7, 0)), a7 * f7[1] + b7 * m7[1], a7 * f7[2] + b7 * m7[2])
        e6 = (a6 * f6[0] + b6 * (m6[0] - hit(6, 0)), a6 * f6[1] + b6 * m6[1], a6 * f6[2] + b6 * m6[2])
        k7, k6 = curl_p(e7, zero), curl_p(e6, e7)
        h7 = tuple(h7[c] + s * k7[c] for c in range(3))
        h6 = tuple(h6[c] + s * k6[c] for c in range(3))
        put(to_hi, 2, h7[1])
        put(to_hi, 3, h7[2])
        m7 = curl_m(h7, h6)
        e7 = (a7 * e7[0] + b7 * (m7[0] - hit(7, 1)), a7 * e7[1] + b7 * m7[1], a7 * e7[2] + b7 * m7[2])
        k7 = curl_p(e7, zero)
        put(to_hi, 4, h7[1] + s * k7[1])
        put(to_hi, 5, h7[2] + s * k7[2])
        s = row_mask
        m_first = s * first_l

        def l0(x):
            return tuple(tle[g, c, x] for c in range(3))

        def w0(x):
            return tuple(tb[x] * f for f in l0(x))

        def m0(x):
            return tuple(tlh[g, c, x] for c in range(3))

        def step_m(x):
            return tuple(f + m_first * k for f, k in zip(m0(x), curl_p(w0(x), w0(x + 1))))

        q0, v0 = l0(0), w0(0)
        put(to_lo, 6, v0[1])
        put(to_lo, 7, v0[2])
        m = curl_m(step_m(0), zero)
        put(to_lo, 8, a0 * q0[1] - CC * m[1])
        put(to_lo, 9, a0 * q0[2] - CC * m[2])
        q7 = l0(7)
        k7 = curl_p(w0(7), zero)
        n7 = tuple(f + m_first * t for f, t in zip(m0(7), k7))
        put(to_hi, 6, n7[1])
        put(to_hi, 7, n7[2])
        m = curl_m(n7, step_m(6))
        k7 = curl_p(tuple(b7 * (a7 * q7[c] - CC * m[c]) for c in range(3)), zero)
        put(to_hi, 8, n7[1] + s * k7[1])
        put(to_hi, 9, n7[2] + s * k7[2])
        return carry

    lax.fori_loop(0, groups, forward_planes, 0, unroll=True)


def planes(own, one, two, amp, tow, depth_n, lat_n):
    g = one.shape[0]
    vm = pl.BlockSpec(memory_space=pltpu.VMEM)
    sm = pl.BlockSpec(memory_space=pltpu.SMEM)
    field = jax.ShapeDtypeStruct((g, 3, 8, ROWS, 128), F32)
    coef = jax.ShapeDtypeStruct((8, ROWS, 128), F32)
    return pl.pallas_call(
        functools.partial(planes_kernel, depth_n, lat_n),
        out_shape=(
            field,
            field,
            field,
            field,
            coef,
            coef,
            jax.ShapeDtypeStruct((g, chunk(TO_LO), 128), F32),
            jax.ShapeDtypeStruct((g, chunk(TO_HI), 128), F32),
        ),
        in_specs=[vm] * 7 + [sm] * 2,
        out_specs=(vm,) * 8,
        input_output_aliases={0: 0, 1: 1, 2: 2, 3: 3},
        compiler_params=pltpu.CompilerParams(vmem_limit_bytes=24 * 1024 * 1024),
        name="planes",
    )(*own, one, two, amp, tow)


SLOTS = 24
STRIDE = 8 * ROWS


def e_at(g, n, c, x):
    return pl.ds(pl.multiple_of((g * 9 + n * 3 + c) * STRIDE + x * ROWS, 8), ROWS)


def triple(ref, g, x):
    return tuple(ref[g, c, x] for c in range(3))


def inside(n, x):
    return n + 1 <= x <= 6 - n


def weighted(old, drive, weight):
    total = None
    for c in range(3):
        t = (-2.0 * KK * old[c][0:16] - CC * KK * drive[c][0:16]) * weight[c][0:16]
        total = t if total is None else total + t
    return total


def take_samples(store, rcell, use, put):
    k = lax.broadcasted_iota(jnp.int32, (SLOTS, 128), 0)
    step = k // 3 % 3
    lane = lanes()

    def body(r, c0):
        cell = rcell[r]
        z, x, y = cell // 1024, cell // 128 % 8, cell % 128
        rows = store[pl.ds(x * ROWS + z, SLOTS, stride=STRIDE), :]
        near = (x >= step + 1) & (x <= 6 - step)
        put(r, jnp.where((lane == y) & use(near), rows, 0.0))
        return c0

    lax.fori_loop(0, rcell.shape[0], body, 0, unroll=True)


def tow_at(tow, g, depth_at, lat_at, lat_n):
    cell = tow[g]
    lz = cell // (1024 * lat_n) - depth_at * 16
    lx = cell // 128 % (8 * lat_n) - lat_at * 8
    point = jnp.where((zrow() == lz) & (lanes() == cell % 128), 1.0, 0.0)
    return lx, point


def inner_kernel(
    lat_n, te, th, tle, tlh, ta, tb, amp, tow, rcell, hh, mm, l1, l2, d0, ei, acc, samp
):
    groups = te.shape[0]
    depth_at = lax.axis_index("depth")
    lat_at = lax.axis_index("lat")
    row_mask = first_row_mask(depth_at)
    acc[...] = jnp.zeros_like(acc)

    def one_group(g, carry):
        lx, point = tow_at(tow, g, depth_at, lat_at, lat_n)
        lam = (tle, l1, l2)
        for n in range(2):
            s = row_mask * unstepped(16, -2) if n == 0 else row_mask
            w = {}

            def scaled(x, n=n, w=w):
                if x not in w:
                    w[x] = tuple(tb[x] * f for f in triple(lam[n], g, x))
                return w[x]

            for x in range(n, 7 - n):
                k = curl_p(scaled(x), scaled(x + 1))
                base = triple(tlh if n == 0 else mm, g, x)
                for c in range(3):
                    mm[g, c, x] = base[c] + s * k[c]
            for x in range(n + 1, 7 - n):
                k = curl_m(triple(mm, g, x), triple(mm, g, x - 1))
                old = triple(lam[n], g, x)
                for c in range(3):
                    lam[n + 1][g, c, x] = ta[x] * old[c] - CC * k[c]
        def e_of(n, x):
            if n == 0:
                return triple(te, g, x)
            return tuple(ei[e_at(g, n - 1, c, x), :] for c in range(3))

        for n in range(3):
            s = -CC * (row_mask * unstepped(17, -3) if n == 0 else row_mask)
            for x in range(n, 7 - n):
                k = curl_p(e_of(n, x), e_of(n, x + 1))
                base = triple(th if n == 0 else hh, g, x)
                for c in range(3):
                    hh[g, c, x] = base[c] + s * k[c]
            for x in range(n + 1, 7 - n):
                k = curl_m(triple(hh, g, x), triple(hh, g, x - 1))
                k = (k[0] - jnp.where(lx == x, amp[g, n], 0.0) * point, k[1], k[2])
                old = e_of(n, x)
                for c in range(3):
                    ei[e_at(g, n, c, x), :] = ta[x] * old[c] + tb[x] * k[c]
                if n == 0 and x in (1, 6):
                    for c in range(3):
                        d0[g, c, x // 6] = k[c][0:16]
                else:
                    acc[x] += weighted(old, k, triple(lam[2 - n], g, x))
        return carry

    lax.fori_loop(0, groups, one_group, 0, unroll=True)

    def put(r, values):
        samp[r] = values

    take_samples(ei, rcell, lambda near: near, put)


def inner(te, th, tle, tlh, ta, tb, amp, tow, rcell, lat_n):
    g, n = te.shape[0], rcell.shape[0]
    vm = pl.BlockSpec(memory_space=pltpu.VMEM)
    sm = pl.BlockSpec(memory_space=pltpu.SMEM)
    field = jax.ShapeDtypeStruct((g, 3, 8, ROWS, 128), F32)
    return pl.pallas_call(
        functools.partial(inner_kernel, lat_n),
        out_shape=(
            field,
            field,
            field,
            field,
            jax.ShapeDtypeStruct((g, 3, 2, 16, 128), F32),
            jax.ShapeDtypeStruct((SLOTS * STRIDE, 128), F32),
            jax.ShapeDtypeStruct((8, 16, 128), F32),
            jax.ShapeDtypeStruct((n, SLOTS, 128), F32),
        ),
        in_specs=[vm] * 6 + [sm] * 3,
        out_specs=(vm,) * 8,
        cost_estimate=pl.CostEstimate(flops=20_000_000, bytes_accessed=12_000_000, transcendentals=0),
        compiler_params=pltpu.CompilerParams(vmem_limit_bytes=24 * 1024 * 1024),
        name="inner",
    )(te, th, tle, tlh, ta, tb, amp, tow, rcell)


def outer_kernel(
    depth_n,
    lat_n,
    te,
    th,
    tle,
    tlh,
    ta,
    tb,
    hh,
    mm,
    l1,
    l2,
    d0,
    ei,
    acc,
    samp,
    lo,
    hi,
    amp,
    tow,
    rcell,
    rowner,
    grad,
    send,
    eo,
    ho,
    mo,
    o1,
    o2,
    total,
    count,
):
    groups = te.shape[0]
    depth_at = lax.axis_index("depth")
    lat_at = lax.axis_index("lat")
    row_mask = first_row_mask(depth_at)
    keep = last_row_keep(depth_at, depth_n)
    a8, b8 = coefs(get_conductivity(hi, TO_LO), keep & (lat_at < lat_n - 1))
    al, bl = coefs(get_conductivity(lo, TO_HI), keep)
    left = jnp.where(lat_at == 0, 0.0, 1.0)
    total[...] = acc[...]

    def lam(n, g, x):
        if n == 0:
            return triple(tle, g, x)
        near = inside(n - 1, x)
        return triple((l1 if near else o1) if n == 1 else (l2 if near else o2), g, x)

    def one_group(g, carry):
        def high(k):
            return get_plane(hi, TO_LO, g, k)

        def low(k):
            return get_plane(lo, TO_HI, g, k)

        lx, point = tow_at(tow, g, depth_at, lat_at, lat_n)
        s = row_mask

        def m_of(n, x):
            return triple(mm if n <= x <= 6 - n else mo, g, x)

        def m_step(n, nxt):
            w = {8: nxt if n else (None, 0.0, 0.0)}

            def scaled(x):
                if x not in w:
                    w[x] = tuple(tb[x] * f for f in lam(n, g, x))
                return w[x]

            for x in range(8):
                if n <= x <= 6 - n:
                    continue
                k = curl_p(scaled(x), scaled(x + 1))
                base = triple(tlh, g, x) if n == 0 else m_of(n - 1, x)
                new = tuple(base[c] + (s if n else s * unstepped(16, -2)) * k[c] for c in range(3))
                if n == 0:
                    new = (new[0], new[1] - s * nxt[2], new[2] + s * nxt[1])
                for c in range(3):
                    mo[g, c, x] = new[c]

        def l_step(n, prv):
            out = (o1, o2)[n]
            for x in range(8):
                if inside(n, x):
                    continue
                k = curl_m(m_of(n, x), m_of(n, x - 1) if x else prv)
                old = lam(n, g, x)
                for c in range(3):
                    out[g, c, x] = ta[x] * old[c] - CC * k[c]

        m_step(0, (None, high(6), high(7)))
        first = lam(0, g, 0)
        dy, dz = -s * (tb[0] * first[2]), s * (tb[0] * first[1])
        l_step(0, (None, left * (low(6) + dy), left * (low(7) + dz)))
        last = m_of(0, 7)
        m_step(1, (None, b8 * (high(8) - CC * last[2]), b8 * (high(9) + CC * last[1])))
        wx, wy, wz = -CC * bl * (dmy(dz) - dmz(dy)), CC * bl * dz, -CC * bl * dy
        first = lam(1, g, 0)
        dy = dy + s * (dpz(wx) - (tb[0] * first[2] - wz))
        dz = dz + s * ((tb[0] * first[1] - wy) - dpy(wx))
        l_step(1, (None, left * (low(8) + dy), left * (low(9) + dz)))
        s = -CC * row_mask

        def e_of(n, x):
            if n == 0:
                return triple(te, g, x)
            ref = ei if inside(n - 1, x) else eo
            return tuple(ref[e_at(g, n - 1, c, x), :] for c in range(3))

        def h_of(n, x):
            return triple(hh if n <= x <= 6 - n else ho, g, x)

        def h_step(n, nxt):
            for x in range(8):
                if n <= x <= 6 - n:
                    continue
                after = (nxt if n else (None, 0.0, 0.0)) if x == 7 else e_of(n, x + 1)
                k = curl_p(e_of(n, x), after)
                base = triple(th, g, x) if n == 0 else h_of(n - 1, x)
                new = tuple(base[c] + (s if n else s * unstepped(17, -3)) * k[c] for c in range(3))
                if n == 0:
                    new = (new[0], new[1] - s * nxt[2], new[2] + s * nxt[1])
                for c in range(3):
                    ho[g, c, x] = new[c]

        def e_step(n, prv):
            for x in range(8):
                old = e_of(n, x)
                if inside(n, x):
                    if n == 0 and x in (1, 6):
                        k = tuple(d0[g, c, x // 6] for c in range(3))
                        total[x] += weighted(old, k, lam(2, g, x))
                    continue
                k = curl_m(h_of(n, x), h_of(n, x - 1) if x else prv)
                k = (k[0] - jnp.where(lx == x, amp[g, n], 0.0) * point, k[1], k[2])
                for c in range(3):
                    eo[e_at(g, n, c, x), :] = ta[x] * old[c] + tb[x] * k[c]
                total[x] += weighted(old, k, lam(2 - n, g, x))

        h_step(0, (None, high(0), high(1)))
        first = e_of(0, 0)
        dy, dz = -s * first[2], s * first[1]
        e_step(0, (None, left * (low(0) + dy), left * (low(1) + dz)))
        last = h_of(0, 7)
        uy, uz = b8 * last[2], -b8 * last[1]
        h_step(1, (None, high(2) + uy, high(3) + uz))
        ex, ey, ez = bl * (dmy(dz) - dmz(dy)), -bl * dz, bl * dy
        first = e_of(1, 0)
        dy = dy + s * (dpz(ex) - (first[2] - ez))
        dz = dz + s * ((first[1] - ey) - dpy(ex))
        e_step(1, (None, left * (low(2) + dy), left * (low(3) + dz)))
        last = h_of(1, 7)
        gx, gy, gz = s * (dpy(uz) - dpz(uy)), s * uz, -s * uy
        h_step(
            2,
            (
                None,
                high(4) + a8 * uy + b8 * (dmz(gx) - gz + last[2]),
                high(5) + a8 * uz + b8 * (gy - last[1] - dmy(gx)),
            ),
        )
        hx, hy, hz = s * (dpy(ez) - dpz(ey)), -s * ez, s * ey
        ex, ey, ez = (
            al * ex + bl * (dmy(dz) - dmz(dy)),
            al * ey + bl * (dmz(hx) - dz + hz),
            al * ez + bl * (dy - hy - dmy(hx)),
        )
        first = e_of(2, 0)
        dy = dy + s * (dpz(ex) - (first[2] - ez))
        dz = dz + s * ((first[1] - ey) - dpy(ex))
        e_step(2, (None, left * (low(4) + dy), left * (low(5) + dz)))
        return carry

    lax.fori_loop(0, groups, one_group, 0, unroll=True)
    for x in range(8):
        for half in range(2):
            rows = pl.ds(half * 64 + x, 8, stride=8)
            inv = tb[x, half * 8 : half * 8 + 8] * (1.0 / CC)
            grad[rows, :] = total[x, half * 8 : half * 8 + 8] * inv * inv
    send[...] = jnp.zeros_like(send)
    for o in range(send.shape[0]):
        count[o] = 0
    r24, lane = lax.broadcasted_iota(jnp.int32, (SLOTS, 128), 0), lanes()
    used = (r24 == lane) & (r24 < groups * 9)

    def put(r, values):
        o = rowner[r]
        slot = count[o]
        count[o] = slot + 1
        values = jnp.sum(samp[r] + values, axis=-1, keepdims=True)
        send[o, pl.ds(slot, 1), :] = jnp.sum(jnp.where(used, values, 0.0), axis=0, keepdims=True)

    take_samples(eo, rcell, jnp.logical_not, put)


def outer(te, th, tle, tlh, ta, tb, kept, lo, hi, amp, tow, rcell, rowner, depth_n, lat_n):
    g = te.shape[0]
    vm = pl.BlockSpec(memory_space=pltpu.VMEM)
    sm = pl.BlockSpec(memory_space=pltpu.SMEM)
    return pl.pallas_call(
        functools.partial(outer_kernel, depth_n, lat_n),
        out_shape=(
            jax.ShapeDtypeStruct((128, 128), F32),
            jax.ShapeDtypeStruct((lat_n, 2, 128), F32),
        ),
        in_specs=[vm] * 16 + [sm] * 4,
        out_specs=(vm,) * 2,
        scratch_shapes=[pltpu.VMEM((SLOTS * STRIDE, 128), F32)]
        + [pltpu.VMEM((g, 3, 8, ROWS, 128), F32)] * 4
        + [pltpu.VMEM((8, 16, 128), F32), pltpu.SMEM((lat_n,), jnp.int32)],
        cost_estimate=pl.CostEstimate(flops=10_000_000, bytes_accessed=12_000_000, transcendentals=0),
        compiler_params=pltpu.CompilerParams(vmem_limit_bytes=24 * 1024 * 1024),
        name="outer",
    )(te, th, tle, tlh, ta, tb, *kept, lo, hi, amp, tow, rcell, rowner)


def finish_kernel(mine, theirs, got, total, lines):
    total[...] = mine[...] + theirs[...]
    for slot in range(2):
        table = jnp.transpose(got[:, slot, :])
        for g in range(lines.shape[0]):
            lines[g, :, slot, :] = table[g * 9 : g * 9 + 9]


def finish(mine, theirs, got, groups):
    vm = pl.BlockSpec(memory_space=pltpu.VMEM)
    return pl.pallas_call(
        finish_kernel,
        out_shape=(
            jax.ShapeDtypeStruct(mine.shape, F32),
            jax.ShapeDtypeStruct((groups, 9, 2, got.shape[0]), F32),
        ),
        in_specs=[vm] * 3,
        out_specs=(vm,) * 2,
        compiler_params=pltpu.CompilerParams(vmem_limit_bytes=24 * 1024 * 1024),
        name="finish",
    )(mine, theirs, got)


def across(value, step):
    n = lax.axis_size("src")
    return lax.ppermute(value, "src", [(i, i ^ step) for i in range(n) if i ^ step < n])


def per_device(
    conductivity, e_start, h_start, e_weight, h_weight, source_amp, tow_cell, rec_cell, rec_owner
):
    groups = e_start.shape[0]
    depth_n, lat_n = lax.axis_size("depth"), lax.axis_size("lat")

    def flat(f):
        return f.reshape(groups, 3, 128, 128)

    e, h, le, lh = flat(e_start), flat(h_start), flat(e_weight), flat(h_weight)
    cond = conductivity.reshape(128, 128)
    fields = [
        pltpu.with_memory_space_constraint(f, pltpu.HBM) for f in (e, h, le, lh, cond)
    ]
    one, two = pack(*fields)
    one = swapped(one, "depth", 0)
    two = swapped(two, "depth", 1)
    own = own_planes(*fields)
    te, th, tle, tlh, ta, tb, to_lo, to_hi = planes(
        own, one, two, source_amp, tow_cell, depth_n, lat_n
    )
    cells, owners = rec_cell.reshape(-1), rec_owner.reshape(-1)
    hi = shifted(to_lo, "lat", -1)
    lo = shifted(to_hi, "lat", 1)
    kept = inner(te, th, tle, tlh, ta, tb, source_amp, tow_cell, cells, lat_n)
    grad, send = outer(
        te,
        th,
        tle,
        tlh,
        ta,
        tb,
        kept,
        lo,
        hi,
        source_amp,
        tow_cell,
        cells,
        owners,
        depth_n,
        lat_n,
    )
    got = lax.all_to_all(send, "lat", split_axis=0, concat_axis=0, tiled=True)
    every = lax.all_gather(grad, "src", axis=0, tiled=False)
    total, lines = finish(every[0] + every[1], every[2] + every[3], got, groups)
    total = total.reshape(16, 8, 128)
    lines = jnp.transpose(lines.reshape(groups, 1, 1, 9, 2, lat_n), (0, 1, 2, 5, 4, 3))
    return (total, lines)


def solution(mesh):
    placed = (
        P("depth", "lat", None),
        P("src", None, "depth", "lat", None),
        P("src", None, "depth", "lat", None),
        P("src", None, "depth", "lat", None),
        P("src", None, "depth", "lat", None),
        P("src", None),
        P("src"),
        P("depth", "lat", None),
        P("depth", "lat", None, None),
    )
    return jax.shard_map(
        per_device,
        mesh=mesh,
        in_specs=placed,
        out_specs=(P("depth", "lat", None), P("src", "depth", "lat", None, None, None)),
        check_vma=False,
    )
```

```python
import functools

import jax
import jax.numpy as jnp
from jax import lax
from jax.experimental import pallas as pl
from jax.experimental.pallas import tpu as pltpu
from jax.sharding import PartitionSpec as P

CC = 0.5
KK = 0.5
ROWS = 24
F32 = jnp.float32
UP = (0, 2, 4, 5)
DN = (1, 4, 5, 7)
SPAN = 8


def shifted(block, axis, distance):
    n = lax.axis_size(axis)
    route = [(i, i + distance) for i in range(n) if 0 <= i + distance < n]
    return lax.ppermute(block, axis, route)


def swapped(block, axis, first):
    n = lax.axis_size(axis)
    lower = range(first, n - 1, 2)
    return lax.ppermute(block, axis, [p for i in lower for p in ((i, i + 1), (i + 1, i))])


def lanes(rows=ROWS):
    return lax.broadcasted_iota(jnp.int32, (rows, 128), 1)


def zrow():
    r = lax.broadcasted_iota(jnp.int32, (ROWS, 128), 0)
    return jnp.where(r < 20, r, r - ROWS)


def yp(f):
    return jnp.where(lanes(f.shape[0]) == 127, 0.0, pltpu.roll(f, 127, 1))


def ym(f):
    return jnp.where(lanes() == 0, 0.0, pltpu.roll(f, 1, 1))


def zp(f):
    return pltpu.roll(f, ROWS - 1, 0)


def zm(f):
    return pltpu.roll(f, 1, 0)


def dpy(f):
    return yp(f) - f


def dpz(f):
    return zp(f) - f


def dmy(f):
    return f - ym(f)


def dmz(f):
    return f - zm(f)


def curl_p(f, nxt):
    fx, fy, fz = f
    return (dpy(fz) - dpz(fy), dpz(fx) - (nxt[2] - fz), (nxt[1] - fy) - dpy(fx))


def curl_m(f, prv):
    fx, fy, fz = f
    return (dmy(fz) - dmz(fy), dmz(fx) - (fz - prv[2]), (fy - prv[1]) - dmy(fx))


def coefs(conductivity, keep):
    inv = 1.0 / (1.0 + KK * conductivity)
    a, b = (1.0 - KK * conductivity) * inv, CC * inv
    if keep is True:
        return a, b
    return jnp.where(keep, a, 0.0), jnp.where(keep, b, 0.0)


def first_row_mask(depth_at):
    return jnp.where((zrow() < 0) & (depth_at == 0), 0.0, 1.0)


def unstepped(*rows):
    z = zrow()
    done = z == rows[0]
    for row in rows[1:]:
        done = done | (z == row)
    return jnp.where(done, 0.0, 1.0)


def last_row_keep(depth_at, depth_n):
    return jnp.logical_not((zrow() > 15) & (depth_at == depth_n - 1))


def stepped(fields, row, base, s, xp):
    fx, fy, fz = (fields(c, row) for c in range(3))
    gx, gy = fields(0, row + 1), fields(1, row + 1)
    return (
        base(0, row) + s * (dpy(fz) - (gy - fy)),
        base(1, row) + s * ((gx - fx) - (xp(fz) - fz)),
        base(2, row) + s * ((xp(fy) - fy) - dpy(fx)),
    )


def pack_kernel(e, h, le, lh, cond, one, two, ve, vh, vl, vm, vc, sems):
    even = lax.axis_index("depth") % 2 == 0
    copies = []
    for ref, dst in ((e, ve), (h, vh), (le, vl), (lh, vm)):
        n = dst.shape[2] // 16
        for k, first in enumerate((0, 16 - n)):
            copies.append(
                pltpu.make_async_copy(
                    ref.at[:, :, pl.ds(first * 8, n * 8)],
                    dst.at[:, :, pl.ds(k * n * 8, n * 8)],
                    sems.at[len(copies)],
                )
            )
    for k, first in enumerate((0, 14)):
        copies.append(
            pltpu.make_async_copy(
                cond.at[pl.ds(first * 8, 16)], vc.at[pl.ds(k * 16, 16)], sems.at[len(copies)]
            )
        )
    for c in copies:
        c.start()
    for c in copies:
        c.wait()
    sub = lax.broadcasted_iota(jnp.int32, (8, 128), 0)

    def xp(f):
        return jnp.where(sub == 7, 0.0, pltpu.roll(f, 7, 0))

    def tile(ref, g, c, z):
        n = ref.shape[2] // 16
        k = z if z < n else z - 16 + 2 * n
        return ref[g, c, k * 8 : k * 8 + 8]

    def layer(z):
        k = z if z < 2 else z - 12
        return vc[k * 8 : k * 8 + 8]

    def fill(up, dn):
        for g in range(e.shape[0]):

            def e_of(c, z, g=g):
                return tile(ve, g, c, z)

            def h_of(c, z, g=g):
                return tile(vh, g, c, z)

            def w_of(c, z, g=g):
                return CC / (1.0 + KK * layer(z)) * tile(vl, g, c, z)

            def m_of(c, z, g=g):
                return tile(vm, g, c, z)

            h17 = stepped(e_of, 1, h_of, -CC, xp)
            h3 = stepped(e_of, 13, h_of, -CC, xp)
            m16 = stepped(w_of, 0, m_of, 1.0, xp)
            m2 = stepped(w_of, 14, m_of, 1.0, xp)
            extra = jnp.where(sub == 0, e_of(2, 13), 0.0)
            extra = jnp.where(sub == 1, pltpu.roll(tile(vl, g, 2, 14), 1, 0), extra)
            for c in range(3):
                blank = jnp.zeros((8, 128), F32)
                ups = (e_of(c, 0), e_of(c, 1), h_of(c, 0), h17[c], tile(vl, g, c, 0), m16[c])
                ups += (layer(0), layer(1)) if g == 0 and c == 0 else (blank, blank)
                dns = (
                    e_of(c, 14),
                    e_of(c, 15),
                    h3[c] if c < 2 else extra,
                    h_of(c, 14),
                    h_of(c, 15),
                    tile(vl, g, c, 15),
                    m2[c] if c < 2 else layer(14 + g % 2),
                    m_of(c, 15),
                )
                for k in range(SPAN):
                    up[g, c, k * 8 : k * 8 + 8] = ups[k]
                    dn[g, c, k * 8 : k * 8 + 8] = dns[k]

    @pl.when(even)
    def _():
        fill(two, one)

    @pl.when(jnp.logical_not(even))
    def _():
        fill(one, two)


def pack(e, h, le, lh, cond):
    g = e.shape[0]
    message = jax.ShapeDtypeStruct((g, 3, SPAN * 8, 128), F32)
    return pl.pallas_call(
        pack_kernel,
        out_shape=(message, message),
        in_specs=[pl.BlockSpec(memory_space=pl.ANY)] * 5,
        out_specs=(pl.BlockSpec(memory_space=pltpu.VMEM),) * 2,
        scratch_shapes=[pltpu.VMEM((g, 3, 2 * n * 8, 128), F32) for n in (3, 3, 2, 2)]
        + [pltpu.VMEM((32, 128), F32), pltpu.SemaphoreType.DMA((10,))],
        compiler_params=pltpu.CompilerParams(vmem_limit_bytes=24 * 1024 * 1024),
        name="pack",
    )(e, h, le, lh, cond)


TO_LO = ((3, 17),) * 2 + (((2, 16),) * 2 + ((1, 15),) * 2) * 2
TO_HI = ((2, 17),) * 2 + (((1, 16),) * 2 + ((0, 15),) * 2) * 2


def offset(table, k):
    return sum(lo + hi + 1 for lo, hi in table[:k])


def chunk(table):
    return -(-(offset(table, len(table)) + 12) // 8) * 8


def put_plane(ref, table, g, k, value):
    lo, hi = table[k]
    at = offset(table, k)
    ref[g, at : at + hi + 1] = value[0 : hi + 1]
    if lo:
        ref[g, at + hi + 1 : at + hi + 1 + lo] = value[ROWS - lo : ROWS]


def get_plane(ref, table, g, k):
    lo, hi = table[k]
    at = offset(table, k)
    end = at + lo + hi + 1
    rest = ref[g, end - 8 : end]
    if hi > 15:
        r = lax.broadcasted_iota(jnp.int32, (8, 128), 0)
        rest = jnp.where(r < 4, ref[g, at + 16 : at + 24], rest)
    return jnp.concatenate([ref[g, at : at + 16], rest], axis=0)


def put_conductivity(ref, table, value):
    at = offset(table, len(table))
    ref[0, at : at + 8] = value[0:8]
    ref[1, at : at + 8] = value[8:16]
    ref[1, at + 8 : at + 10] = value[16:18]
    ref[1, at + 10 : at + 12] = value[22:24]


def get_conductivity(ref, table):
    at = offset(table, len(table))
    r = lax.broadcasted_iota(jnp.int32, (8, 128), 0)
    rest = ref[1, at + 4 : at + 12]
    rest = jnp.where(r < 4, pltpu.roll(rest, 4, 0), rest)
    return jnp.concatenate([ref[0, at : at + 8], ref[1, at : at + 8], rest], axis=0)


def own_kernel(e, h, le, lh, cond, te, th, tle, tlh, ta, tb, tc, be, bh, ble, blh, bc, sems):
    pairs = ((e, be), (h, bh), (le, ble), (lh, blh), (cond, bc))
    copies = [pltpu.make_async_copy(src, dst, sems.at[k]) for k, (src, dst) in enumerate(pairs)]
    for c in copies:
        c.start()
    for k, (src, dst) in enumerate(((be, te), (bh, th), (ble, tle), (blh, tlh))):
        copies[k].wait()

        def body(g, carry, src=src, dst=dst):
            for c in range(3):
                for x in range(8):
                    dst[g, c, x, 0:8] = src[g, c, pl.ds(x, 8, stride=8), :]
                    dst[g, c, x, 8:16] = src[g, c, pl.ds(64 + x, 8, stride=8), :]
            return carry

        lax.fori_loop(0, e.shape[0], body, 0)
    copies[4].wait()
    for x in range(8):
        for half in range(2):
            value = bc[pl.ds(half * 64 + x, 8, stride=8), :]
            at = pl.ds(half * 8, 8)
            tc[x, at] = value
            ta[x, at], tb[x, at] = coefs(value, True)


def own_planes(e, h, le, lh, cond):
    g = e.shape[0]
    vm = pl.BlockSpec(memory_space=pltpu.VMEM)
    field = jax.ShapeDtypeStruct((g, 3, 8, ROWS, 128), F32)
    return pl.pallas_call(
        own_kernel,
        out_shape=(field,) * 4
        + (jax.ShapeDtypeStruct((8, ROWS, 128), F32),) * 2
        + (jax.ShapeDtypeStruct((8, 16, 128), F32),),
        in_specs=[pl.BlockSpec(memory_space=pl.ANY)] * 5,
        out_specs=(vm,) * 7,
        scratch_shapes=[pltpu.VMEM((g, 3, 128, 128), F32)] * 4
        + [pltpu.VMEM((128, 128), F32), pltpu.SemaphoreType.DMA((5,))],
        cost_estimate=pl.CostEstimate(flops=5_000_000, bytes_accessed=8_000_000, transcendentals=0),
        compiler_params=pltpu.CompilerParams(vmem_limit_bytes=24 * 1024 * 1024),
        name="own",
    )(e, h, le, lh, cond)


def planes_kernel(
    depth_n,
    lat_n,
    ie,
    ih,
    ile,
    ilh,
    ia,
    ib,
    tc,
    one,
    two,
    amp,
    tow,
    te,
    th,
    tle,
    tlh,
    ta,
    tb,
    to_lo,
    to_hi,
):
    groups = te.shape[0]
    depth_at = lax.axis_index("depth")
    lat_at = lax.axis_index("lat")

    even = depth_at % 2 == 0

    r8 = lax.broadcasted_iota(jnp.int32, (8, 128), 0)

    def halos(up, dn):
        def halo(g, carry):
            for c in range(3):
                for x in range(8):
                    hi = up[g, c, pl.ds(x, 8, stride=8), :]
                    lo = dn[g, c, pl.ds(x, 8, stride=8), :]
                    for field, dst in enumerate((te, th, tle, tlh)):
                        a = pltpu.roll(hi, 8 - UP[field], 0) if UP[field] else hi
                        b = pltpu.roll(lo, 7 - DN[field], 0) if DN[field] != 7 else lo
                        dst[g, c, x, 16:24] = jnp.where(r8 < 4, a, b)
            te[g, 2, 0, 21:22] = dn[g, 2, 16:17]
            tle[g, 2, 0, 22:23] = dn[g, 2, 17:18]
            return carry

        lax.fori_loop(0, groups, halo, 0)

    @pl.when(even)
    def _():
        halos(one, two)

    @pl.when(jnp.logical_not(even))
    def _():
        halos(two, one)

    keep = last_row_keep(depth_at, depth_n)

    def edge(first, second, g, c, slot):
        rows = pl.ds(slot * 8, 8)
        return jnp.where(even, first[g, c, rows, :], second[g, c, rows, :])

    u0, u1 = (edge(one, two, 0, 0, 6 + k) for k in range(2))
    d0, d1 = (edge(two, one, k, 2, 6) for k in range(2))
    for x in range(8):
        rest = jnp.where(r8 == 0, u0[x : x + 1], 1.0)
        rest = jnp.where(r8 == 1, u1[x : x + 1], rest)
        rest = jnp.where(r8 == 6, d0[x : x + 1], rest)
        rest = jnp.where(r8 == 7, d1[x : x + 1], rest)
        ta[x, 16:24], tb[x, 16:24] = coefs(rest, keep[16:24])
        if x == 0:
            put_conductivity(to_lo, TO_LO, jnp.concatenate([tc[x], rest], axis=0))
        if x == 7:
            put_conductivity(to_hi, TO_HI, jnp.concatenate([tc[x], rest], axis=0))
    row_mask = first_row_mask(depth_at)
    z, lane = zrow(), lanes()

    first_e, first_l = unstepped(17, -3), unstepped(16, -2)

    def forward_planes(g, carry):
        s = -CC * row_mask
        s_first = s * first_e
        cell = tow[g]
        lz = cell // (1024 * lat_n) - depth_at * 16
        lx = cell // 128 % (8 * lat_n) - lat_at * 8
        point = jnp.where((z == lz) & (lane == cell % 128), 1.0, 0.0)

        def e0(x):
            return tuple(te[g, c, x] for c in range(3))

        def h0(x):
            return tuple(th[g, c, x] for c in range(3))

        def step_h(x):
            return tuple(f + s_first * k for f, k in zip(h0(x), curl_p(e0(x), e0(x + 1))))

        def put(ref, k, value):
            put_plane(ref, TO_LO if ref is to_lo else TO_HI, g, k, value)

        def hit(x, n):
            return jnp.where(lx == x, amp[g, n], 0.0) * point

        zero = (None, 0.0, 0.0)
        a0, b0, a1, b1 = ta[0], tb[0], ta[1], tb[1]
        f0, f1 = e0(0), e0(1)
        h1, k1 = step_h(0), step_h(1)
        put(to_lo, 0, f0[1])
        put(to_lo, 1, f0[2])
        m = curl_m(h1, zero)
        e1 = (a0 * f0[0] + b0 * (m[0] - hit(0, 0)), a0 * f0[1] + b0 * m[1], a0 * f0[2] + b0 * m[2])
        put(to_lo, 2, e1[1])
        put(to_lo, 3, e1[2])
        m = curl_m(k1, h1)
        k = curl_p(e1, (None, a1 * f1[1] + b1 * m[1], a1 * f1[2] + b1 * m[2]))
        h2 = tuple(h1[c] + s * k[c] for c in range(3))
        m = curl_m(h2, zero)
        put(to_lo, 4, a0 * e1[1] + b0 * m[1])
        put(to_lo, 5, a0 * e1[2] + b0 * m[2])
        a7, b7, a6, b6 = ta[7], tb[7], ta[6], tb[6]
        f7, f6 = e0(7), e0(6)
        k = curl_p(f7, zero)
        h7 = tuple(f + s_first * t for f, t in zip(h0(7), k))
        put(to_hi, 0, h7[1])
        put(to_hi, 1, h7[2])
        h6, h5 = step_h(6), step_h(5)
        m7, m6 = curl_m(h7, h6), curl_m(h6, h5)
        e7 = (a7 * f7[0] + b7 * (m7[0] - hit(7, 0)), a7 * f7[1] + b7 * m7[1], a7 * f7[2] + b7 * m7[2])
        e6 = (a6 * f6[0] + b6 * (m6[0] - hit(6, 0)), a6 * f6[1] + b6 * m6[1], a6 * f6[2] + b6 * m6[2])
        k7, k6 = curl_p(e7, zero), curl_p(e6, e7)
        h7 = tuple(h7[c] + s * k7[c] for c in range(3))
        h6 = tuple(h6[c] + s * k6[c] for c in range(3))
        put(to_hi, 2, h7[1])
        put(to_hi, 3, h7[2])
        m7 = curl_m(h7, h6)
        e7 = (a7 * e7[0] + b7 * (m7[0] - hit(7, 1)), a7 * e7[1] + b7 * m7[1], a7 * e7[2] + b7 * m7[2])
        k7 = curl_p(e7, zero)
        put(to_hi, 4, h7[1] + s * k7[1])
        put(to_hi, 5, h7[2] + s * k7[2])
        s = row_mask
        m_first = s * first_l

        def l0(x):
            return tuple(tle[g, c, x] for c in range(3))

        def w0(x):
            return tuple(tb[x] * f for f in l0(x))

        def m0(x):
            return tuple(tlh[g, c, x] for c in range(3))

        def step_m(x):
            return tuple(f + m_first * k for f, k in zip(m0(x), curl_p(w0(x), w0(x + 1))))

        q0, v0 = l0(0), w0(0)
        put(to_lo, 6, v0[1])
        put(to_lo, 7, v0[2])
        m = curl_m(step_m(0), zero)
        put(to_lo, 8, a0 * q0[1] - CC * m[1])
        put(to_lo, 9, a0 * q0[2] - CC * m[2])
        q7 = l0(7)
        k7 = curl_p(w0(7), zero)
        n7 = tuple(f + m_first * t for f, t in zip(m0(7), k7))
        put(to_hi, 6, n7[1])
        put(to_hi, 7, n7[2])
        m = curl_m(n7, step_m(6))
        k7 = curl_p(tuple(b7 * (a7 * q7[c] - CC * m[c]) for c in range(3)), zero)
        put(to_hi, 8, n7[1] + s * k7[1])
        put(to_hi, 9, n7[2] + s * k7[2])
        return carry

    lax.fori_loop(0, groups, forward_planes, 0, unroll=True)


def planes(own, one, two, amp, tow, depth_n, lat_n):
    g = one.shape[0]
    vm = pl.BlockSpec(memory_space=pltpu.VMEM)
    sm = pl.BlockSpec(memory_space=pltpu.SMEM)
    field = jax.ShapeDtypeStruct((g, 3, 8, ROWS, 128), F32)
    coef = jax.ShapeDtypeStruct((8, ROWS, 128), F32)
    return pl.pallas_call(
        functools.partial(planes_kernel, depth_n, lat_n),
        out_shape=(
            field,
            field,
            field,
            field,
            coef,
            coef,
            jax.ShapeDtypeStruct((g, chunk(TO_LO), 128), F32),
            jax.ShapeDtypeStruct((g, chunk(TO_HI), 128), F32),
        ),
        in_specs=[vm] * 9 + [sm] * 2,
        out_specs=(vm,) * 8,
        input_output_aliases={0: 0, 1: 1, 2: 2, 3: 3, 4: 4, 5: 5},
        compiler_params=pltpu.CompilerParams(vmem_limit_bytes=24 * 1024 * 1024),
        name="planes",
    )(*own, one, two, amp, tow)


SLOTS = 24
STRIDE = 8 * ROWS


def e_at(g, n, c, x):
    return pl.ds(pl.multiple_of((g * 9 + n * 3 + c) * STRIDE + x * ROWS, 8), ROWS)


def triple(ref, g, x):
    return tuple(ref[g, c, x] for c in range(3))


def inside(n, x):
    return n + 1 <= x <= 6 - n


def weighted(old, drive, weight):
    total = None
    for c in range(3):
        t = (-2.0 * KK * old[c][0:16] - CC * KK * drive[c][0:16]) * weight[c][0:16]
        total = t if total is None else total + t
    return total


def take_samples(store, rcell, use, put):
    k = lax.broadcasted_iota(jnp.int32, (SLOTS, 128), 0)
    step = k // 3 % 3
    lane = lanes()

    def body(r, c0):
        cell = rcell[r]
        z, x, y = cell // 1024, cell // 128 % 8, cell % 128
        rows = store[pl.ds(x * ROWS + z, SLOTS, stride=STRIDE), :]
        near = (x >= step + 1) & (x <= 6 - step)
        put(r, jnp.where((lane == y) & use(near), rows, 0.0))
        return c0

    lax.fori_loop(0, rcell.shape[0], body, 0, unroll=True)


def tow_at(tow, g, depth_at, lat_at, lat_n):
    cell = tow[g]
    lz = cell // (1024 * lat_n) - depth_at * 16
    lx = cell // 128 % (8 * lat_n) - lat_at * 8
    point = jnp.where((zrow() == lz) & (lanes() == cell % 128), 1.0, 0.0)
    return lx, point


def inner_kernel(
    lat_n, te, th, tle, tlh, ta, tb, amp, tow, rcell, hh, mm, l1, l2, d0, ei, acc, samp
):
    groups = te.shape[0]
    depth_at = lax.axis_index("depth")
    lat_at = lax.axis_index("lat")
    row_mask = first_row_mask(depth_at)
    acc[...] = jnp.zeros_like(acc)

    def one_group(g, carry):
        lx, point = tow_at(tow, g, depth_at, lat_at, lat_n)
        lam = (tle, l1, l2)
        for n in range(2):
            s = row_mask * unstepped(16, -2) if n == 0 else row_mask
            w = {}

            def scaled(x, n=n, w=w):
                if x not in w:
                    w[x] = tuple(tb[x] * f for f in triple(lam[n], g, x))
                return w[x]

            for x in range(n, 7 - n):
                k = curl_p(scaled(x), scaled(x + 1))
                base = triple(tlh if n == 0 else mm, g, x)
                for c in range(3):
                    mm[g, c, x] = base[c] + s * k[c]
            for x in range(n + 1, 7 - n):
                k = curl_m(triple(mm, g, x), triple(mm, g, x - 1))
                old = triple(lam[n], g, x)
                for c in range(3):
                    lam[n + 1][g, c, x] = ta[x] * old[c] - CC * k[c]
        def e_of(n, x):
            if n == 0:
                return triple(te, g, x)
            return tuple(ei[e_at(g, n - 1, c, x), :] for c in range(3))

        for n in range(3):
            s = -CC * (row_mask * unstepped(17, -3) if n == 0 else row_mask)
            for x in range(n, 7 - n):
                k = curl_p(e_of(n, x), e_of(n, x + 1))
                base = triple(th if n == 0 else hh, g, x)
                for c in range(3):
                    hh[g, c, x] = base[c] + s * k[c]
            for x in range(n + 1, 7 - n):
                k = curl_m(triple(hh, g, x), triple(hh, g, x - 1))
                k = (k[0] - jnp.where(lx == x, amp[g, n], 0.0) * point, k[1], k[2])
                old = e_of(n, x)
                for c in range(3):
                    ei[e_at(g, n, c, x), :] = ta[x] * old[c] + tb[x] * k[c]
                if n == 0 and x in (1, 6):
                    for c in range(3):
                        d0[g, c, x // 6] = k[c][0:16]
                else:
                    acc[x] += weighted(old, k, triple(lam[2 - n], g, x))
        return carry

    lax.fori_loop(0, groups, one_group, 0, unroll=True)

    def put(r, values):
        samp[r] = values

    take_samples(ei, rcell, lambda near: near, put)


def inner(te, th, tle, tlh, ta, tb, amp, tow, rcell, lat_n):
    g, n = te.shape[0], rcell.shape[0]
    vm = pl.BlockSpec(memory_space=pltpu.VMEM)
    sm = pl.BlockSpec(memory_space=pltpu.SMEM)
    field = jax.ShapeDtypeStruct((g, 3, 8, ROWS, 128), F32)
    return pl.pallas_call(
        functools.partial(inner_kernel, lat_n),
        out_shape=(
            field,
            field,
            field,
            field,
            jax.ShapeDtypeStruct((g, 3, 2, 16, 128), F32),
            jax.ShapeDtypeStruct((SLOTS * STRIDE, 128), F32),
            jax.ShapeDtypeStruct((8, 16, 128), F32),
            jax.ShapeDtypeStruct((n, SLOTS, 128), F32),
        ),
        in_specs=[vm] * 6 + [sm] * 3,
        out_specs=(vm,) * 8,
        cost_estimate=pl.CostEstimate(flops=20_000_000, bytes_accessed=12_000_000, transcendentals=0),
        compiler_params=pltpu.CompilerParams(vmem_limit_bytes=24 * 1024 * 1024),
        name="inner",
    )(te, th, tle, tlh, ta, tb, amp, tow, rcell)


def outer_kernel(
    depth_n,
    lat_n,
    te,
    th,
    tle,
    tlh,
    ta,
    tb,
    hh,
    mm,
    l1,
    l2,
    d0,
    ei,
    acc,
    samp,
    lo,
    hi,
    amp,
    tow,
    rcell,
    rowner,
    grad,
    send,
    eo,
    ho,
    mo,
    o1,
    o2,
    total,
    drives,
    staged,
    count,
    sem,
):
    groups = te.shape[0]
    depth_at = lax.axis_index("depth")
    lat_at = lax.axis_index("lat")
    row_mask = first_row_mask(depth_at)
    keep = last_row_keep(depth_at, depth_n)
    a8, b8 = coefs(get_conductivity(hi, TO_LO), keep & (lat_at < lat_n - 1))
    al, bl = coefs(get_conductivity(lo, TO_HI), keep)
    left = jnp.where(lat_at == 0, 0.0, 1.0)
    total[...] = acc[...]

    def lam(n, g, x):
        if n == 0:
            return triple(tle, g, x)
        near = inside(n - 1, x)
        return triple((l1 if near else o1) if n == 1 else (l2 if near else o2), g, x)

    def e_of(n, g, x):
        if n == 0:
            return triple(te, g, x)
        ref = ei if inside(n - 1, x) else eo
        return tuple(ref[e_at(g, n - 1, c, x), :] for c in range(3))

    def forward(g, carry):
        def high(k):
            return get_plane(hi, TO_LO, g, k)

        def low(k):
            return get_plane(lo, TO_HI, g, k)

        lx, point = tow_at(tow, g, depth_at, lat_at, lat_n)
        s = -CC * row_mask

        def h_of(n, x):
            return triple(hh if n <= x <= 6 - n else ho, g, x)

        def h_step(n, nxt):
            for x in range(8):
                if n <= x <= 6 - n:
                    continue
                after = (nxt if n else (None, 0.0, 0.0)) if x == 7 else e_of(n, g, x + 1)
                k = curl_p(e_of(n, g, x), after)
                base = triple(th, g, x) if n == 0 else h_of(n - 1, x)
                new = tuple(base[c] + (s if n else s * unstepped(17, -3)) * k[c] for c in range(3))
                if n == 0:
                    new = (new[0], new[1] - s * nxt[2], new[2] + s * nxt[1])
                for c in range(3):
                    ho[g, c, x] = new[c]

        def e_step(n, prv):
            for x in range(8):
                if inside(n, x):
                    continue
                old = e_of(n, g, x)
                k = curl_m(h_of(n, x), h_of(n, x - 1) if x else prv)
                k = (k[0] - jnp.where(lx == x, amp[g, n], 0.0) * point, k[1], k[2])
                for c in range(3):
                    eo[e_at(g, n, c, x), :] = ta[x] * old[c] + tb[x] * k[c]
                    drives[g, n, c, x] = k[c][0:16]

        h_step(0, (None, high(0), high(1)))
        first = e_of(0, g, 0)
        dy, dz = -s * first[2], s * first[1]
        e_step(0, (None, left * (low(0) + dy), left * (low(1) + dz)))
        last = h_of(0, 7)
        uy, uz = b8 * last[2], -b8 * last[1]
        h_step(1, (None, high(2) + uy, high(3) + uz))
        ex, ey, ez = bl * (dmy(dz) - dmz(dy)), -bl * dz, bl * dy
        first = e_of(1, g, 0)
        dy = dy + s * (dpz(ex) - (first[2] - ez))
        dz = dz + s * ((first[1] - ey) - dpy(ex))
        e_step(1, (None, left * (low(2) + dy), left * (low(3) + dz)))
        last = h_of(1, 7)
        gx, gy, gz = s * (dpy(uz) - dpz(uy)), s * uz, -s * uy
        h_step(
            2,
            (
                None,
                high(4) + a8 * uy + b8 * (dmz(gx) - gz + last[2]),
                high(5) + a8 * uz + b8 * (gy - last[1] - dmy(gx)),
            ),
        )
        hx, hy, hz = s * (dpy(ez) - dpz(ey)), -s * ez, s * ey
        ex, ey, ez = (
            al * ex + bl * (dmy(dz) - dmz(dy)),
            al * ey + bl * (dmz(hx) - dz + hz),
            al * ez + bl * (dy - hy - dmy(hx)),
        )
        first = e_of(2, g, 0)
        dy = dy + s * (dpz(ex) - (first[2] - ez))
        dz = dz + s * ((first[1] - ey) - dpy(ex))
        e_step(2, (None, left * (low(4) + dy), left * (low(5) + dz)))
        return carry

    lax.fori_loop(0, groups, forward, 0, unroll=True)
    staged[...] = jnp.zeros_like(staged)
    for o in range(staged.shape[0]):
        count[o] = 0
    r24, lane = lax.broadcasted_iota(jnp.int32, (SLOTS, 128), 0), lanes()
    used = (r24 == lane) & (r24 < groups * 9)

    def put(r, values):
        o = rowner[r]
        slot = count[o]
        count[o] = slot + 1
        values = jnp.sum(samp[r] + values, axis=-1, keepdims=True)
        staged[o, pl.ds(slot, 1), :] = jnp.sum(jnp.where(used, values, 0.0), axis=0, keepdims=True)

    take_samples(eo, rcell, jnp.logical_not, put)
    leave = pltpu.make_async_copy(staged, send, sem)
    leave.start()

    def adjoint(g, carry):
        def high(k):
            return get_plane(hi, TO_LO, g, k)

        def low(k):
            return get_plane(lo, TO_HI, g, k)

        s = row_mask

        def m_of(n, x):
            return triple(mm if n <= x <= 6 - n else mo, g, x)

        def m_step(n, nxt):
            w = {8: nxt if n else (None, 0.0, 0.0)}

            def scaled(x):
                if x not in w:
                    w[x] = tuple(tb[x] * f for f in lam(n, g, x))
                return w[x]

            for x in range(8):
                if n <= x <= 6 - n:
                    continue
                k = curl_p(scaled(x), scaled(x + 1))
                base = triple(tlh, g, x) if n == 0 else m_of(n - 1, x)
                new = tuple(base[c] + (s if n else s * unstepped(16, -2)) * k[c] for c in range(3))
                if n == 0:
                    new = (new[0], new[1] - s * nxt[2], new[2] + s * nxt[1])
                for c in range(3):
                    mo[g, c, x] = new[c]

        def l_step(n, prv):
            out = (o1, o2)[n]
            for x in range(8):
                if inside(n, x):
                    continue
                k = curl_m(m_of(n, x), m_of(n, x - 1) if x else prv)
                old = lam(n, g, x)
                for c in range(3):
                    out[g, c, x] = ta[x] * old[c] - CC * k[c]

        m_step(0, (None, high(6), high(7)))
        first = lam(0, g, 0)
        dy, dz = -s * (tb[0] * first[2]), s * (tb[0] * first[1])
        l_step(0, (None, left * (low(6) + dy), left * (low(7) + dz)))
        last = m_of(0, 7)
        m_step(1, (None, b8 * (high(8) - CC * last[2]), b8 * (high(9) + CC * last[1])))
        wx, wy, wz = -CC * bl * (dmy(dz) - dmz(dy)), CC * bl * dz, -CC * bl * dy
        first = lam(1, g, 0)
        dy = dy + s * (dpz(wx) - (tb[0] * first[2] - wz))
        dz = dz + s * ((tb[0] * first[1] - wy) - dpy(wx))
        l_step(1, (None, left * (low(8) + dy), left * (low(9) + dz)))
        for n in range(3):
            for x in range(8):
                if n == 0 and x in (1, 6):
                    drive = tuple(d0[g, c, x // 6] for c in range(3))
                elif inside(n, x):
                    continue
                else:
                    drive = tuple(drives[g, n, c, x] for c in range(3))
                total[x] += weighted(e_of(n, g, x), drive, lam(2 - n, g, x))
        return carry

    lax.fori_loop(0, groups, adjoint, 0, unroll=True)
    for x in range(8):
        for half in range(2):
            rows = pl.ds(half * 64 + x, 8, stride=8)
            inv = tb[x, half * 8 : half * 8 + 8] * (1.0 / CC)
            grad[rows, :] = total[x, half * 8 : half * 8 + 8] * inv * inv
    leave.wait()


def outer(te, th, tle, tlh, ta, tb, kept, lo, hi, amp, tow, rcell, rowner, depth_n, lat_n):
    g = te.shape[0]
    vm = pl.BlockSpec(memory_space=pltpu.VMEM)
    sm = pl.BlockSpec(memory_space=pltpu.SMEM)
    return pl.pallas_call(
        functools.partial(outer_kernel, depth_n, lat_n),
        out_shape=(
            jax.ShapeDtypeStruct((128, 128), F32),
            jax.ShapeDtypeStruct((lat_n, 2, 128), F32),
        ),
        in_specs=[vm] * 16 + [sm] * 4,
        out_specs=(vm, pl.BlockSpec(memory_space=pl.ANY)),
        scratch_shapes=[pltpu.VMEM((SLOTS * STRIDE, 128), F32)]
        + [pltpu.VMEM((g, 3, 8, ROWS, 128), F32)] * 4
        + [
            pltpu.VMEM((8, 16, 128), F32),
            pltpu.VMEM((g, 3, 3, 8, 16, 128), F32),
            pltpu.VMEM((lat_n, 2, 128), F32),
            pltpu.SMEM((lat_n,), jnp.int32),
            pltpu.SemaphoreType.DMA(()),
        ],
        cost_estimate=pl.CostEstimate(flops=10_000_000, bytes_accessed=12_000_000, transcendentals=0),
        compiler_params=pltpu.CompilerParams(vmem_limit_bytes=24 * 1024 * 1024),
        name="outer",
    )(te, th, tle, tlh, ta, tb, *kept, lo, hi, amp, tow, rcell, rowner)


def finish_kernel(mine, theirs, got, total, lines):
    total[...] = mine[...] + theirs[...]
    for slot in range(2):
        table = jnp.transpose(got[:, slot, :])
        for g in range(lines.shape[0]):
            lines[g, :, slot, :] = table[g * 9 : g * 9 + 9]


def finish(mine, theirs, got, groups):
    vm = pl.BlockSpec(memory_space=pltpu.VMEM)
    return pl.pallas_call(
        finish_kernel,
        out_shape=(
            jax.ShapeDtypeStruct(mine.shape, F32),
            jax.ShapeDtypeStruct((groups, 9, 2, got.shape[0]), F32),
        ),
        in_specs=[vm] * 3,
        out_specs=(vm,) * 2,
        compiler_params=pltpu.CompilerParams(vmem_limit_bytes=24 * 1024 * 1024),
        name="finish",
    )(mine, theirs, got)


def across(value, step):
    n = lax.axis_size("src")
    return lax.ppermute(value, "src", [(i, i ^ step) for i in range(n) if i ^ step < n])


def per_device(
    conductivity, e_start, h_start, e_weight, h_weight, source_amp, tow_cell, rec_cell, rec_owner
):
    groups = e_start.shape[0]
    depth_n, lat_n = lax.axis_size("depth"), lax.axis_size("lat")

    def flat(f):
        return f.reshape(groups, 3, 128, 128)

    e, h, le, lh = flat(e_start), flat(h_start), flat(e_weight), flat(h_weight)
    cond = conductivity.reshape(128, 128)
    fields = [
        pltpu.with_memory_space_constraint(f, pltpu.HBM) for f in (e, h, le, lh, cond)
    ]
    one, two = pack(*fields)
    one = swapped(one, "depth", 0)
    two = swapped(two, "depth", 1)
    own = own_planes(*fields)
    te, th, tle, tlh, ta, tb, to_lo, to_hi = planes(
        own, one, two, source_amp, tow_cell, depth_n, lat_n
    )
    cells, owners = rec_cell.reshape(-1), rec_owner.reshape(-1)
    hi = shifted(to_lo, "lat", -1)
    lo = shifted(to_hi, "lat", 1)
    kept = inner(te, th, tle, tlh, ta, tb, source_amp, tow_cell, cells, lat_n)
    grad, send = outer(
        te,
        th,
        tle,
        tlh,
        ta,
        tb,
        kept,
        lo,
        hi,
        source_amp,
        tow_cell,
        cells,
        owners,
        depth_n,
        lat_n,
    )
    got = lax.all_to_all(send, "lat", split_axis=0, concat_axis=0, tiled=True)
    every = lax.all_gather(grad, "src", axis=0, tiled=False)
    total, lines = finish(every[0] + every[1], every[2] + every[3], got, groups)
    total = total.reshape(16, 8, 128)
    lines = jnp.transpose(lines.reshape(groups, 1, 1, 9, 2, lat_n), (0, 1, 2, 5, 4, 3))
    return (total, lines)


def solution(mesh):
    placed = (
        P("depth", "lat", None),
        P("src", None, "depth", "lat", None),
        P("src", None, "depth", "lat", None),
        P("src", None, "depth", "lat", None),
        P("src", None, "depth", "lat", None),
        P("src", None),
        P("src"),
        P("depth", "lat", None),
        P("depth", "lat", None, None),
    )
    return jax.shard_map(
        per_device,
        mesh=mesh,
        in_specs=placed,
        out_specs=(P("depth", "lat", None), P("src", "depth", "lat", None, None, None)),
        check_vma=False,
    )
```

```python
import functools

import jax
import jax.numpy as jnp
from jax import lax
from jax.experimental import pallas as pl
from jax.experimental.pallas import tpu as pltpu
from jax.sharding import PartitionSpec as P

CC = 0.5
KK = 0.5
ROWS = 24
F32 = jnp.float32
UP = (0, 2, 4, 5)
DN = (1, 4, 5, 7)
SPAN = 8


def shifted(block, axis, distance):
    n = lax.axis_size(axis)
    route = [(i, i + distance) for i in range(n) if 0 <= i + distance < n]
    return lax.ppermute(block, axis, route)


def swapped(block, axis, first):
    n = lax.axis_size(axis)
    lower = range(first, n - 1, 2)
    return lax.ppermute(block, axis, [p for i in lower for p in ((i, i + 1), (i + 1, i))])


def lanes(rows=ROWS):
    return lax.broadcasted_iota(jnp.int32, (rows, 128), 1)


def zrow():
    r = lax.broadcasted_iota(jnp.int32, (ROWS, 128), 0)
    return jnp.where(r < 20, r, r - ROWS)


def yp(f):
    return jnp.where(lanes(f.shape[0]) == 127, 0.0, pltpu.roll(f, 127, 1))


def ym(f):
    return jnp.where(lanes() == 0, 0.0, pltpu.roll(f, 1, 1))


def zp(f):
    return pltpu.roll(f, ROWS - 1, 0)


def zm(f):
    return pltpu.roll(f, 1, 0)


def dpy(f):
    return yp(f) - f


def dpz(f):
    return zp(f) - f


def dmy(f):
    return f - ym(f)


def dmz(f):
    return f - zm(f)


def curl_p(f, nxt):
    fx, fy, fz = f
    return (dpy(fz) - dpz(fy), dpz(fx) - (nxt[2] - fz), (nxt[1] - fy) - dpy(fx))


def curl_m(f, prv):
    fx, fy, fz = f
    return (dmy(fz) - dmz(fy), dmz(fx) - (fz - prv[2]), (fy - prv[1]) - dmy(fx))


def coefs(conductivity, keep):
    inv = 1.0 / (1.0 + KK * conductivity)
    a, b = (1.0 - KK * conductivity) * inv, CC * inv
    if keep is True:
        return a, b
    return jnp.where(keep, a, 0.0), jnp.where(keep, b, 0.0)


def first_row_mask(depth_at):
    return jnp.where((zrow() < 0) & (depth_at == 0), 0.0, 1.0)


def unstepped(*rows):
    z = zrow()
    done = z == rows[0]
    for row in rows[1:]:
        done = done | (z == row)
    return jnp.where(done, 0.0, 1.0)


def last_row_keep(depth_at, depth_n):
    return jnp.logical_not((zrow() > 15) & (depth_at == depth_n - 1))


def stepped(fields, row, base, s, xp):
    fx, fy, fz = (fields(c, row) for c in range(3))
    gx, gy = fields(0, row + 1), fields(1, row + 1)
    return (
        base(0, row) + s * (dpy(fz) - (gy - fy)),
        base(1, row) + s * ((gx - fx) - (xp(fz) - fz)),
        base(2, row) + s * ((xp(fy) - fy) - dpy(fx)),
    )


def pack_kernel(e, h, le, lh, cond, one, two, ve, vh, vl, vm, vc, sems):
    even = lax.axis_index("depth") % 2 == 0
    copies = []
    for ref, dst in ((e, ve), (h, vh), (le, vl), (lh, vm)):
        n = dst.shape[2] // 16
        for k, first in enumerate((0, 16 - n)):
            copies.append(
                pltpu.make_async_copy(
                    ref.at[:, :, pl.ds(first * 8, n * 8)],
                    dst.at[:, :, pl.ds(k * n * 8, n * 8)],
                    sems.at[len(copies)],
                )
            )
    for k, first in enumerate((0, 14)):
        copies.append(
            pltpu.make_async_copy(
                cond.at[pl.ds(first * 8, 16)], vc.at[pl.ds(k * 16, 16)], sems.at[len(copies)]
            )
        )
    for c in copies:
        c.start()
    sub = lax.broadcasted_iota(jnp.int32, (8, 128), 0)

    def xp(f):
        return jnp.where(sub == 7, 0.0, pltpu.roll(f, 7, 0))

    def tile(ref, g, c, z):
        n = ref.shape[2] // 16
        k = z if z < n else z - 16 + 2 * n
        return ref[g, c, k * 8 : k * 8 + 8]

    def layer(z):
        k = z if z < 2 else z - 12
        return vc[k * 8 : k * 8 + 8]

    def fill(up, dn):
        def store(ref, g, c, slot, value):
            ref[g, c, slot * 8 : slot * 8 + 8] = value

        for c in copies[:4]:
            c.wait()
        for g in range(e.shape[0]):

            def e_of(c, z, g=g):
                return tile(ve, g, c, z)

            def h_of(c, z, g=g):
                return tile(vh, g, c, z)

            h17 = stepped(e_of, 1, h_of, -CC, xp)
            h3 = stepped(e_of, 13, h_of, -CC, xp)
            for c in range(3):
                for k, value in enumerate((e_of(c, 0), e_of(c, 1), h_of(c, 0), h17[c])):
                    store(up, g, c, k, value)
                for k, z in ((0, 14), (1, 15)):
                    store(dn, g, c, k, e_of(c, z))
                    store(dn, g, c, 3 + k, h_of(c, z))
                if c < 2:
                    store(dn, g, c, 2, h3[c])
        for c in copies[4:]:
            c.wait()
        for g in range(e.shape[0]):

            def w_of(c, z, g=g):
                return CC / (1.0 + KK * layer(z)) * tile(vl, g, c, z)

            def m_of(c, z, g=g):
                return tile(vm, g, c, z)

            m16 = stepped(w_of, 0, m_of, 1.0, xp)
            m2 = stepped(w_of, 14, m_of, 1.0, xp)
            extra = jnp.where(sub == 0, tile(ve, g, 2, 13), 0.0)
            extra = jnp.where(sub == 1, pltpu.roll(tile(vl, g, 2, 14), 1, 0), extra)
            store(dn, g, 2, 2, extra)
            for c in range(3):
                blank = jnp.zeros((8, 128), F32)
                last = (layer(0), layer(1)) if g == 0 and c == 0 else (blank, blank)
                for k, value in enumerate((tile(vl, g, c, 0), m16[c]) + last):
                    store(up, g, c, 4 + k, value)
                store(dn, g, c, 5, tile(vl, g, c, 15))
                store(dn, g, c, 6, m2[c] if c < 2 else layer(14 + g % 2))
                store(dn, g, c, 7, m_of(c, 15))

    @pl.when(even)
    def _():
        fill(two, one)

    @pl.when(jnp.logical_not(even))
    def _():
        fill(one, two)


def pack(e, h, le, lh, cond):
    g = e.shape[0]
    message = jax.ShapeDtypeStruct((g, 3, SPAN * 8, 128), F32)
    return pl.pallas_call(
        pack_kernel,
        out_shape=(message, message),
        in_specs=[pl.BlockSpec(memory_space=pl.ANY)] * 5,
        out_specs=(pl.BlockSpec(memory_space=pltpu.VMEM),) * 2,
        scratch_shapes=[pltpu.VMEM((g, 3, 2 * n * 8, 128), F32) for n in (3, 3, 2, 2)]
        + [pltpu.VMEM((32, 128), F32), pltpu.SemaphoreType.DMA((10,))],
        compiler_params=pltpu.CompilerParams(vmem_limit_bytes=24 * 1024 * 1024),
        name="pack",
    )(e, h, le, lh, cond)


TO_LO = ((3, 17),) * 2 + (((2, 16),) * 2 + ((1, 15),) * 2) * 2
TO_HI = ((2, 17),) * 2 + (((1, 16),) * 2 + ((0, 15),) * 2) * 2


def offset(table, k):
    return sum(lo + hi + 1 for lo, hi in table[:k])


def chunk(table):
    return -(-(offset(table, len(table)) + 12) // 8) * 8


def put_plane(ref, table, g, k, value):
    lo, hi = table[k]
    at = offset(table, k)
    ref[g, at : at + hi + 1] = value[0 : hi + 1]
    if lo:
        ref[g, at + hi + 1 : at + hi + 1 + lo] = value[ROWS - lo : ROWS]


def get_plane(ref, table, g, k):
    lo, hi = table[k]
    at = offset(table, k)
    end = at + lo + hi + 1
    rest = ref[g, end - 8 : end]
    if hi > 15:
        r = lax.broadcasted_iota(jnp.int32, (8, 128), 0)
        rest = jnp.where(r < 4, ref[g, at + 16 : at + 24], rest)
    return jnp.concatenate([ref[g, at : at + 16], rest], axis=0)


def put_conductivity(ref, table, value):
    at = offset(table, len(table))
    ref[0, at : at + 8] = value[0:8]
    ref[1, at : at + 8] = value[8:16]
    ref[1, at + 8 : at + 10] = value[16:18]
    ref[1, at + 10 : at + 12] = value[22:24]


def get_conductivity(ref, table):
    at = offset(table, len(table))
    r = lax.broadcasted_iota(jnp.int32, (8, 128), 0)
    rest = ref[1, at + 4 : at + 12]
    rest = jnp.where(r < 4, pltpu.roll(rest, 4, 0), rest)
    return jnp.concatenate([ref[0, at : at + 8], ref[1, at : at + 8], rest], axis=0)


def own_kernel(e, h, le, lh, cond, te, th, tle, tlh, ta, tb, tc, be, bh, ble, blh, bc, sems):
    pairs = ((e, be), (h, bh), (le, ble), (lh, blh), (cond, bc))
    copies = [pltpu.make_async_copy(src, dst, sems.at[k]) for k, (src, dst) in enumerate(pairs)]
    for c in copies:
        c.start()
    for k, (src, dst) in enumerate(((be, te), (bh, th), (ble, tle), (blh, tlh))):
        copies[k].wait()

        def body(g, carry, src=src, dst=dst):
            for c in range(3):
                for x in range(8):
                    dst[g, c, x, 0:8] = src[g, c, pl.ds(x, 8, stride=8), :]
                    dst[g, c, x, 8:16] = src[g, c, pl.ds(64 + x, 8, stride=8), :]
            return carry

        lax.fori_loop(0, e.shape[0], body, 0)
    copies[4].wait()
    for x in range(8):
        for half in range(2):
            value = bc[pl.ds(half * 64 + x, 8, stride=8), :]
            at = pl.ds(half * 8, 8)
            tc[x, at] = value
            ta[x, at], tb[x, at] = coefs(value, True)


def own_planes(e, h, le, lh, cond):
    g = e.shape[0]
    vm = pl.BlockSpec(memory_space=pltpu.VMEM)
    field = jax.ShapeDtypeStruct((g, 3, 8, ROWS, 128), F32)
    return pl.pallas_call(
        own_kernel,
        out_shape=(field,) * 4
        + (jax.ShapeDtypeStruct((8, ROWS, 128), F32),) * 2
        + (jax.ShapeDtypeStruct((8, 16, 128), F32),),
        in_specs=[pl.BlockSpec(memory_space=pl.ANY)] * 5,
        out_specs=(vm,) * 7,
        scratch_shapes=[pltpu.VMEM((g, 3, 128, 128), F32)] * 4
        + [pltpu.VMEM((128, 128), F32), pltpu.SemaphoreType.DMA((5,))],
        cost_estimate=pl.CostEstimate(flops=5_000_000, bytes_accessed=8_000_000, transcendentals=0),
        compiler_params=pltpu.CompilerParams(vmem_limit_bytes=24 * 1024 * 1024),
        name="own",
    )(e, h, le, lh, cond)


def planes_kernel(
    depth_n,
    lat_n,
    ie,
    ih,
    ile,
    ilh,
    ia,
    ib,
    tc,
    one,
    two,
    amp,
    tow,
    te,
    th,
    tle,
    tlh,
    ta,
    tb,
    to_lo,
    to_hi,
):
    groups = te.shape[0]
    depth_at = lax.axis_index("depth")
    lat_at = lax.axis_index("lat")

    even = depth_at % 2 == 0

    r8 = lax.broadcasted_iota(jnp.int32, (8, 128), 0)

    def halos(up, dn):
        def halo(g, carry):
            for c in range(3):
                for x in range(8):
                    hi = up[g, c, pl.ds(x, 8, stride=8), :]
                    lo = dn[g, c, pl.ds(x, 8, stride=8), :]
                    for field, dst in enumerate((te, th, tle, tlh)):
                        a = pltpu.roll(hi, 8 - UP[field], 0) if UP[field] else hi
                        b = pltpu.roll(lo, 7 - DN[field], 0) if DN[field] != 7 else lo
                        dst[g, c, x, 16:24] = jnp.where(r8 < 4, a, b)
            te[g, 2, 0, 21:22] = dn[g, 2, 16:17]
            tle[g, 2, 0, 22:23] = dn[g, 2, 17:18]
            return carry

        lax.fori_loop(0, groups, halo, 0)

    @pl.when(even)
    def _():
        halos(one, two)

    @pl.when(jnp.logical_not(even))
    def _():
        halos(two, one)

    keep = last_row_keep(depth_at, depth_n)

    def edge(first, second, g, c, slot):
        rows = pl.ds(slot * 8, 8)
        return jnp.where(even, first[g, c, rows, :], second[g, c, rows, :])

    u0, u1 = (edge(one, two, 0, 0, 6 + k) for k in range(2))
    d0, d1 = (edge(two, one, k, 2, 6) for k in range(2))
    for x in range(8):
        rest = jnp.where(r8 == 0, u0[x : x + 1], 1.0)
        rest = jnp.where(r8 == 1, u1[x : x + 1], rest)
        rest = jnp.where(r8 == 6, d0[x : x + 1], rest)
        rest = jnp.where(r8 == 7, d1[x : x + 1], rest)
        ta[x, 16:24], tb[x, 16:24] = coefs(rest, keep[16:24])
        if x == 0:
            put_conductivity(to_lo, TO_LO, jnp.concatenate([tc[x], rest], axis=0))
        if x == 7:
            put_conductivity(to_hi, TO_HI, jnp.concatenate([tc[x], rest], axis=0))
    row_mask = first_row_mask(depth_at)
    z, lane = zrow(), lanes()

    first_e, first_l = unstepped(17, -3), unstepped(16, -2)

    def forward_planes(g, carry):
        s = -CC * row_mask
        s_first = s * first_e
        cell = tow[g]
        lz = cell // (1024 * lat_n) - depth_at * 16
        lx = cell // 128 % (8 * lat_n) - lat_at * 8
        point = jnp.where((z == lz) & (lane == cell % 128), 1.0, 0.0)

        def e0(x):
            return tuple(te[g, c, x] for c in range(3))

        def h0(x):
            return tuple(th[g, c, x] for c in range(3))

        def step_h(x):
            return tuple(f + s_first * k for f, k in zip(h0(x), curl_p(e0(x), e0(x + 1))))

        def put(ref, k, value):
            put_plane(ref, TO_LO if ref is to_lo else TO_HI, g, k, value)

        def hit(x, n):
            return jnp.where(lx == x, amp[g, n], 0.0) * point

        zero = (None, 0.0, 0.0)
        a0, b0, a1, b1 = ta[0], tb[0], ta[1], tb[1]
        f0, f1 = e0(0), e0(1)
        h1, k1 = step_h(0), step_h(1)
        put(to_lo, 0, f0[1])
        put(to_lo, 1, f0[2])
        m = curl_m(h1, zero)
        e1 = (a0 * f0[0] + b0 * (m[0] - hit(0, 0)), a0 * f0[1] + b0 * m[1], a0 * f0[2] + b0 * m[2])
        put(to_lo, 2, e1[1])
        put(to_lo, 3, e1[2])
        m = curl_m(k1, h1)
        k = curl_p(e1, (None, a1 * f1[1] + b1 * m[1], a1 * f1[2] + b1 * m[2]))
        h2 = tuple(h1[c] + s * k[c] for c in range(3))
        m = curl_m(h2, zero)
        put(to_lo, 4, a0 * e1[1] + b0 * m[1])
        put(to_lo, 5, a0 * e1[2] + b0 * m[2])
        a7, b7, a6, b6 = ta[7], tb[7], ta[6], tb[6]
        f7, f6 = e0(7), e0(6)
        k = curl_p(f7, zero)
        h7 = tuple(f + s_first * t for f, t in zip(h0(7), k))
        put(to_hi, 0, h7[1])
        put(to_hi, 1, h7[2])
        h6, h5 = step_h(6), step_h(5)
        m7, m6 = curl_m(h7, h6), curl_m(h6, h5)
        e7 = (a7 * f7[0] + b7 * (m7[0] - hit(7, 0)), a7 * f7[1] + b7 * m7[1], a7 * f7[2] + b7 * m7[2])
        e6 = (a6 * f6[0] + b6 * (m6[0] - hit(6, 0)), a6 * f6[1] + b6 * m6[1], a6 * f6[2] + b6 * m6[2])
        k7, k6 = curl_p(e7, zero), curl_p(e6, e7)
        h7 = tuple(h7[c] + s * k7[c] for c in range(3))
        h6 = tuple(h6[c] + s * k6[c] for c in range(3))
        put(to_hi, 2, h7[1])
        put(to_hi, 3, h7[2])
        m7 = curl_m(h7, h6)
        e7 = (a7 * e7[0] + b7 * (m7[0] - hit(7, 1)), a7 * e7[1] + b7 * m7[1], a7 * e7[2] + b7 * m7[2])
        k7 = curl_p(e7, zero)
        put(to_hi, 4, h7[1] + s * k7[1])
        put(to_hi, 5, h7[2] + s * k7[2])
        s = row_mask
        m_first = s * first_l

        def l0(x):
            return tuple(tle[g, c, x] for c in range(3))

        def w0(x):
            return tuple(tb[x] * f for f in l0(x))

        def m0(x):
            return tuple(tlh[g, c, x] for c in range(3))

        def step_m(x):
            return tuple(f + m_first * k for f, k in zip(m0(x), curl_p(w0(x), w0(x + 1))))

        q0, v0 = l0(0), w0(0)
        put(to_lo, 6, v0[1])
        put(to_lo, 7, v0[2])
        m = curl_m(step_m(0), zero)
        put(to_lo, 8, a0 * q0[1] - CC * m[1])
        put(to_lo, 9, a0 * q0[2] - CC * m[2])
        q7 = l0(7)
        k7 = curl_p(w0(7), zero)
        n7 = tuple(f + m_first * t for f, t in zip(m0(7), k7))
        put(to_hi, 6, n7[1])
        put(to_hi, 7, n7[2])
        m = curl_m(n7, step_m(6))
        k7 = curl_p(tuple(b7 * (a7 * q7[c] - CC * m[c]) for c in range(3)), zero)
        put(to_hi, 8, n7[1] + s * k7[1])
        put(to_hi, 9, n7[2] + s * k7[2])
        return carry

    lax.fori_loop(0, groups, forward_planes, 0, unroll=True)


def planes(own, one, two, amp, tow, depth_n, lat_n):
    g = one.shape[0]
    vm = pl.BlockSpec(memory_space=pltpu.VMEM)
    sm = pl.BlockSpec(memory_space=pltpu.SMEM)
    field = jax.ShapeDtypeStruct((g, 3, 8, ROWS, 128), F32)
    coef = jax.ShapeDtypeStruct((8, ROWS, 128), F32)
    return pl.pallas_call(
        functools.partial(planes_kernel, depth_n, lat_n),
        out_shape=(
            field,
            field,
            field,
            field,
            coef,
            coef,
            jax.ShapeDtypeStruct((g, chunk(TO_LO), 128), F32),
            jax.ShapeDtypeStruct((g, chunk(TO_HI), 128), F32),
        ),
        in_specs=[vm] * 9 + [sm] * 2,
        out_specs=(vm,) * 8,
        input_output_aliases={0: 0, 1: 1, 2: 2, 3: 3, 4: 4, 5: 5},
        compiler_params=pltpu.CompilerParams(vmem_limit_bytes=24 * 1024 * 1024),
        name="planes",
    )(*own, one, two, amp, tow)


SLOTS = 24
STRIDE = 8 * ROWS


def e_at(g, n, c, x):
    return pl.ds(pl.multiple_of((g * 9 + n * 3 + c) * STRIDE + x * ROWS, 8), ROWS)


def triple(ref, g, x):
    return tuple(ref[g, c, x] for c in range(3))


def inside(n, x):
    return n + 1 <= x <= 6 - n


def weighted(old, drive, weight):
    total = None
    for c in range(3):
        t = (-2.0 * KK * old[c][0:16] - CC * KK * drive[c][0:16]) * weight[c][0:16]
        total = t if total is None else total + t
    return total


def take_samples(store, rcell, use, put):
    k = lax.broadcasted_iota(jnp.int32, (SLOTS, 128), 0)
    step = k // 3 % 3
    lane = lanes()

    def body(r, c0):
        cell = rcell[r]
        z, x, y = cell // 1024, cell // 128 % 8, cell % 128
        rows = store[pl.ds(x * ROWS + z, SLOTS, stride=STRIDE), :]
        near = (x >= step + 1) & (x <= 6 - step)
        put(r, jnp.where((lane == y) & use(near), rows, 0.0))
        return c0

    lax.fori_loop(0, rcell.shape[0], body, 0, unroll=True)


def tow_at(tow, g, depth_at, lat_at, lat_n):
    cell = tow[g]
    lz = cell // (1024 * lat_n) - depth_at * 16
    lx = cell // 128 % (8 * lat_n) - lat_at * 8
    point = jnp.where((zrow() == lz) & (lanes() == cell % 128), 1.0, 0.0)
    return lx, point


def inner_kernel(
    lat_n, te, th, tle, tlh, ta, tb, amp, tow, rcell, hh, mm, l1, l2, d0, ei, acc, samp
):
    groups = te.shape[0]
    depth_at = lax.axis_index("depth")
    lat_at = lax.axis_index("lat")
    row_mask = first_row_mask(depth_at)
    acc[...] = jnp.zeros_like(acc)

    def one_group(g, carry):
        lx, point = tow_at(tow, g, depth_at, lat_at, lat_n)
        lam = (tle, l1, l2)
        for n in range(2):
            s = row_mask * unstepped(16, -2) if n == 0 else row_mask
            w = {}

            def scaled(x, n=n, w=w):
                if x not in w:
                    w[x] = tuple(tb[x] * f for f in triple(lam[n], g, x))
                return w[x]

            for x in range(n, 7 - n):
                k = curl_p(scaled(x), scaled(x + 1))
                base = triple(tlh if n == 0 else mm, g, x)
                for c in range(3):
                    mm[g, c, x] = base[c] + s * k[c]
            for x in range(n + 1, 7 - n):
                k = curl_m(triple(mm, g, x), triple(mm, g, x - 1))
                old = triple(lam[n], g, x)
                for c in range(3):
                    lam[n + 1][g, c, x] = ta[x] * old[c] - CC * k[c]
        def e_of(n, x):
            if n == 0:
                return triple(te, g, x)
            return tuple(ei[e_at(g, n - 1, c, x), :] for c in range(3))

        for n in range(3):
            s = -CC * (row_mask * unstepped(17, -3) if n == 0 else row_mask)
            for x in range(n, 7 - n):
                k = curl_p(e_of(n, x), e_of(n, x + 1))
                base = triple(th if n == 0 else hh, g, x)
                for c in range(3):
                    hh[g, c, x] = base[c] + s * k[c]
            for x in range(n + 1, 7 - n):
                k = curl_m(triple(hh, g, x), triple(hh, g, x - 1))
                k = (k[0] - jnp.where(lx == x, amp[g, n], 0.0) * point, k[1], k[2])
                old = e_of(n, x)
                for c in range(3):
                    ei[e_at(g, n, c, x), :] = ta[x] * old[c] + tb[x] * k[c]
                if n == 0 and x in (1, 6):
                    for c in range(3):
                        d0[g, c, x // 6] = k[c][0:16]
                else:
                    acc[x] += weighted(old, k, triple(lam[2 - n], g, x))
        return carry

    lax.fori_loop(0, groups, one_group, 0, unroll=True)

    def put(r, values):
        samp[r] = values

    take_samples(ei, rcell, lambda near: near, put)


def inner(te, th, tle, tlh, ta, tb, amp, tow, rcell, lat_n):
    g, n = te.shape[0], rcell.shape[0]
    vm = pl.BlockSpec(memory_space=pltpu.VMEM)
    sm = pl.BlockSpec(memory_space=pltpu.SMEM)
    field = jax.ShapeDtypeStruct((g, 3, 8, ROWS, 128), F32)
    return pl.pallas_call(
        functools.partial(inner_kernel, lat_n),
        out_shape=(
            field,
            field,
            field,
            field,
            jax.ShapeDtypeStruct((g, 3, 2, 16, 128), F32),
            jax.ShapeDtypeStruct((SLOTS * STRIDE, 128), F32),
            jax.ShapeDtypeStruct((8, 16, 128), F32),
            jax.ShapeDtypeStruct((n, SLOTS, 128), F32),
        ),
        in_specs=[vm] * 6 + [sm] * 3,
        out_specs=(vm,) * 8,
        cost_estimate=pl.CostEstimate(flops=20_000_000, bytes_accessed=12_000_000, transcendentals=0),
        compiler_params=pltpu.CompilerParams(vmem_limit_bytes=24 * 1024 * 1024),
        name="inner",
    )(te, th, tle, tlh, ta, tb, amp, tow, rcell)


def outer_kernel(
    depth_n,
    lat_n,
    te,
    th,
    tle,
    tlh,
    ta,
    tb,
    hh,
    mm,
    l1,
    l2,
    d0,
    ei,
    acc,
    samp,
    lo,
    hi,
    amp,
    tow,
    rcell,
    rowner,
    grad,
    send,
    eo,
    ho,
    mo,
    o1,
    o2,
    total,
    drives,
    staged,
    count,
    sem,
):
    groups = te.shape[0]
    depth_at = lax.axis_index("depth")
    lat_at = lax.axis_index("lat")
    row_mask = first_row_mask(depth_at)
    keep = last_row_keep(depth_at, depth_n)
    a8, b8 = coefs(get_conductivity(hi, TO_LO), keep & (lat_at < lat_n - 1))
    al, bl = coefs(get_conductivity(lo, TO_HI), keep)
    left = jnp.where(lat_at == 0, 0.0, 1.0)
    total[...] = acc[...]

    def lam(n, g, x):
        if n == 0:
            return triple(tle, g, x)
        near = inside(n - 1, x)
        return triple((l1 if near else o1) if n == 1 else (l2 if near else o2), g, x)

    def e_of(n, g, x):
        if n == 0:
            return triple(te, g, x)
        ref = ei if inside(n - 1, x) else eo
        return tuple(ref[e_at(g, n - 1, c, x), :] for c in range(3))

    def forward(g, carry):
        def high(k):
            return get_plane(hi, TO_LO, g, k)

        def low(k):
            return get_plane(lo, TO_HI, g, k)

        lx, point = tow_at(tow, g, depth_at, lat_at, lat_n)
        s = -CC * row_mask

        def h_of(n, x):
            return triple(hh if n <= x <= 6 - n else ho, g, x)

        def h_step(n, nxt):
            for x in range(8):
                if n <= x <= 6 - n:
                    continue
                after = (nxt if n else (None, 0.0, 0.0)) if x == 7 else e_of(n, g, x + 1)
                k = curl_p(e_of(n, g, x), after)
                base = triple(th, g, x) if n == 0 else h_of(n - 1, x)
                new = tuple(base[c] + (s if n else s * unstepped(17, -3)) * k[c] for c in range(3))
                if n == 0:
                    new = (new[0], new[1] - s * nxt[2], new[2] + s * nxt[1])
                for c in range(3):
                    ho[g, c, x] = new[c]

        def e_step(n, prv):
            for x in range(8):
                if inside(n, x):
                    continue
                old = e_of(n, g, x)
                k = curl_m(h_of(n, x), h_of(n, x - 1) if x else prv)
                k = (k[0] - jnp.where(lx == x, amp[g, n], 0.0) * point, k[1], k[2])
                for c in range(3):
                    eo[e_at(g, n, c, x), :] = ta[x] * old[c] + tb[x] * k[c]
                    drives[g, n, c, x] = k[c][0:16]

        h_step(0, (None, high(0), high(1)))
        first = e_of(0, g, 0)
        dy, dz = -s * first[2], s * first[1]
        e_step(0, (None, left * (low(0) + dy), left * (low(1) + dz)))
        last = h_of(0, 7)
        uy, uz = b8 * last[2], -b8 * last[1]
        h_step(1, (None, high(2) + uy, high(3) + uz))
        ex, ey, ez = bl * (dmy(dz) - dmz(dy)), -bl * dz, bl * dy
        first = e_of(1, g, 0)
        dy = dy + s * (dpz(ex) - (first[2] - ez))
        dz = dz + s * ((first[1] - ey) - dpy(ex))
        e_step(1, (None, left * (low(2) + dy), left * (low(3) + dz)))
        last = h_of(1, 7)
        gx, gy, gz = s * (dpy(uz) - dpz(uy)), s * uz, -s * uy
        h_step(
            2,
            (
                None,
                high(4) + a8 * uy + b8 * (dmz(gx) - gz + last[2]),
                high(5) + a8 * uz + b8 * (gy - last[1] - dmy(gx)),
            ),
        )
        hx, hy, hz = s * (dpy(ez) - dpz(ey)), -s * ez, s * ey
        ex, ey, ez = (
            al * ex + bl * (dmy(dz) - dmz(dy)),
            al * ey + bl * (dmz(hx) - dz + hz),
            al * ez + bl * (dy - hy - dmy(hx)),
        )
        first = e_of(2, g, 0)
        dy = dy + s * (dpz(ex) - (first[2] - ez))
        dz = dz + s * ((first[1] - ey) - dpy(ex))
        e_step(2, (None, left * (low(4) + dy), left * (low(5) + dz)))
        return carry

    lax.fori_loop(0, groups, forward, 0, unroll=True)
    staged[...] = jnp.zeros_like(staged)
    for o in range(staged.shape[0]):
        count[o] = 0
    r24, lane = lax.broadcasted_iota(jnp.int32, (SLOTS, 128), 0), lanes()
    used = (r24 == lane) & (r24 < groups * 9)

    def put(r, values):
        o = rowner[r]
        slot = count[o]
        count[o] = slot + 1
        values = jnp.sum(samp[r] + values, axis=-1, keepdims=True)
        staged[o, pl.ds(slot, 1), :] = jnp.sum(jnp.where(used, values, 0.0), axis=0, keepdims=True)

    take_samples(eo, rcell, jnp.logical_not, put)
    leave = pltpu.make_async_copy(staged, send, sem)
    leave.start()

    def adjoint(g, carry):
        def high(k):
            return get_plane(hi, TO_LO, g, k)

        def low(k):
            return get_plane(lo, TO_HI, g, k)

        s = row_mask

        def m_of(n, x):
            return triple(mm if n <= x <= 6 - n else mo, g, x)

        def m_step(n, nxt):
            w = {8: nxt if n else (None, 0.0, 0.0)}

            def scaled(x):
                if x not in w:
                    w[x] = tuple(tb[x] * f for f in lam(n, g, x))
                return w[x]

            for x in range(8):
                if n <= x <= 6 - n:
                    continue
                k = curl_p(scaled(x), scaled(x + 1))
                base = triple(tlh, g, x) if n == 0 else m_of(n - 1, x)
                new = tuple(base[c] + (s if n else s * unstepped(16, -2)) * k[c] for c in range(3))
                if n == 0:
                    new = (new[0], new[1] - s * nxt[2], new[2] + s * nxt[1])
                for c in range(3):
                    mo[g, c, x] = new[c]

        def l_step(n, prv):
            out = (o1, o2)[n]
            for x in range(8):
                if inside(n, x):
                    continue
                k = curl_m(m_of(n, x), m_of(n, x - 1) if x else prv)
                old = lam(n, g, x)
                for c in range(3):
                    out[g, c, x] = ta[x] * old[c] - CC * k[c]

        m_step(0, (None, high(6), high(7)))
        first = lam(0, g, 0)
        dy, dz = -s * (tb[0] * first[2]), s * (tb[0] * first[1])
        l_step(0, (None, left * (low(6) + dy), left * (low(7) + dz)))
        last = m_of(0, 7)
        m_step(1, (None, b8 * (high(8) - CC * last[2]), b8 * (high(9) + CC * last[1])))
        wx, wy, wz = -CC * bl * (dmy(dz) - dmz(dy)), CC * bl * dz, -CC * bl * dy
        first = lam(1, g, 0)
        dy = dy + s * (dpz(wx) - (tb[0] * first[2] - wz))
        dz = dz + s * ((tb[0] * first[1] - wy) - dpy(wx))
        l_step(1, (None, left * (low(8) + dy), left * (low(9) + dz)))
        for n in range(3):
            for x in range(8):
                if n == 0 and x in (1, 6):
                    drive = tuple(d0[g, c, x // 6] for c in range(3))
                elif inside(n, x):
                    continue
                else:
                    drive = tuple(drives[g, n, c, x] for c in range(3))
                total[x] += weighted(e_of(n, g, x), drive, lam(2 - n, g, x))
        return carry

    lax.fori_loop(0, groups, adjoint, 0, unroll=True)
    for x in range(8):
        for half in range(2):
            rows = pl.ds(half * 64 + x, 8, stride=8)
            inv = tb[x, half * 8 : half * 8 + 8] * (1.0 / CC)
            grad[rows, :] = total[x, half * 8 : half * 8 + 8] * inv * inv
    leave.wait()


def outer(te, th, tle, tlh, ta, tb, kept, lo, hi, amp, tow, rcell, rowner, depth_n, lat_n):
    g = te.shape[0]
    vm = pl.BlockSpec(memory_space=pltpu.VMEM)
    sm = pl.BlockSpec(memory_space=pltpu.SMEM)
    return pl.pallas_call(
        functools.partial(outer_kernel, depth_n, lat_n),
        out_shape=(
            jax.ShapeDtypeStruct((128, 128), F32),
            jax.ShapeDtypeStruct((lat_n, 2, 128), F32),
        ),
        in_specs=[vm] * 16 + [sm] * 4,
        out_specs=(vm, pl.BlockSpec(memory_space=pl.ANY)),
        scratch_shapes=[pltpu.VMEM((SLOTS * STRIDE, 128), F32)]
        + [pltpu.VMEM((g, 3, 8, ROWS, 128), F32)] * 4
        + [
            pltpu.VMEM((8, 16, 128), F32),
            pltpu.VMEM((g, 3, 3, 8, 16, 128), F32),
            pltpu.VMEM((lat_n, 2, 128), F32),
            pltpu.SMEM((lat_n,), jnp.int32),
            pltpu.SemaphoreType.DMA(()),
        ],
        cost_estimate=pl.CostEstimate(flops=10_000_000, bytes_accessed=12_000_000, transcendentals=0),
        compiler_params=pltpu.CompilerParams(vmem_limit_bytes=24 * 1024 * 1024),
        name="outer",
    )(te, th, tle, tlh, ta, tb, *kept, lo, hi, amp, tow, rcell, rowner)


def finish_kernel(mine, theirs, got, total, lines):
    total[...] = mine[...] + theirs[...]
    for slot in range(2):
        table = jnp.transpose(got[:, slot, :])
        for g in range(lines.shape[0]):
            lines[g, :, slot, :] = table[g * 9 : g * 9 + 9]


def finish(mine, theirs, got, groups):
    vm = pl.BlockSpec(memory_space=pltpu.VMEM)
    return pl.pallas_call(
        finish_kernel,
        out_shape=(
            jax.ShapeDtypeStruct(mine.shape, F32),
            jax.ShapeDtypeStruct((groups, 9, 2, got.shape[0]), F32),
        ),
        in_specs=[vm] * 3,
        out_specs=(vm,) * 2,
        compiler_params=pltpu.CompilerParams(vmem_limit_bytes=24 * 1024 * 1024),
        name="finish",
    )(mine, theirs, got)


def across(value, step):
    n = lax.axis_size("src")
    return lax.ppermute(value, "src", [(i, i ^ step) for i in range(n) if i ^ step < n])


def per_device(
    conductivity, e_start, h_start, e_weight, h_weight, source_amp, tow_cell, rec_cell, rec_owner
):
    groups = e_start.shape[0]
    depth_n, lat_n = lax.axis_size("depth"), lax.axis_size("lat")

    def flat(f):
        return f.reshape(groups, 3, 128, 128)

    e, h, le, lh = flat(e_start), flat(h_start), flat(e_weight), flat(h_weight)
    cond = conductivity.reshape(128, 128)
    fields = [
        pltpu.with_memory_space_constraint(f, pltpu.HBM) for f in (e, h, le, lh, cond)
    ]
    one, two = pack(*fields)
    one = swapped(one, "depth", 0)
    two = swapped(two, "depth", 1)
    own = own_planes(*fields)
    te, th, tle, tlh, ta, tb, to_lo, to_hi = planes(
        own, one, two, source_amp, tow_cell, depth_n, lat_n
    )
    cells, owners = rec_cell.reshape(-1), rec_owner.reshape(-1)
    hi = shifted(to_lo, "lat", -1)
    lo = shifted(to_hi, "lat", 1)
    kept = inner(te, th, tle, tlh, ta, tb, source_amp, tow_cell, cells, lat_n)
    grad, send = outer(
        te,
        th,
        tle,
        tlh,
        ta,
        tb,
        kept,
        lo,
        hi,
        source_amp,
        tow_cell,
        cells,
        owners,
        depth_n,
        lat_n,
    )
    got = lax.all_to_all(send, "lat", split_axis=0, concat_axis=0, tiled=True)
    every = lax.all_gather(grad, "src", axis=0, tiled=False)
    total, lines = finish(every[0] + every[1], every[2] + every[3], got, groups)
    total = total.reshape(16, 8, 128)
    lines = jnp.transpose(lines.reshape(groups, 1, 1, 9, 2, lat_n), (0, 1, 2, 5, 4, 3))
    return (total, lines)


def solution(mesh):
    placed = (
        P("depth", "lat", None),
        P("src", None, "depth", "lat", None),
        P("src", None, "depth", "lat", None),
        P("src", None, "depth", "lat", None),
        P("src", None, "depth", "lat", None),
        P("src", None),
        P("src"),
        P("depth", "lat", None),
        P("depth", "lat", None, None),
    )
    return jax.shard_map(
        per_device,
        mesh=mesh,
        in_specs=placed,
        out_specs=(P("depth", "lat", None), P("src", "depth", "lat", None, None, None)),
        check_vma=False,
    )
```
